256 devices in a mesh: ty: 8 (over y, z_hi), tx: 16 (over x, z_lo), pa: 2 (over core).
Axes of the slice: x: 4, y: 4, z: 8 (z_hi: 2, z_lo: 4; z = z_hi * 4 + z_lo), core: 2. Of those that a mesh axis runs over, the one named last changes fastest.
Arguments:
- object_field: float32 [2, 8192, 4096], P(None, 'ty', 'tx'), may hold values from -6 to 6
- probe_field: float32 [2, 128, 128], replicated, may hold values from -6 to 6
- amplitudes: bfloat16 [8, 16, 128, 128, 128], P('ty', 'tx', 'pa'), may hold values from 0.049804688 to 1.5
- start_row: int32 [8, 16, 128], P('ty', 'tx', 'pa'), may hold values from 0 to 1023
- start_col: int32 [8, 16, 128], P('ty', 'tx', 'pa'), may hold values from 0 to 255
- counts: int32 [8, 16], replicated, may hold values from 16 to 96, as said below
Outputs:
- object_grad: float32 [2, 8192, 4096], P(None, 'ty', 'tx')
- probe_grad: float32 [2, 128, 128], replicated
The draws below stay inside these ranges and needn't reach their ends.
Inputs may be any that keep to these rules, and one draw needn't show every extreme that they name: Tile (a, b) uses its first counts[a, b] slots; some tile uses exactly 96.
All inputs are finite; a program needn't handle non-finite values.
Results may differ from the reference program's by a relative error of at most 0.0007.
The reference program's roundings to bfloat16 on the way count: a program that leaves them out, or rounds other values in their place, can miss the bound.
Values may be sent and summed in bfloat16 or wider, within the bound.
A program may use at most 64 MiB of HBM per device.

```python
import math
import jax
import jax.numpy as jnp
from jax import lax

PATCH = 128
TR = 1024
TC = 256
CAP = 128
BLK = 8
TROWS = 8
TCOLS = 16
NR = 8192
NC = 4096


def draw_counts(key, part):
    most = CAP * 3 // 4
    values = jax.random.randint(key, (TROWS * TCOLS,), CAP // 8, most + 1, dtype=jnp.int32)
    chosen = jax.random.randint(jax.random.fold_in(key, 7), (), 0, TROWS * TCOLS, dtype=jnp.int32)
    values = values.at[chosen].set(most)
    return values.reshape(TROWS, TCOLS).astype(jnp.int32)


def plant(values, stream_key, smallest, high):
    longest = values.shape.index(max(values.shape))
    spots = []
    for shift in (0, 1):
        where = [jax.random.randint(jax.random.fold_in(stream_key, axis), (), 0, length) for axis, length in enumerate(values.shape)]
        where[longest] = (where[longest] + shift) % values.shape[longest]
        spots.append(tuple(where))
    return values.at[spots[0]].set(smallest).at[spots[1]].set(high)


def block_scale(rng, extent, pieces, least, top_value):
    level, own = 1.0, jax.random.fold_in(rng, 6)
    for position, blocks in pieces:
        draws = jnp.exp(jax.random.uniform(jax.random.fold_in(own, position), (blocks,), jnp.float32, least / len(pieces), top_value / len(pieces)))
        level = level * jnp.repeat(draws, extent[position] // blocks).reshape([-1 if axis == position else 1 for axis in range(len(extent))])
    return level


def gaussian(stream_key, dims, spread, most, split=(), held_as=jnp.bfloat16):
    values = spread * jax.random.normal(stream_key, dims, jnp.float32)
    if split:
        values = values * block_scale(stream_key, dims, split, -0.22, 0.18)
    return jnp.clip(values, -most, most).astype(held_as)


def setup_inputs(seed: int = 0) -> dict:
    splits = jax.random.split(jax.random.key(seed), 7)
    return {
        "object_field": gaussian(splits[0], (2, NR, NC), 1.0, 6.0, ((1, 8), (2, 16)), jnp.float32),
        "probe_field": gaussian(splits[1], (2, PATCH, PATCH), 1.0, 6.0, (), jnp.float32),
        "amplitudes": jnp.clip(jnp.exp(math.log(1.5) - 3.4051113 * jax.random.uniform(splits[2], (TROWS, TCOLS, CAP, PATCH, PATCH), jnp.float32) ** block_scale(splits[2], (TROWS, TCOLS, CAP, PATCH, PATCH), ((0, 8), (1, 16), (2, 2)), -0.2, 0.2)), 0.049804688, 1.5).astype(jnp.bfloat16),
        "start_row": plant(jax.random.randint(splits[3], (TROWS, TCOLS, CAP), 0, TR), jax.random.fold_in(splits[3], 1), 0, TR - 1).astype(jnp.int32),
        "start_col": plant(jax.random.randint(splits[4], (TROWS, TCOLS, CAP), 0, TC), jax.random.fold_in(splits[4], 1), 0, TC - 1).astype(jnp.int32),
        "counts": draw_counts(jax.random.fold_in(splits[6], 71), 0),
    }


def dft_table(length, inverse):
    freqs = jnp.arange(length, dtype=jnp.int32)
    phase = freqs[:, None] * freqs[None, :] % length
    angle = phase.astype(jnp.float32) * (2.0 * math.pi / length)
    scale = 1.0 / math.sqrt(length)
    cosine = jnp.cos(angle) * scale
    sine = jnp.sin(angle) * scale
    if inverse:
        upper = jnp.concatenate([cosine, sine], axis=1)
        lower = jnp.concatenate([-sine, cosine], axis=1)
    else:
        upper = jnp.concatenate([cosine, -sine], axis=1)
        lower = jnp.concatenate([sine, cosine], axis=1)
    return jnp.concatenate([upper, lower], axis=0).astype(jnp.bfloat16)

def along_last(real_part, imag_part, table):
    length = real_part.shape[-1]
    stacked = jnp.concatenate([real_part, imag_part], axis=-1).astype(jnp.float32)
    result = jnp.einsum('bnk,kj->bnj', stacked, table.astype(jnp.float32), precision=lax.Precision.HIGHEST)
    return (result[..., :length], result[..., length:])

def patch_terms(patches, measured, probe_field, usable, forward_table, inverse_table):
    probe_re = probe_field[0]
    probe_im = probe_field[1]
    patch_re = patches[:, 0]
    patch_im = patches[:, 1]
    psi_re = (probe_re * patch_re - probe_im * patch_im).astype(jnp.bfloat16)
    psi_im = (probe_re * patch_im + probe_im * patch_re).astype(jnp.bfloat16)
    half_re, half_im = along_last(psi_re, psi_im, forward_table)
    half_re = jnp.swapaxes(half_re.astype(jnp.bfloat16), 1, 2)
    half_im = jnp.swapaxes(half_im.astype(jnp.bfloat16), 1, 2)
    wave_re, wave_im = along_last(half_re, half_im, forward_table)
    level = jnp.swapaxes(measured, 1, 2).astype(jnp.float32)
    modulus = jnp.sqrt(wave_re * wave_re + wave_im * wave_im + 1.0)
    factor = jnp.where(usable[:, None, None], 1.0 - level / modulus, 0.0)
    chi_re = (wave_re * factor).astype(jnp.bfloat16)
    chi_im = (wave_im * factor).astype(jnp.bfloat16)
    back_re, back_im = along_last(chi_re, chi_im, inverse_table)
    back_re = jnp.swapaxes(back_re.astype(jnp.bfloat16), 1, 2)
    back_im = jnp.swapaxes(back_im.astype(jnp.bfloat16), 1, 2)
    grad_re, grad_im = along_last(back_re, back_im, inverse_table)
    object_re = probe_re * grad_re + probe_im * grad_im
    object_im = probe_re * grad_im - probe_im * grad_re
    probe_part_re = lax.optimization_barrier(jnp.sum(patch_re * grad_re + patch_im * grad_im, axis=0))
    probe_part_im = lax.optimization_barrier(jnp.sum(patch_re * grad_im - patch_im * grad_re, axis=0))
    return (object_re, object_im, jnp.stack([probe_part_re, probe_part_im]))

def reference(object_field, probe_field, amplitudes, start_row, start_col, counts):
    width = PATCH
    padded = jnp.pad(object_field, ((0, 0), (0, width), (0, width)))
    tile_rows = jnp.arange(TROWS, dtype=jnp.int32)[:, None, None] * TR
    tile_cols = jnp.arange(TCOLS, dtype=jnp.int32)[None, :, None] * TC
    all_rows = (start_row + tile_rows).reshape(-1).astype(jnp.int32)
    all_cols = (start_col + tile_cols).reshape(-1).astype(jnp.int32)
    slots = jnp.arange(CAP, dtype=jnp.int32)[None, None, :]
    all_usable = (slots < counts[:, :, None]).reshape(-1)
    all_measured = amplitudes.reshape(-1, width, width)
    forward_table = dft_table(width, False)
    inverse_table = dft_table(width, True)
    nblocks = TROWS * TCOLS * CAP // BLK
    zero = jnp.int32(0)

    def block_step(block_index, carry):
        grad_field, probe_acc = carry
        first = (block_index * BLK).astype(jnp.int32)
        block_rows = lax.dynamic_slice_in_dim(all_rows, first, BLK)
        block_cols = lax.dynamic_slice_in_dim(all_cols, first, BLK)
        usable = lax.dynamic_slice_in_dim(all_usable, first, BLK)
        measured = lax.dynamic_slice_in_dim(all_measured, first, BLK)
        patches = jnp.stack([lax.dynamic_slice(padded, (zero, block_rows[member], block_cols[member]), (2, width, width)) for member in range(BLK)])
        object_re, object_im, probe_part = patch_terms(patches, measured, probe_field, usable, forward_table, inverse_table)
        for member in range(BLK):
            where_at = (zero, block_rows[member], block_cols[member])
            current = lax.dynamic_slice(grad_field, where_at, (2, width, width))
            added = current + jnp.stack([object_re[member], object_im[member]])
            grad_field = lax.dynamic_update_slice(grad_field, added, where_at)
        return (grad_field, probe_acc + probe_part)
    init = (jnp.zeros(padded.shape, jnp.float32), jnp.zeros((2, width, width), jnp.float32))
    grad_field, probe_acc = lax.fori_loop(0, nblocks, block_step, init)
    object_grad = grad_field[:, :NR, :NC]
    probe_grad = probe_acc / jnp.sum(counts).astype(jnp.float32)
    return (object_grad, probe_grad)
```

```python
import functools
import math

import jax
import jax.numpy as jnp
import ml_dtypes
import numpy as np
from jax import lax
from jax.experimental import pallas as pl
from jax.experimental.pallas import tpu as pltpu
from jax.sharding import PartitionSpec as P

BLK = 8

N = 128

def dft_tables(length):
    freqs = np.arange(length)
    angle = (freqs[:, None] * freqs[None, :] % length) * (2.0 * math.pi / length)
    cosine = np.cos(angle) / math.sqrt(length)
    sine = np.sin(angle) / math.sqrt(length)
    forward = np.block([[cosine, -sine], [sine, cosine]]).astype(ml_dtypes.bfloat16)
    inverse = np.block([[cosine, sine], [-sine, cosine]]).astype(ml_dtypes.bfloat16)
    return forward, inverse

def mm(a, b):
    return jnp.dot(a, b, preferred_element_type=jnp.float32)

def patch_kernel(B, rows_ref, cols_ref, lim_ref, ext_ref, probe_ref, amp_ref, fwd_ref, inv_ref,
                 acc_ref, pg_ref, patch_ref):
    acc_ref[...] = jnp.zeros_like(acc_ref)
    pg_ref[...] = jnp.zeros_like(pg_ref)
    lane = lax.broadcasted_iota(jnp.int32, (N, N), 1)
    last = lim_ref[0]

    def body(it, _):
        pos = []
        psis = []
        for b in range(B):
            i = it * B + b
            slot = jnp.minimum(i, last - 1)
            r = rows_ref[slot]
            c = cols_ref[slot]
            j = c // N
            s = c % N
            pos.append((slot, i < last, r, j, s))
            back = (N - s) % N
            high = lane >= s
            parts = []
            for p in range(2):
                v = jnp.where(high, ext_ref[p, j, pl.ds(r, N), :], ext_ref[p, j + 1, pl.ds(r, N), :])
                v = pltpu.roll(v, back, 1)
                patch_ref[b, p] = v
                parts.append(v)
            pre, pim = probe_ref[0], probe_ref[1]
            psi_re = pre * parts[0] - pim * parts[1]
            psi_im = pre * parts[1] + pim * parts[0]
            psis.append(jnp.concatenate([psi_re.astype(jnp.bfloat16), psi_im.astype(jnp.bfloat16)], axis=1))
        half = mm(jnp.concatenate(psis, axis=0), fwd_ref[...]).astype(jnp.bfloat16)
        rhs = jnp.concatenate(
            [jnp.concatenate([half[b * N:(b + 1) * N, q * N:(q + 1) * N] for b in range(B)], axis=1) for q in range(2)], axis=0)
        wave = mm(inv_ref[...], rhs)
        chis = [[], []]
        for b in range(B):
            slot, ok, r, j, s = pos[b]
            wre = wave[:N, b * N:(b + 1) * N]
            wim = wave[N:, b * N:(b + 1) * N]
            level = amp_ref[slot].astype(jnp.float32)
            use = ok.astype(jnp.float32)
            factor = (1.0 - level * lax.rsqrt(wre * wre + wim * wim + 1.0)) * use
            chis[0].append((wre * factor).astype(jnp.bfloat16))
            chis[1].append((wim * factor).astype(jnp.bfloat16))
        rhs2 = jnp.concatenate([jnp.concatenate(chis[q], axis=1) for q in range(2)], axis=0)
        bk = mm(fwd_ref[...], rhs2).astype(jnp.bfloat16)
        lhs = jnp.concatenate([jnp.concatenate([bk[q * N:(q + 1) * N, b * N:(b + 1) * N] for q in range(2)], axis=1) for b in range(B)], axis=0)
        grad = mm(lhs, inv_ref[...])
        tre = pg_ref[0]
        tim = pg_ref[1]
        for b in range(B):
            slot, ok, r, j, s = pos[b]
            gre = grad[b * N:(b + 1) * N, :N]
            gim = grad[b * N:(b + 1) * N, N:]
            pre, pim = probe_ref[0], probe_ref[1]
            qre, qim = patch_ref[b, 0], patch_ref[b, 1]
            tre = tre + (qre * gre + qim * gim)
            tim = tim + (qre * gim - qim * gre)
            obj = (pre * gre + pim * gim, pre * gim - pim * gre)
            high = lane >= s
            for p in range(2):
                o = pltpu.roll(obj[p], s, 1)
                acc_ref[p, j, pl.ds(r, N), :] += jnp.where(high, o, 0.0)
                acc_ref[p, j + 1, pl.ds(r, N), :] += jnp.where(high, 0.0, o)
        pg_ref[0] = tre
        pg_ref[1] = tim
        return 0

    lax.fori_loop(0, (last + B - 1) // B, body, 0)

def patches(rows, cols, lim, ext, probe, amp, fwd, inv, B=2):
    return pl.pallas_call(
        functools.partial(patch_kernel, B),
        out_shape=(jax.ShapeDtypeStruct(ext.shape, jnp.float32), jax.ShapeDtypeStruct((2, N, N), jnp.float32)),
        in_specs=[pl.BlockSpec(memory_space=pltpu.SMEM)] * 3 + [pl.BlockSpec(memory_space=pltpu.VMEM)] * 5,
        out_specs=(pl.BlockSpec(memory_space=pltpu.VMEM),) * 2,
        scratch_shapes=[pltpu.VMEM((B, 2, N, N), jnp.float32)],
        compiler_params=pltpu.CompilerParams(vmem_limit_bytes=48 << 20),
        name="patches",
    )(rows, cols, lim, ext, probe, amp, fwd, inv)


def from_behind(value, axis, steps):
    count = lax.axis_size(axis)
    initial, last = (max(0, -steps), min(count, count - steps))
    return lax.ppermute(value, axis, [(source, source + steps) for source in range(initial, last)])


def shards(object_field, probe_field, amplitudes, start_row, start_col, counts):
    height, width = object_field.shape[1:]
    half = start_row.shape[-1]
    row_place = lax.axis_index("ty")
    col_place = lax.axis_index("tx")
    core_place = lax.axis_index("pa")
    right = from_behind(object_field[:, :, :N], "tx", -1)
    top = jnp.concatenate([object_field[:, :N], right[:, :N]], axis=2)
    below = from_behind(top, "ty", -1)
    blocks = [object_field[:, :, q * N:(q + 1) * N] for q in range(width // N)] + [right]
    extended = jnp.stack(
        [jnp.concatenate([block, below[:, :, q * N:(q + 1) * N]], axis=1) for q, block in enumerate(blocks)], axis=1
    )
    nvalid = jnp.clip(counts[row_place, col_place] - core_place * half, 0, half)
    forward, inverse = dft_tables(N)
    grad, probe_part = patches(
        start_row[0, 0], start_col[0, 0], nvalid[None], extended, probe_field, amplitudes[0, 0],
        jnp.asarray(forward), jnp.asarray(inverse), BLK)
    arrived = from_behind(grad[:, -1], "tx", 1)
    grad = grad[:, :-1].at[:, 0].add(arrived)
    arrived_below = from_behind(grad[:, :, height:], "ty", 1)
    tile = grad[:, :, :height].at[:, :, :N].add(arrived_below)
    tile = lax.psum(tile, "pa")
    object_grad = jnp.concatenate([tile[:, q] for q in range(width // N)], axis=2)
    probe_total = lax.psum(probe_part, ("ty", "tx", "pa"))
    return object_grad, probe_total / jnp.sum(counts).astype(jnp.float32)


def solution(mesh):
    return jax.shard_map(
        shards,
        mesh=mesh,
        in_specs=(
            P(None, "ty", "tx"),
            P(),
            P("ty", "tx", "pa", None, None),
            P("ty", "tx", "pa"),
            P("ty", "tx", "pa"),
            P(),
        ),
        out_specs=(P(None, "ty", "tx"), P()),
        check_vma=False,
    )
```

```python
import functools
import math

import jax
import jax.numpy as jnp
import ml_dtypes
import numpy as np
from jax import lax
from jax.experimental import pallas as pl
from jax.experimental.pallas import tpu as pltpu
from jax.sharding import PartitionSpec as P

BLK = 8

N = 128
LEVELS = 32766.0
MESH = pl.DeviceIdType.MESH


def encode(x):
    rows = x.shape[0]
    tiles = x.reshape(rows // 8, 8, N)
    peak = jnp.max(jnp.abs(tiles), axis=0)
    scaled = tiles * (LEVELS / jnp.maximum(peak, 1e-30))[None]
    return jnp.round(scaled.reshape(rows, N)).astype(jnp.int32).astype(jnp.int16), peak * (1.0 / LEVELS)


def decode(code, step):
    rows = code.shape[0]
    value = code.astype(jnp.int32).astype(jnp.float32)
    return (value.reshape(rows // 8, 8, N) * step[None]).reshape(rows, N)


def remote(src, dst, send_sem, recv_sem, where):
    return pltpu.make_async_remote_copy(
        src_ref=src, dst_ref=dst, send_sem=send_sem, recv_sem=recv_sem, device_id=where, device_id_type=MESH)


def collect_kernel(nty, ntx, counts_ref, acc_ref, pg_ref, out_ref, pgo_ref,
                   theirs, pg_theirs, code_out, step_out, code_in, step_in, by_ty, by_tx, part,
                   pair_send, pair_recv, strip_send, strip_recv, ty_send, ty_recv, tx_send, tx_recv, all_send, all_recv):
    ty, tx, me = lax.axis_index("ty"), lax.axis_index("tx"), lax.axis_index("pa")
    other = 1 - me
    height = out_ref.shape[1]
    nq = out_ref.shape[2] // N
    peer = {"pa": other}
    chunk = N // nty
    sizes = (height, nq * N, N)
    offs = (0, height, height + nq * N)
    targets = ({"tx": lax.rem(tx + 1, ntx)}, {"ty": lax.rem(ty + 1, nty)},
               {"tx": lax.rem(tx + 1, ntx), "ty": lax.rem(ty + 1, nty)})
    sources = ({"tx": lax.rem(tx + ntx - 1, ntx)}, {"ty": lax.rem(ty + nty - 1, nty)},
               {"tx": lax.rem(tx + ntx - 1, ntx), "ty": lax.rem(ty + nty - 1, nty)})
    sends = (tx < ntx - 1, ty < nty - 1, jnp.logical_and(tx < ntx - 1, ty < nty - 1))
    gets = (tx > 0, ty > 0, jnp.logical_and(tx > 0, ty > 0))

    barrier = pltpu.get_barrier_semaphore()
    pl.semaphore_signal(barrier, inc=1, device_id=peer, device_id_type=MESH)
    pl.semaphore_signal(barrier, inc=1, device_id=targets[2], device_id_type=MESH)
    pl.semaphore_signal(barrier, inc=1, device_id=sources[2], device_id_type=MESH)

    @pl.loop(1, nty)
    def _(k):
        pl.semaphore_signal(barrier, inc=1, device_id={"ty": lax.rem(ty + k, nty)}, device_id_type=MESH)

    @pl.loop(1, ntx)
    def _(k):
        pl.semaphore_signal(barrier, inc=1, device_id={"tx": lax.rem(tx + k, ntx)}, device_id_type=MESH)

    total = jnp.sum(jnp.sum(counts_ref[...].astype(jnp.float32), axis=1, keepdims=True), axis=0, keepdims=True)
    pl.semaphore_wait(barrier, 1 + 2 + nty - 1 + ntx - 1)

    def swap(n, src, dst):
        return remote(src, dst, pair_send.at[n], pair_recv.at[n], peer)

    right = swap(0, acc_ref.at[other, nq], theirs.at[nq])
    low = [swap(1 + q, acc_ref.at[other, q, pl.ds(height, N)], theirs.at[q, pl.ds(height, N)]) for q in range(nq)]
    probe_swap = swap(1 + nq, pg_ref.at[other], pg_theirs)
    body = [swap(2 + nq + q, acc_ref.at[other, q, pl.ds(0, height)], theirs.at[q, pl.ds(0, height)]) for q in range(nq)]
    right.start()
    for c in low:
        c.start()
    probe_swap.start()
    for c in reversed(body):
        c.start()

    def strip(n):
        size, off = sizes[n], offs[n]
        return (remote(code_out.at[pl.ds(off, size)], code_in.at[pl.ds(off, size)],
                       strip_send.at[2 * n], strip_recv.at[2 * n], targets[n]),
                remote(step_out.at[n], step_in.at[n], strip_send.at[2 * n + 1], strip_recv.at[2 * n + 1], targets[n]))

    def pack(n, value):
        code_out[pl.ds(offs[n], sizes[n])], step_out[n] = encode(value)

        @pl.when(sends[n])
        def _():
            for c in strip(n):
                c.start()

    right.wait()
    pack(0, acc_ref[me, nq, :height] + theirs[nq, :height])
    for c in low:
        c.wait()
    pack(1, jnp.concatenate([acc_ref[me, q, height:] + theirs[q, height:] for q in range(nq)], axis=0))
    pack(2, acc_ref[me, nq, height:] + theirs[nq, height:])

    probe_swap.wait()
    part[...] = pg_ref[me] + pg_theirs[...]

    def ty_copy(k):
        return remote(part.at[pl.ds(pl.multiple_of(k * chunk, chunk), chunk)], by_ty.at[ty], ty_send.at[k], ty_recv.at[ty], {"ty": k})

    def ty_arrival(k):
        return remote(part.at[pl.ds(0, chunk)], by_ty.at[k], ty_send.at[k], ty_recv.at[k], {"ty": k})

    @pl.loop(1, nty)
    def _(k):
        ty_copy(lax.rem(ty + k, nty)).start()

    by_ty[ty] = part[pl.ds(pl.multiple_of(ty * chunk, chunk), chunk)]

    for q in reversed(range(nq)):
        body[q].wait()
        out_ref[me, :, q * N:(q + 1) * N] = acc_ref[me, q, :height] + theirs[q, :height]

    early = [remote(out_ref.at[me, pl.ds(N, height - N), pl.ds(N, (nq - 1) * N)], out_ref.at[me, pl.ds(N, height - N), pl.ds(N, (nq - 1) * N)],
                    pair_send.at[2 + 2 * nq], pair_recv.at[2 + 2 * nq], peer)]
    early[0].start()

    @pl.loop(1, nty)
    def _(k):
        ty_arrival(lax.rem(ty + k, nty)).wait_recv()

    mine = by_ty[0]
    for k in range(1, nty):
        mine = mine + by_ty[k]
    by_tx[tx] = mine

    def tx_copy(k):
        return remote(by_tx.at[tx], by_tx.at[tx], tx_send.at[k], tx_recv.at[tx], {"tx": k})

    def tx_arrival(k):
        return remote(by_tx.at[tx], by_tx.at[k], tx_send.at[k], tx_recv.at[k], {"tx": k})

    @pl.loop(1, ntx)
    def _(k):
        tx_copy(lax.rem(tx + k, ntx)).start()

    @pl.when(gets[1])
    def _():
        for c in strip(1):
            c.wait_recv()
        for q in range(nq):
            out_ref[me, :N, q * N:(q + 1) * N] += decode(code_in[pl.ds(offs[1] + q * N, N)], step_in[1])

    @pl.when(gets[2])
    def _():
        for c in strip(2):
            c.wait_recv()
        out_ref[me, :N, :N] += decode(code_in[pl.ds(offs[2], N)], step_in[2])

    @pl.when(gets[0])
    def _():
        for c in strip(0):
            c.wait_recv()
        out_ref[me, :, :N] += decode(code_in[pl.ds(0, height)], step_in[0])

    late = [remote(out_ref.at[me, :, pl.ds(0, N)], out_ref.at[me, :, pl.ds(0, N)],
                   pair_send.at[3 + 2 * nq], pair_recv.at[3 + 2 * nq], peer),
            remote(out_ref.at[me, pl.ds(0, N), pl.ds(N, (nq - 1) * N)], out_ref.at[me, pl.ds(0, N), pl.ds(N, (nq - 1) * N)],
                   pair_send.at[4 + 2 * nq], pair_recv.at[4 + 2 * nq], peer)]
    for c in late:
        c.start()

    @pl.loop(1, ntx)
    def _(k):
        tx_arrival(lax.rem(tx + k, ntx)).wait_recv()

    mine = by_tx[0]
    for k in range(1, ntx):
        mine = mine + by_tx[k]
    pgo_ref[me, pl.ds(pl.multiple_of(ty * chunk, chunk), chunk)] = mine / total

    def all_copy(k, at):
        place = pgo_ref.at[me, pl.ds(pl.multiple_of(at * chunk, chunk), chunk)]
        return remote(place, place, all_send.at[k], all_recv.at[at], {"ty": k})

    @pl.loop(1, nty)
    def _(k):
        all_copy(lax.rem(ty + k, nty), ty).start()

    @pl.loop(1, nty)
    def _(k):
        at = lax.rem(ty + k, nty)
        all_copy(at, at).wait_recv()

    last = swap(5 + 2 * nq, pgo_ref.at[me], pgo_ref.at[me])
    last.start()

    for n in range(3):
        @pl.when(sends[n])
        def _():
            for c in strip(n):
                c.wait_send()

    @pl.loop(1, nty)
    def _(k):
        at = lax.rem(ty + k, nty)
        ty_copy(at).wait_send()
        all_copy(at, ty).wait_send()

    @pl.loop(1, ntx)
    def _(k):
        tx_copy(lax.rem(tx + k, ntx)).wait_send()

    for c in early + late:
        c.wait()
    last.wait()


def collect(counts, acc, pg, height, width):
    nty, ntx = lax.axis_size("ty"), lax.axis_size("tx")
    nq = width // N
    rows = height + nq * N + N
    chunk = N // nty
    vmem = pl.BlockSpec(memory_space=pltpu.VMEM)
    return pl.pallas_call(
        functools.partial(collect_kernel, nty, ntx),
        out_shape=(jax.ShapeDtypeStruct((2, height, width), jnp.float32), jax.ShapeDtypeStruct((2, N, N), jnp.float32)),
        in_specs=[vmem] * 3,
        out_specs=(vmem, vmem),
        scratch_shapes=[
            pltpu.VMEM((nq + 1, height + N, N), jnp.float32),
            pltpu.VMEM((N, N), jnp.float32),
            pltpu.VMEM((rows, N), jnp.int16),
            pltpu.VMEM((3, 8, N), jnp.float32),
            pltpu.VMEM((rows, N), jnp.int16),
            pltpu.VMEM((3, 8, N), jnp.float32),
            pltpu.VMEM((nty, chunk, N), jnp.float32),
            pltpu.VMEM((ntx, chunk, N), jnp.float32),
            pltpu.VMEM((N, N), jnp.float32),
            pltpu.SemaphoreType.DMA((6 + 2 * nq,)),
            pltpu.SemaphoreType.DMA((6 + 2 * nq,)),
            pltpu.SemaphoreType.DMA((6,)),
            pltpu.SemaphoreType.DMA((6,)),
            pltpu.SemaphoreType.DMA((nty,)),
            pltpu.SemaphoreType.DMA((nty,)),
            pltpu.SemaphoreType.DMA((ntx,)),
            pltpu.SemaphoreType.DMA((ntx,)),
            pltpu.SemaphoreType.DMA((nty,)),
            pltpu.SemaphoreType.DMA((nty,)),
        ],
        compiler_params=pltpu.CompilerParams(collective_id=1, has_side_effects=True, vmem_limit_bytes=40 << 20),
        name="collect",
    )(counts, acc, pg)


def dft_tables(length):
    freqs = np.arange(length)
    angle = (freqs[:, None] * freqs[None, :] % length) * (2.0 * math.pi / length)
    cosine = np.cos(angle) / math.sqrt(length)
    sine = np.sin(angle) / math.sqrt(length)
    forward = np.block([[cosine, -sine], [sine, cosine]]).astype(ml_dtypes.bfloat16)
    inverse = np.block([[cosine, sine], [-sine, cosine]]).astype(ml_dtypes.bfloat16)
    return forward, inverse

def mm(a, b):
    return jnp.dot(a, b, preferred_element_type=jnp.float32)

def patch_kernel(B, rows_ref, cols_ref, lim_ref, ext_ref, probe_ref, amp_ref, fwd_ref, inv_ref,
                 acc_ref, pg_ref, patch_ref):
    acc_ref[...] = jnp.zeros_like(acc_ref)
    pg_ref[...] = jnp.zeros_like(pg_ref)
    lane = lax.broadcasted_iota(jnp.int32, (N, N), 1)
    last = lim_ref[0]

    def body(it, _):
        pos = []
        psis = []
        for b in range(B):
            i = it * B + b
            slot = jnp.minimum(i, last - 1)
            r = rows_ref[slot]
            c = cols_ref[slot]
            j = c // N
            s = c % N
            pos.append((slot, i < last, r, j, s))
            back = (N - s) % N
            high = lane >= s
            parts = []
            for p in range(2):
                v = jnp.where(high, ext_ref[p, j, pl.ds(r, N), :], ext_ref[p, j + 1, pl.ds(r, N), :])
                v = pltpu.roll(v, back, 1)
                patch_ref[b, p] = v
                parts.append(v)
            pre, pim = probe_ref[0], probe_ref[1]
            psi_re = pre * parts[0] - pim * parts[1]
            psi_im = pre * parts[1] + pim * parts[0]
            psis.append(jnp.concatenate([psi_re.astype(jnp.bfloat16), psi_im.astype(jnp.bfloat16)], axis=1))
        half = mm(jnp.concatenate(psis, axis=0), fwd_ref[...]).astype(jnp.bfloat16)
        rhs = jnp.concatenate(
            [jnp.concatenate([half[b * N:(b + 1) * N, q * N:(q + 1) * N] for b in range(B)], axis=1) for q in range(2)], axis=0)
        wave = mm(inv_ref[...], rhs)
        chis = [[], []]
        for b in range(B):
            slot, ok, r, j, s = pos[b]
            wre = wave[:N, b * N:(b + 1) * N]
            wim = wave[N:, b * N:(b + 1) * N]
            level = amp_ref[slot].astype(jnp.float32)
            use = ok.astype(jnp.float32)
            factor = (1.0 - level * lax.rsqrt(wre * wre + wim * wim + 1.0)) * use
            chis[0].append((wre * factor).astype(jnp.bfloat16))
            chis[1].append((wim * factor).astype(jnp.bfloat16))
        rhs2 = jnp.concatenate([jnp.concatenate(chis[q], axis=1) for q in range(2)], axis=0)
        bk = mm(fwd_ref[...], rhs2).astype(jnp.bfloat16)
        lhs = jnp.concatenate([jnp.concatenate([bk[q * N:(q + 1) * N, b * N:(b + 1) * N] for q in range(2)], axis=1) for b in range(B)], axis=0)
        grad = mm(lhs, inv_ref[...])
        tre = pg_ref[0]
        tim = pg_ref[1]
        for b in range(B):
            slot, ok, r, j, s = pos[b]
            gre = grad[b * N:(b + 1) * N, :N]
            gim = grad[b * N:(b + 1) * N, N:]
            pre, pim = probe_ref[0], probe_ref[1]
            qre, qim = patch_ref[b, 0], patch_ref[b, 1]
            tre = tre + (qre * gre + qim * gim)
            tim = tim + (qre * gim - qim * gre)
            obj = (pre * gre + pim * gim, pre * gim - pim * gre)
            high = lane >= s
            for p in range(2):
                o = pltpu.roll(obj[p], s, 1)
                acc_ref[p, j, pl.ds(r, N), :] += jnp.where(high, o, 0.0)
                acc_ref[p, j + 1, pl.ds(r, N), :] += jnp.where(high, 0.0, o)
        pg_ref[0] = tre
        pg_ref[1] = tim
        return 0

    lax.fori_loop(0, (last + B - 1) // B, body, 0)

def patches(rows, cols, lim, ext, probe, amp, fwd, inv, B=2):
    return pl.pallas_call(
        functools.partial(patch_kernel, B),
        out_shape=(jax.ShapeDtypeStruct(ext.shape, jnp.float32), jax.ShapeDtypeStruct((2, N, N), jnp.float32)),
        in_specs=[pl.BlockSpec(memory_space=pltpu.SMEM)] * 3 + [pl.BlockSpec(memory_space=pltpu.VMEM)] * 5,
        out_specs=(pl.BlockSpec(memory_space=pltpu.VMEM),) * 2,
        scratch_shapes=[pltpu.VMEM((B, 2, N, N), jnp.float32)],
        compiler_params=pltpu.CompilerParams(vmem_limit_bytes=48 << 20),
        name="patches",
    )(rows, cols, lim, ext, probe, amp, fwd, inv)


def from_behind(value, axis, steps):
    count = lax.axis_size(axis)
    initial, last = (max(0, -steps), min(count, count - steps))
    return lax.ppermute(value, axis, [(source, source + steps) for source in range(initial, last)])


def shards(object_field, probe_field, amplitudes, start_row, start_col, counts):
    height, width = object_field.shape[1:]
    half = start_row.shape[-1]
    row_place = lax.axis_index("ty")
    col_place = lax.axis_index("tx")
    core_place = lax.axis_index("pa")
    right = from_behind(object_field[:, :, :N], "tx", -1)
    top = jnp.concatenate([object_field[:, :N], right[:, :N]], axis=2)
    below = from_behind(top, "ty", -1)
    blocks = [object_field[:, :, q * N:(q + 1) * N] for q in range(width // N)] + [right]
    extended = jnp.stack(
        [jnp.concatenate([block, below[:, :, q * N:(q + 1) * N]], axis=1) for q, block in enumerate(blocks)], axis=1
    )
    nvalid = jnp.clip(counts[row_place, col_place] - core_place * half, 0, half)
    forward, inverse = dft_tables(N)
    grad, probe_part = patches(
        start_row[0, 0], start_col[0, 0], nvalid[None], extended, probe_field, amplitudes[0, 0],
        jnp.asarray(forward), jnp.asarray(inverse), BLK)
    return collect(counts, grad, probe_part, height, width)


def solution(mesh):
    return jax.shard_map(
        shards,
        mesh=mesh,
        in_specs=(
            P(None, "ty", "tx"),
            P(),
            P("ty", "tx", "pa", None, None),
            P("ty", "tx", "pa"),
            P("ty", "tx", "pa"),
            P(),
        ),
        out_specs=(P(None, "ty", "tx"), P()),
        check_vma=False,
    )
```

```python
import functools
import math

import jax
import jax.numpy as jnp
import ml_dtypes
import numpy as np
from jax import lax
from jax.experimental import pallas as pl
from jax.experimental.pallas import tpu as pltpu
from jax.sharding import PartitionSpec as P

BLK = 8

N = 128
LEVELS = 32766.0
MESH = pl.DeviceIdType.MESH


def encode(x):
    rows = x.shape[0]
    tiles = x.reshape(rows // 8, 8, N)
    peak = jnp.max(jnp.abs(tiles), axis=0)
    scaled = tiles * (LEVELS / jnp.maximum(peak, 1e-30))[None]
    return jnp.round(scaled.reshape(rows, N)).astype(jnp.int32).astype(jnp.int16), peak * (1.0 / LEVELS)


def decode(code, step):
    rows = code.shape[0]
    value = code.astype(jnp.int32).astype(jnp.float32)
    return (value.reshape(rows // 8, 8, N) * step[None]).reshape(rows, N)


def remote(src, dst, send_sem, recv_sem, where):
    return pltpu.make_async_remote_copy(
        src_ref=src, dst_ref=dst, send_sem=send_sem, recv_sem=recv_sem, device_id=where, device_id_type=MESH)


def collect_kernel(nty, ntx, zh, zl, counts_ref, acc_ref, pg_ref, out_ref, pgo_ref,
                   theirs, pg_theirs, code_out, step_out, code_in, step_in, by_line, by_plane, part,
                   pair_send, pair_recv, strip_send, strip_recv, line_send, line_recv, plane_send, plane_recv, all_send, all_recv):
    ty, tx, me = lax.axis_index("ty"), lax.axis_index("tx"), lax.axis_index("pa")
    other = 1 - me
    height = out_ref.shape[1]
    nq = out_ref.shape[2] // N
    peer = {"pa": other}
    nline, nplane = zh * zl, (nty // zh) * (ntx // zl)
    chunk = N // nline
    line_id = lax.rem(ty, zh) * zl + lax.rem(tx, zl)
    plane_id = (ty // zh) * (ntx // zl) + tx // zl

    def in_line(k):
        return {"ty": (ty // zh) * zh + k // zl, "tx": (tx // zl) * zl + lax.rem(k, zl)}

    def in_plane(k):
        return {"ty": (k // (ntx // zl)) * zh + lax.rem(ty, zh), "tx": lax.rem(k, ntx // zl) * zl + lax.rem(tx, zl)}

    def next_in_line(k):
        return lax.rem(line_id + k, nline)

    def next_in_plane(k):
        return lax.rem(plane_id + k, nplane)

    sizes = (height, nq * N, N)
    offs = (0, height, height + nq * N)
    targets = ({"tx": lax.rem(tx + 1, ntx)}, {"ty": lax.rem(ty + 1, nty)},
               {"tx": lax.rem(tx + 1, ntx), "ty": lax.rem(ty + 1, nty)})
    sources = ({"tx": lax.rem(tx + ntx - 1, ntx)}, {"ty": lax.rem(ty + nty - 1, nty)},
               {"tx": lax.rem(tx + ntx - 1, ntx), "ty": lax.rem(ty + nty - 1, nty)})
    sends = (tx < ntx - 1, ty < nty - 1, jnp.logical_and(tx < ntx - 1, ty < nty - 1))
    gets = (tx > 0, ty > 0, jnp.logical_and(tx > 0, ty > 0))

    barrier = pltpu.get_barrier_semaphore()
    for where in (peer,) + targets + sources:
        pl.semaphore_signal(barrier, inc=1, device_id=where, device_id_type=MESH)

    @pl.loop(1, nline)
    def _(k):
        pl.semaphore_signal(barrier, inc=1, device_id=in_line(next_in_line(k)), device_id_type=MESH)

    @pl.loop(1, nplane)
    def _(k):
        pl.semaphore_signal(barrier, inc=1, device_id=in_plane(next_in_plane(k)), device_id_type=MESH)

    total = jnp.sum(jnp.sum(counts_ref[...].astype(jnp.float32), axis=1, keepdims=True), axis=0, keepdims=True)
    pl.semaphore_wait(barrier, 1 + 6 + nline - 1 + nplane - 1)

    def swap(n, src, dst):
        return remote(src, dst, pair_send.at[n], pair_recv.at[n], peer)

    probe_swap = swap(1 + nq, pg_ref.at[other], pg_theirs)
    right = swap(0, acc_ref.at[other, nq], theirs.at[nq])
    low = [swap(1 + q, acc_ref.at[other, q, pl.ds(height, N)], theirs.at[q, pl.ds(height, N)]) for q in range(nq)]
    body = [swap(2 + nq + q, acc_ref.at[other, q, pl.ds(0, height)], theirs.at[q, pl.ds(0, height)]) for q in range(nq)]
    probe_swap.start()
    for c in low:
        c.start()
    right.start()
    for c in reversed(body):
        c.start()

    def strip(n):
        size, off = sizes[n], offs[n]
        return (remote(code_out.at[pl.ds(off, size)], code_in.at[pl.ds(off, size)],
                       strip_send.at[2 * n], strip_recv.at[2 * n], targets[n]),
                remote(step_out.at[n], step_in.at[n], strip_send.at[2 * n + 1], strip_recv.at[2 * n + 1], targets[n]))

    def pack(n, value):
        code_out[pl.ds(offs[n], sizes[n])], step_out[n] = encode(value)

        @pl.when(sends[n])
        def _():
            for c in strip(n):
                c.start()

    def rows_of(k):
        return pl.ds(pl.multiple_of(k * chunk, chunk), chunk)

    def line_copy(k):
        return remote(part.at[rows_of(k)], by_line.at[line_id], line_send.at[k], line_recv.at[line_id], in_line(k))

    def line_arrival(k):
        return remote(part.at[rows_of(k)], by_line.at[k], line_send.at[k], line_recv.at[k], in_line(k))

    def plane_copy(k):
        return remote(by_plane.at[plane_id], by_plane.at[plane_id], plane_send.at[k], plane_recv.at[plane_id], in_plane(k))

    def plane_arrival(k):
        return remote(by_plane.at[plane_id], by_plane.at[k], plane_send.at[k], plane_recv.at[k], in_plane(k))

    def all_copy(k, at):
        place = pgo_ref.at[me, rows_of(at)]
        return remote(place, place, all_send.at[k], all_recv.at[at], in_line(k))

    probe_swap.wait()
    part[...] = pg_ref[me] + pg_theirs[...]

    @pl.loop(1, nline)
    def _(k):
        line_copy(next_in_line(k)).start()

    by_line[line_id] = part[rows_of(line_id)]

    for c in low:
        c.wait()
    pack(1, jnp.concatenate([acc_ref[me, q, height:] + theirs[q, height:] for q in range(nq)], axis=0))
    right.wait()
    pack(2, acc_ref[me, nq, height:] + theirs[nq, height:])
    pack(0, acc_ref[me, nq, :height] + theirs[nq, :height])

    @pl.loop(1, nline)
    def _(k):
        line_arrival(next_in_line(k)).wait_recv()

    mine = by_line[0]
    for k in range(1, nline):
        mine = mine + by_line[k]
    by_plane[plane_id] = mine

    @pl.loop(1, nplane)
    def _(k):
        plane_copy(next_in_plane(k)).start()

    for q in reversed(range(nq)):
        body[q].wait()
        out_ref[me, :, q * N:(q + 1) * N] = acc_ref[me, q, :height] + theirs[q, :height]

    def final(n, rows, columns):
        place = out_ref.at[me, rows, columns]
        return swap(n, place, place)

    rest = pl.ds(N, (nq - 1) * N)
    early = final(2 + 2 * nq, pl.ds(N, height - N), rest)
    early.start()

    @pl.loop(1, nplane)
    def _(k):
        plane_arrival(next_in_plane(k)).wait_recv()

    mine = by_plane[0]
    for k in range(1, nplane):
        mine = mine + by_plane[k]
    pgo_ref[me, rows_of(line_id)] = mine / total

    @pl.loop(1, nline)
    def _(k):
        all_copy(next_in_line(k), line_id).start()

    @pl.when(gets[1])
    def _():
        for c in strip(1):
            c.wait_recv()
        for q in range(nq):
            out_ref[me, :N, q * N:(q + 1) * N] += decode(code_in[pl.ds(offs[1] + q * N, N)], step_in[1])

    @pl.when(gets[2])
    def _():
        for c in strip(2):
            c.wait_recv()
        out_ref[me, :N, :N] += decode(code_in[pl.ds(offs[2], N)], step_in[2])

    @pl.when(gets[0])
    def _():
        for c in strip(0):
            c.wait_recv()
        out_ref[me, :, :N] += decode(code_in[pl.ds(0, height)], step_in[0])

    late = [final(3 + 2 * nq, pl.ds(0, height), pl.ds(0, N)), final(4 + 2 * nq, pl.ds(0, N), rest)]
    for c in late:
        c.start()

    @pl.loop(1, nline)
    def _(k):
        at = next_in_line(k)
        all_copy(at, at).wait_recv()

    last = swap(5 + 2 * nq, pgo_ref.at[me], pgo_ref.at[me])
    last.start()

    for n in range(3):
        @pl.when(sends[n])
        def _():
            for c in strip(n):
                c.wait_send()

    @pl.loop(1, nline)
    def _(k):
        at = next_in_line(k)
        line_copy(at).wait_send()
        all_copy(at, line_id).wait_send()

    @pl.loop(1, nplane)
    def _(k):
        plane_copy(next_in_plane(k)).wait_send()

    early.wait()
    for c in late:
        c.wait()
    last.wait()


def collect(counts, acc, pg, height, width, zh=2, zl=4):
    nty, ntx = lax.axis_size("ty"), lax.axis_size("tx")
    nq = width // N
    rows = height + nq * N + N
    nline, nplane = zh * zl, (nty // zh) * (ntx // zl)
    chunk = N // nline
    vmem = pl.BlockSpec(memory_space=pltpu.VMEM)
    dma = pltpu.SemaphoreType.DMA
    return pl.pallas_call(
        functools.partial(collect_kernel, nty, ntx, zh, zl),
        out_shape=(jax.ShapeDtypeStruct((2, height, width), jnp.float32), jax.ShapeDtypeStruct((2, N, N), jnp.float32)),
        in_specs=[vmem] * 3,
        out_specs=(vmem, vmem),
        scratch_shapes=[
            pltpu.VMEM((nq + 1, height + N, N), jnp.float32),
            pltpu.VMEM((N, N), jnp.float32),
            pltpu.VMEM((rows, N), jnp.int16),
            pltpu.VMEM((3, 8, N), jnp.float32),
            pltpu.VMEM((rows, N), jnp.int16),
            pltpu.VMEM((3, 8, N), jnp.float32),
            pltpu.VMEM((nline, chunk, N), jnp.float32),
            pltpu.VMEM((nplane, chunk, N), jnp.float32),
            pltpu.VMEM((N, N), jnp.float32),
            dma((6 + 2 * nq,)), dma((6 + 2 * nq,)), dma((6,)), dma((6,)),
            dma((nline,)), dma((nline,)), dma((nplane,)), dma((nplane,)), dma((nline,)), dma((nline,)),
        ],
        compiler_params=pltpu.CompilerParams(collective_id=1, has_side_effects=True, vmem_limit_bytes=40 << 20),
        name="collect",
    )(counts, acc, pg)


def spread_kernel(nty, ntx, cuts, obj_ref, amp_ref, rows_ref, cols_ref, ext_ref, shared_ref, list_ref,
                  spots, local_sem, strip_send, strip_recv, pair_send, pair_recv):
    ty, tx, me = lax.axis_index("ty"), lax.axis_index("tx"), lax.axis_index("pa")
    other = 1 - me
    height = obj_ref.shape[1]
    nq = obj_ref.shape[2] // N
    slots = amp_ref.shape[0]
    moved = slots // 2
    peer = {"pa": other}
    up, down = lax.rem(ty + nty - 1, nty), lax.rem(ty + 1, nty)
    left, right = lax.rem(tx + ntx - 1, ntx), lax.rem(tx + 1, ntx)

    barrier = pltpu.get_barrier_semaphore()
    for where in (peer, {"tx": left}, {"tx": right}, {"ty": up}, {"ty": down}, {"tx": left, "ty": up}, {"tx": right, "ty": down}):
        pl.semaphore_signal(barrier, inc=1, device_id=where, device_id_type=MESH)

    local = [pltpu.make_async_copy(obj_ref.at[p, :, pl.ds(q * N, N)], ext_ref.at[p, q, pl.ds(0, height)], local_sem.at[p * nq + q])
             for p in range(2) for q in range(nq)]
    local.append(pltpu.make_async_copy(amp_ref, shared_ref.at[pl.ds(me * moved, slots)], local_sem.at[2 * nq]))
    places = [pltpu.make_async_copy(rows_ref, spots.at[0], local_sem.at[2 * nq + 1]),
              pltpu.make_async_copy(cols_ref, spots.at[1], local_sem.at[2 * nq + 2])]
    for c in places + local:
        c.start()
    for c in places:
        c.wait()
    list_ref[me, 0:1, :slots] = spots[0, 0]
    list_ref[me, 1:2, :slots] = spots[1, 0]

    step = height // cuts
    has_right, has_below = tx < ntx - 1, ty < nty - 1
    gives_left, gives_up = tx > 0, ty > 0
    pieces = [(gives_up, has_below, {"ty": up}, q, height, 0, N, q) for q in range(nq)]
    pieces.append((jnp.logical_and(gives_left, gives_up), jnp.logical_and(has_right, has_below), {"tx": left, "ty": up}, nq, height, 0, N, 0))
    pieces += [(gives_left, has_right, {"tx": left}, nq, k * step, k * step, step, 0) for k in range(cuts)]

    def strip(n):
        _, _, where, q, row, first, size, source = pieces[n]
        return remote(obj_ref.at[me, pl.ds(first, size), pl.ds(source * N, N)], ext_ref.at[me, q, pl.ds(row, size)],
                      strip_send.at[n], strip_recv.at[n], where)

    def forward(n):
        _, _, _, q, row, _, size, _ = pieces[n]
        place = ext_ref.at[me, q, pl.ds(row, size)]
        return remote(place, place, pair_send.at[n], pair_recv.at[n], peer)

    pl.semaphore_wait(barrier, 7)
    for n, piece in enumerate(pieces):
        @pl.when(piece[0])
        def _():
            strip(n).start()

    extra = len(pieces)
    lists = remote(list_ref.at[me], list_ref.at[me], pair_send.at[extra], pair_recv.at[extra], peer)
    lists.start()
    move = remote(amp_ref.at[pl.ds(moved, slots - moved)], shared_ref.at[pl.ds(0, slots - moved)],
                  pair_send.at[extra + 1], pair_recv.at[extra + 1], peer)

    @pl.when(me == 0)
    def _():
        move.start()

    for n, piece in enumerate(pieces):
        @pl.when(jnp.logical_not(piece[1]))
        def _():
            _, _, _, q, row, _, size, _ = piece
            for p in range(2):
                ext_ref[p, q, row:row + size] = jnp.zeros((size, N), jnp.float32)

    order = list(range(nq + 1, len(pieces))) + list(range(nq + 1))
    for n in order:
        @pl.when(pieces[n][1])
        def _():
            strip(n).wait_recv()
            forward(n).start()

    for c in local:
        c.wait()
    lists.wait()

    @pl.when(me == 0)
    def _():
        move.wait_send()

    @pl.when(me == 1)
    def _():
        move.wait_recv()

    for n, piece in enumerate(pieces):
        @pl.when(piece[0])
        def _():
            strip(n).wait_send()

        @pl.when(piece[1])
        def _():
            forward(n).wait()


def spread(obj, amp, rows, cols, cuts=4):
    nty, ntx = lax.axis_size("ty"), lax.axis_size("tx")
    height, width = obj.shape[1:]
    slots = amp.shape[0]
    nq = width // N
    pieces = nq + 1 + cuts
    vmem = pl.BlockSpec(memory_space=pltpu.VMEM)
    hbm = pl.BlockSpec(memory_space=pltpu.HBM)
    dma = pltpu.SemaphoreType.DMA
    return pl.pallas_call(
        functools.partial(spread_kernel, nty, ntx, cuts),
        out_shape=(
            jax.ShapeDtypeStruct((2, nq + 1, height + N, N), jnp.float32),
            jax.ShapeDtypeStruct((slots + slots // 2, N, N), jnp.bfloat16),
            jax.ShapeDtypeStruct((2, 8, N), jnp.int32),
        ),
        in_specs=[hbm] * 4,
        out_specs=(vmem, vmem, vmem),
        scratch_shapes=[
            pltpu.VMEM((2, 1, 1, slots), jnp.int32),
            dma((2 * nq + 3,)), dma((pieces,)), dma((pieces,)), dma((pieces + 2,)), dma((pieces + 2,)),
        ],
        compiler_params=pltpu.CompilerParams(collective_id=0, has_side_effects=True, vmem_limit_bytes=40 << 20),
        name="spread",
    )(obj, amp, rows, cols)


def dft_tables(length):
    freqs = np.arange(length)
    angle = (freqs[:, None] * freqs[None, :] % length) * (2.0 * math.pi / length)
    cosine = np.cos(angle) / math.sqrt(length)
    sine = np.sin(angle) / math.sqrt(length)
    forward = np.block([[cosine, -sine], [sine, cosine]]).astype(ml_dtypes.bfloat16)
    inverse = np.block([[cosine, sine], [-sine, cosine]]).astype(ml_dtypes.bfloat16)
    return forward, inverse

def mm(a, b):
    return jnp.dot(a, b, preferred_element_type=jnp.float32)

def patch_kernel(B, slots, counts_ref, list_ref, ext_ref, probe_ref, amp_ref, fwd_ref, inv_ref,
                 acc_ref, pg_ref, patch_ref):
    acc_ref[...] = jnp.zeros_like(acc_ref)
    pg_ref[...] = jnp.zeros_like(pg_ref)
    lane = lax.broadcasted_iota(jnp.int32, (N, N), 1)
    me = lax.axis_index("pa")
    count = counts_ref[lax.axis_index("ty"), lax.axis_index("tx")]
    moved = slots // 2
    split = jnp.maximum((count + 1) // 2, jnp.minimum(count, moved))
    first = jnp.where(me == 0, 0, split)
    last = jnp.where(me == 0, split, count)

    def body(it, _):
        pos = []
        psis = []
        for b in range(B):
            i = first + it * B + b
            number = jnp.minimum(i, last - 1)
            r = list_ref[number // slots, 0, number % slots]
            c = list_ref[number // slots, 1, number % slots]
            slot = number - me * moved
            j = c // N
            s = c % N
            pos.append((slot, i < last, r, j, s))
            back = (N - s) % N
            high = lane >= s
            parts = []
            for p in range(2):
                v = jnp.where(high, ext_ref[p, j, pl.ds(r, N), :], ext_ref[p, j + 1, pl.ds(r, N), :])
                v = pltpu.roll(v, back, 1)
                patch_ref[b, p] = v
                parts.append(v)
            pre, pim = probe_ref[0], probe_ref[1]
            psi_re = pre * parts[0] - pim * parts[1]
            psi_im = pre * parts[1] + pim * parts[0]
            psis.append(jnp.concatenate([psi_re.astype(jnp.bfloat16), psi_im.astype(jnp.bfloat16)], axis=1))
        half = mm(jnp.concatenate(psis, axis=0), fwd_ref[...]).astype(jnp.bfloat16)
        rhs = jnp.concatenate(
            [jnp.concatenate([half[b * N:(b + 1) * N, q * N:(q + 1) * N] for b in range(B)], axis=1) for q in range(2)], axis=0)
        wave = mm(inv_ref[...], rhs)
        chis = [[], []]
        for b in range(B):
            slot, ok, r, j, s = pos[b]
            wre = wave[:N, b * N:(b + 1) * N]
            wim = wave[N:, b * N:(b + 1) * N]
            level = amp_ref[slot].astype(jnp.float32)
            use = ok.astype(jnp.float32)
            factor = (1.0 - level * lax.rsqrt(wre * wre + wim * wim + 1.0)) * use
            chis[0].append((wre * factor).astype(jnp.bfloat16))
            chis[1].append((wim * factor).astype(jnp.bfloat16))
        rhs2 = jnp.concatenate([jnp.concatenate(chis[q], axis=1) for q in range(2)], axis=0)
        bk = mm(fwd_ref[...], rhs2).astype(jnp.bfloat16)
        lhs = jnp.concatenate([jnp.concatenate([bk[q * N:(q + 1) * N, b * N:(b + 1) * N] for q in range(2)], axis=1) for b in range(B)], axis=0)
        grad = mm(lhs, inv_ref[...])
        tre = pg_ref[0]
        tim = pg_ref[1]
        for b in range(B):
            slot, ok, r, j, s = pos[b]
            gre = grad[b * N:(b + 1) * N, :N]
            gim = grad[b * N:(b + 1) * N, N:]
            pre, pim = probe_ref[0], probe_ref[1]
            qre, qim = patch_ref[b, 0], patch_ref[b, 1]
            tre = tre + (qre * gre + qim * gim)
            tim = tim + (qre * gim - qim * gre)
            obj = (pre * gre + pim * gim, pre * gim - pim * gre)
            high = lane >= s
            for p in range(2):
                o = pltpu.roll(obj[p], s, 1)
                acc_ref[p, j, pl.ds(r, N), :] += jnp.where(high, o, 0.0)
                acc_ref[p, j + 1, pl.ds(r, N), :] += jnp.where(high, 0.0, o)
        pg_ref[0] = tre
        pg_ref[1] = tim
        return 0

    lax.fori_loop(0, (last - first + B - 1) // B, body, 0)

def patches(counts, lists, ext, probe, amp, fwd, inv, B):
    smem = pl.BlockSpec(memory_space=pltpu.SMEM)
    vmem = pl.BlockSpec(memory_space=pltpu.VMEM)
    return pl.pallas_call(
        functools.partial(patch_kernel, B, amp.shape[0] * 2 // 3),
        out_shape=(jax.ShapeDtypeStruct(ext.shape, jnp.float32), jax.ShapeDtypeStruct((2, N, N), jnp.float32)),
        in_specs=[smem] * 2 + [vmem] * 5,
        out_specs=(vmem, vmem),
        scratch_shapes=[pltpu.VMEM((B, 2, N, N), jnp.float32)],
        compiler_params=pltpu.CompilerParams(vmem_limit_bytes=40 << 20),
        name="patches",
    )(counts, lists, ext, probe, amp, fwd, inv)


def shards(object_field, probe_field, amplitudes, start_row, start_col, counts):
    height, width = object_field.shape[1:]
    extended, shared, lists = spread(object_field, amplitudes[0, 0], start_row, start_col)
    forward, inverse = dft_tables(N)
    grad, probe_part = patches(
        counts, lists, extended, probe_field, shared, jnp.asarray(forward), jnp.asarray(inverse), BLK)
    return collect(counts, grad, probe_part, height, width)


def solution(mesh):
    return jax.shard_map(
        shards,
        mesh=mesh,
        in_specs=(
            P(None, "ty", "tx"),
            P(),
            P("ty", "tx", "pa", None, None),
            P("ty", "tx", "pa"),
            P("ty", "tx", "pa"),
            P(),
        ),
        out_specs=(P(None, "ty", "tx"), P()),
        check_vma=False,
    )
```

```python
import functools
import math

import jax
import jax.numpy as jnp
import ml_dtypes
import numpy as np
from jax import lax
from jax.experimental import pallas as pl
from jax.experimental.pallas import tpu as pltpu
from jax.sharding import PartitionSpec as P

BLK = 8

N = 128
LEVELS = 32766.0
MESH = pl.DeviceIdType.MESH


def encode(x):
    rows = x.shape[0]
    tiles = x.reshape(rows // 8, 8, N)
    peak = jnp.max(jnp.abs(tiles), axis=0)
    scaled = tiles * (LEVELS / jnp.maximum(peak, 1e-30))[None]
    return jnp.round(scaled.reshape(rows, N)).astype(jnp.int32).astype(jnp.int16), peak * (1.0 / LEVELS)


def decode(code, step):
    rows = code.shape[0]
    value = code.astype(jnp.int32).astype(jnp.float32)
    return (value.reshape(rows // 8, 8, N) * step[None]).reshape(rows, N)


def remote(src, dst, send_sem, recv_sem, where):
    return pltpu.make_async_remote_copy(
        src_ref=src, dst_ref=dst, send_sem=send_sem, recv_sem=recv_sem, device_id=where, device_id_type=MESH)


def collect_kernel(nty, ntx, zh, zl, counts_ref, acc_ref, pg_ref, out_ref, pgo_ref,
                   theirs, pg_theirs, code_out, step_out, code_in, step_in, by_line, by_plane, part,
                   pair_send, pair_recv, strip_send, strip_recv, line_send, line_recv, plane_send, plane_recv, all_send, all_recv):
    ty, tx, me = lax.axis_index("ty"), lax.axis_index("tx"), lax.axis_index("pa")
    other = 1 - me
    height = out_ref.shape[1]
    nq = out_ref.shape[2] // N
    peer = {"pa": other}
    nline, nplane = zh * zl, (nty // zh) * (ntx // zl)
    chunk = N // nline
    line_id = lax.rem(ty, zh) * zl + lax.rem(tx, zl)
    plane_id = (ty // zh) * (ntx // zl) + tx // zl

    def in_line(k):
        return {"ty": (ty // zh) * zh + k // zl, "tx": (tx // zl) * zl + lax.rem(k, zl)}

    def in_plane(k):
        return {"ty": (k // (ntx // zl)) * zh + lax.rem(ty, zh), "tx": lax.rem(k, ntx // zl) * zl + lax.rem(tx, zl)}

    def next_in_line(k):
        return lax.rem(line_id + k, nline)

    def next_in_plane(k):
        return lax.rem(plane_id + k, nplane)

    sizes = (height, nq * N, N)
    offs = (0, height, height + nq * N)
    targets = ({"tx": lax.rem(tx + 1, ntx)}, {"ty": lax.rem(ty + 1, nty)},
               {"tx": lax.rem(tx + 1, ntx), "ty": lax.rem(ty + 1, nty)})
    sources = ({"tx": lax.rem(tx + ntx - 1, ntx)}, {"ty": lax.rem(ty + nty - 1, nty)},
               {"tx": lax.rem(tx + ntx - 1, ntx), "ty": lax.rem(ty + nty - 1, nty)})
    sends = (tx < ntx - 1, ty < nty - 1, jnp.logical_and(tx < ntx - 1, ty < nty - 1))
    gets = (tx > 0, ty > 0, jnp.logical_and(tx > 0, ty > 0))

    barrier = pltpu.get_barrier_semaphore()
    for where in (peer,) + targets + sources:
        pl.semaphore_signal(barrier, inc=1, device_id=where, device_id_type=MESH)

    @pl.loop(1, nline)
    def _(k):
        pl.semaphore_signal(barrier, inc=1, device_id=in_line(next_in_line(k)), device_id_type=MESH)

    @pl.loop(1, nplane)
    def _(k):
        pl.semaphore_signal(barrier, inc=1, device_id=in_plane(next_in_plane(k)), device_id_type=MESH)

    total = jnp.sum(jnp.sum(counts_ref[...].astype(jnp.float32), axis=1, keepdims=True), axis=0, keepdims=True)
    pl.semaphore_wait(barrier, 1 + 6 + nline - 1 + nplane - 1)

    def swap(n, src, dst):
        return remote(src, dst, pair_send.at[n], pair_recv.at[n], peer)

    probe_swap = swap(1 + nq, pg_ref.at[other], pg_theirs)
    right = swap(0, acc_ref.at[other, nq], theirs.at[nq])
    low = [swap(1 + q, acc_ref.at[other, q, pl.ds(height, N)], theirs.at[q, pl.ds(height, N)]) for q in range(nq)]
    body = [swap(2 + nq + q, acc_ref.at[other, q, pl.ds(0, height)], theirs.at[q, pl.ds(0, height)]) for q in range(nq)]
    probe_swap.start()
    for c in low:
        c.start()
    right.start()
    for c in reversed(body):
        c.start()

    def strip(n):
        size, off = sizes[n], offs[n]
        return (remote(code_out.at[pl.ds(off, size)], code_in.at[pl.ds(off, size)],
                       strip_send.at[2 * n], strip_recv.at[2 * n], targets[n]),
                remote(step_out.at[n], step_in.at[n], strip_send.at[2 * n + 1], strip_recv.at[2 * n + 1], targets[n]))

    def pack(n, value):
        code_out[pl.ds(offs[n], sizes[n])], step_out[n] = encode(value)

        @pl.when(sends[n])
        def _():
            for c in strip(n):
                c.start()

    def rows_of(k):
        return pl.ds(pl.multiple_of(k * chunk, chunk), chunk)

    def line_copy(k):
        return remote(part.at[rows_of(k)], by_line.at[line_id], line_send.at[k], line_recv.at[line_id], in_line(k))

    def line_arrival(k):
        return remote(part.at[rows_of(k)], by_line.at[k], line_send.at[k], line_recv.at[k], in_line(k))

    def plane_copy(k):
        return remote(by_plane.at[plane_id], by_plane.at[plane_id], plane_send.at[k], plane_recv.at[plane_id], in_plane(k))

    def plane_arrival(k):
        return remote(by_plane.at[plane_id], by_plane.at[k], plane_send.at[k], plane_recv.at[k], in_plane(k))

    def all_copy(k, at):
        place = pgo_ref.at[me, rows_of(at)]
        return remote(place, place, all_send.at[k], all_recv.at[at], in_line(k))

    probe_swap.wait()
    part[...] = pg_ref[me] + pg_theirs[...]

    @pl.loop(1, nline)
    def _(k):
        line_copy(next_in_line(k)).start()

    by_line[line_id] = part[rows_of(line_id)]

    for c in low:
        c.wait()
    pack(1, jnp.concatenate([acc_ref[me, q, height:] + theirs[q, height:] for q in range(nq)], axis=0))
    right.wait()
    pack(2, acc_ref[me, nq, height:] + theirs[nq, height:])
    pack(0, acc_ref[me, nq, :height] + theirs[nq, :height])

    @pl.loop(1, nline)
    def _(k):
        line_arrival(next_in_line(k)).wait_recv()

    mine = by_line[0]
    for k in range(1, nline):
        mine = mine + by_line[k]
    by_plane[plane_id] = mine

    @pl.loop(1, nplane)
    def _(k):
        plane_copy(next_in_plane(k)).start()

    for q in reversed(range(nq)):
        body[q].wait()
        out_ref[me, :, q * N:(q + 1) * N] = acc_ref[me, q, :height] + theirs[q, :height]

    def final(n, rows, columns):
        place = out_ref.at[me, rows, columns]
        return swap(n, place, place)

    rest = pl.ds(N, (nq - 1) * N)
    early = final(2 + 2 * nq, pl.ds(N, height - N), rest)
    early.start()

    @pl.loop(1, nplane)
    def _(k):
        plane_arrival(next_in_plane(k)).wait_recv()

    mine = by_plane[0]
    for k in range(1, nplane):
        mine = mine + by_plane[k]
    pgo_ref[me, rows_of(line_id)] = mine / total

    @pl.loop(1, nline)
    def _(k):
        all_copy(next_in_line(k), line_id).start()

    @pl.when(gets[1])
    def _():
        for c in strip(1):
            c.wait_recv()
        for q in range(nq):
            out_ref[me, :N, q * N:(q + 1) * N] += decode(code_in[pl.ds(offs[1] + q * N, N)], step_in[1])

    @pl.when(gets[2])
    def _():
        for c in strip(2):
            c.wait_recv()
        out_ref[me, :N, :N] += decode(code_in[pl.ds(offs[2], N)], step_in[2])

    @pl.when(gets[0])
    def _():
        for c in strip(0):
            c.wait_recv()
        out_ref[me, :, :N] += decode(code_in[pl.ds(0, height)], step_in[0])

    late = [final(3 + 2 * nq, pl.ds(0, height), pl.ds(0, N)), final(4 + 2 * nq, pl.ds(0, N), rest)]
    for c in late:
        c.start()

    @pl.loop(1, nline)
    def _(k):
        at = next_in_line(k)
        all_copy(at, at).wait_recv()

    last = swap(5 + 2 * nq, pgo_ref.at[me], pgo_ref.at[me])
    last.start()

    for n in range(3):
        @pl.when(sends[n])
        def _():
            for c in strip(n):
                c.wait_send()

    @pl.loop(1, nline)
    def _(k):
        at = next_in_line(k)
        line_copy(at).wait_send()
        all_copy(at, line_id).wait_send()

    @pl.loop(1, nplane)
    def _(k):
        plane_copy(next_in_plane(k)).wait_send()

    early.wait()
    for c in late:
        c.wait()
    last.wait()


def collect(counts, acc, pg, height, width, zh=2, zl=4):
    nty, ntx = lax.axis_size("ty"), lax.axis_size("tx")
    nq = width // N
    rows = height + nq * N + N
    nline, nplane = zh * zl, (nty // zh) * (ntx // zl)
    chunk = N // nline
    vmem = pl.BlockSpec(memory_space=pltpu.VMEM)
    dma = pltpu.SemaphoreType.DMA
    return pl.pallas_call(
        functools.partial(collect_kernel, nty, ntx, zh, zl),
        out_shape=(jax.ShapeDtypeStruct((2, height, width), jnp.float32), jax.ShapeDtypeStruct((2, N, N), jnp.float32)),
        in_specs=[vmem] * 3,
        out_specs=(vmem, vmem),
        scratch_shapes=[
            pltpu.VMEM((nq + 1, height + N, N), jnp.float32),
            pltpu.VMEM((N, N), jnp.float32),
            pltpu.VMEM((rows, N), jnp.int16),
            pltpu.VMEM((3, 8, N), jnp.float32),
            pltpu.VMEM((rows, N), jnp.int16),
            pltpu.VMEM((3, 8, N), jnp.float32),
            pltpu.VMEM((nline, chunk, N), jnp.float32),
            pltpu.VMEM((nplane, chunk, N), jnp.float32),
            pltpu.VMEM((N, N), jnp.float32),
            dma((6 + 2 * nq,)), dma((6 + 2 * nq,)), dma((6,)), dma((6,)),
            dma((nline,)), dma((nline,)), dma((nplane,)), dma((nplane,)), dma((nline,)), dma((nline,)),
        ],
        compiler_params=pltpu.CompilerParams(collective_id=1, has_side_effects=True, vmem_limit_bytes=40 << 20),
        name="collect",
    )(counts, acc, pg)


WIDE = 524287.0
SPREAD_VMEM = 40 << 20


def encode_wide(x):
    rows = x.shape[0]
    tiles = x.reshape(rows // 8, 8, N)
    peak = jnp.max(jnp.abs(tiles), axis=0)
    scaled = tiles * (WIDE / jnp.maximum(peak, 1e-30))[None]
    number = jnp.round(scaled.reshape(rows, N)).astype(jnp.int32)
    return number, peak * (1.0 / WIDE)


def split_wide(number):
    quarter = number.shape[0] // 4
    low = number & 15
    word = -32768
    for g in range(4):
        word = word + (low[g * quarter:(g + 1) * quarter] << (4 * g))
    return (number >> 4).astype(jnp.int16), word.astype(jnp.int16)


def decode_wide(high, word, step):
    rows = high.shape[0]
    low = word.astype(jnp.int32) + 32768
    low = jnp.concatenate([(low >> (4 * g)) & 15 for g in range(4)], axis=0)
    value = ((high.astype(jnp.int32) << 4) + low).astype(jnp.float32)
    return (value.reshape(rows // 8, 8, N) * step[None]).reshape(rows, N)


def spread_kernel(nty, ntx, cuts, obj_ref, amp_ref, rows_ref, cols_ref, ext_ref, shared_ref, list_ref,
                  spots, code_out, step_out, code_in, step_in, code_pair, step_pair,
                  local_sem, strip_send, strip_recv, pair_send, pair_recv):
    ty, tx, me = lax.axis_index("ty"), lax.axis_index("tx"), lax.axis_index("pa")
    other = 1 - me
    height = obj_ref.shape[1]
    nq = obj_ref.shape[2] // N
    slots = amp_ref.shape[0]
    moved = slots // 2
    peer = {"pa": other}
    up, down = lax.rem(ty + nty - 1, nty), lax.rem(ty + 1, nty)
    left, right = lax.rem(tx + ntx - 1, ntx), lax.rem(tx + 1, ntx)

    barrier = pltpu.get_barrier_semaphore()
    for where in (peer, {"tx": left}, {"tx": right}, {"ty": up}, {"ty": down}, {"tx": left, "ty": up}, {"tx": right, "ty": down}):
        pl.semaphore_signal(barrier, inc=1, device_id=where, device_id_type=MESH)

    def load(p, q):
        return pltpu.make_async_copy(obj_ref.at[p, :, pl.ds(q * N, N)], ext_ref.at[p, q, pl.ds(0, height)], local_sem.at[p * nq + q])

    mine = [load(me, q) for q in range(nq)]
    local = [load(other, q) for q in range(nq)]
    local.append(pltpu.make_async_copy(amp_ref, shared_ref.at[pl.ds(me * moved, slots)], local_sem.at[2 * nq]))
    places = [pltpu.make_async_copy(rows_ref, spots.at[0], local_sem.at[2 * nq + 1]),
              pltpu.make_async_copy(cols_ref, spots.at[1], local_sem.at[2 * nq + 2])]
    for c in mine + places + local:
        c.start()

    size = height // cuts
    long, short = size * 5 // 4, N * 5 // 4
    has_right, has_below = tx < ntx - 1, ty < nty - 1
    gives_left, gives_up = tx > 0, ty > 0
    base = cuts * long
    pieces = [(gives_up, has_below, {"ty": up}, q, height, N, base + q * short, base + q * short, cuts) for q in range(nq)]
    pieces.append((jnp.logical_and(gives_left, gives_up), jnp.logical_and(has_right, has_below), {"tx": left, "ty": up},
                   nq, height, N, base, base + nq * short, cuts + 1))
    pieces += [(gives_left, has_right, {"tx": left}, nq, k * size, size, k * long, k * long, k) for k in range(cuts)]
    steps = [(gives_up, has_below, {"ty": up}, cuts, cuts, 1),
             (jnp.logical_and(gives_left, gives_up), jnp.logical_and(has_right, has_below), {"tx": left, "ty": up}, cuts, cuts + 1, 1),
             (gives_left, has_right, {"tx": left}, 0, 0, cuts)]
    npieces = len(pieces)

    def strip(n):
        _, _, where, _, _, rows, out, into, _ = pieces[n]
        length = rows * 5 // 4
        return remote(code_out.at[pl.ds(out, length)], code_in.at[pl.ds(into, length)], strip_send.at[n], strip_recv.at[n], where)

    def strip_step(n):
        _, _, where, out, into, number = steps[n]
        return remote(step_out.at[pl.ds(out, number)], step_in.at[pl.ds(into, number)],
                      strip_send.at[npieces + n], strip_recv.at[npieces + n], where)

    def forward(n):
        place = pl.ds(pieces[n][7], pieces[n][5] * 5 // 4)
        return remote(code_in.at[place], code_pair.at[place], pair_send.at[n], pair_recv.at[n], peer)

    def forward_step(n):
        place = pl.ds(steps[n][4], steps[n][5])
        return remote(step_in.at[place], step_pair.at[place], pair_send.at[npieces + n], pair_recv.at[npieces + n], peer)

    def store(off, number):
        rows = number.shape[0]
        code_out[off:off + rows], code_out[off + rows:off + rows * 5 // 4] = split_wide(number)

    for c in mine:
        c.wait()
    number, step_out[cuts] = encode_wide(jnp.concatenate([ext_ref[me, q, :N] for q in range(nq)], axis=0))
    for q in range(nq):
        store(base + q * short, number[q * N:(q + 1) * N])
    for k in range(cuts):
        number, step_out[k] = encode_wide(ext_ref[me, 0, k * size:(k + 1) * size])
        store(k * long, number)
    for c in places:
        c.wait()
    list_ref[me, 0:1, :slots] = spots[0, 0]
    list_ref[me, 1:2, :slots] = spots[1, 0]

    pl.semaphore_wait(barrier, 7)
    for n in range(3):
        @pl.when(steps[n][0])
        def _():
            strip_step(n).start()
    for n in range(npieces):
        @pl.when(pieces[n][0])
        def _():
            strip(n).start()

    extra = npieces + 3
    lists = remote(list_ref.at[me], list_ref.at[me], pair_send.at[extra], pair_recv.at[extra], peer)
    lists.start()
    move = remote(amp_ref.at[pl.ds(moved, slots - moved)], shared_ref.at[pl.ds(0, slots - moved)],
                  pair_send.at[extra + 1], pair_recv.at[extra + 1], peer)

    @pl.when(me == 0)
    def _():
        move.start()

    for n in range(npieces):
        @pl.when(jnp.logical_not(pieces[n][1]))
        def _():
            for p in range(2):
                ext_ref[p, pieces[n][3], pieces[n][4]:pieces[n][4] + pieces[n][5]] = jnp.zeros((pieces[n][5], N), jnp.float32)

    def place(n, p, code, step):
        _, _, _, q, row, rows, _, off, which = pieces[n]
        ext_ref[p, q, row:row + rows] = decode_wide(code[off:off + rows], code[off + rows:off + rows * 5 // 4], step[which])

    for n in range(3):
        @pl.when(steps[n][1])
        def _():
            strip_step(n).wait_recv()
            forward_step(n).start()

    order = list(range(nq + 1, npieces)) + list(range(nq + 1))
    for n in order:
        @pl.when(pieces[n][1])
        def _():
            strip(n).wait_recv()
            forward(n).start()
            place(n, me, code_in, step_in)

    for n in range(3):
        @pl.when(steps[n][1])
        def _():
            forward_step(n).wait_recv()

    for n in order:
        @pl.when(pieces[n][1])
        def _():
            forward(n).wait_recv()
            place(n, other, code_pair, step_pair)

    for c in local:
        c.wait()
    lists.wait()

    @pl.when(me == 0)
    def _():
        move.wait_send()

    @pl.when(me == 1)
    def _():
        move.wait_recv()

    for n in range(npieces):
        @pl.when(pieces[n][0])
        def _():
            strip(n).wait_send()

        @pl.when(pieces[n][1])
        def _():
            forward(n).wait_send()

    for n in range(3):
        @pl.when(steps[n][0])
        def _():
            strip_step(n).wait_send()

        @pl.when(steps[n][1])
        def _():
            forward_step(n).wait_send()


def spread(obj, amp, rows, cols, cuts=4):
    nty, ntx = lax.axis_size("ty"), lax.axis_size("tx")
    height, width = obj.shape[1:]
    slots = amp.shape[0]
    nq = width // N
    copies = nq + 1 + cuts + 3
    total = height * 5 // 4 + (nq + 1) * (N * 5 // 4)
    vmem = pl.BlockSpec(memory_space=pltpu.VMEM)
    hbm = pl.BlockSpec(memory_space=pltpu.HBM)
    dma = pltpu.SemaphoreType.DMA
    code, step = pltpu.VMEM((total, N), jnp.int16), pltpu.VMEM((cuts + 2, 8, N), jnp.float32)
    return pl.pallas_call(
        functools.partial(spread_kernel, nty, ntx, cuts),
        out_shape=(
            jax.ShapeDtypeStruct((2, nq + 1, height + N, N), jnp.float32),
            jax.ShapeDtypeStruct((slots + slots // 2, N, N), jnp.bfloat16),
            jax.ShapeDtypeStruct((2, 8, N), jnp.int32),
        ),
        in_specs=[hbm] * 4,
        out_specs=(vmem, vmem, vmem),
        scratch_shapes=[
            pltpu.VMEM((2, 1, 1, slots), jnp.int32),
            code, step, code, step, code, step,
            dma((2 * nq + 3,)), dma((copies,)), dma((copies,)), dma((copies + 2,)), dma((copies + 2,)),
        ],
        compiler_params=pltpu.CompilerParams(collective_id=0, has_side_effects=True, vmem_limit_bytes=SPREAD_VMEM),
        name="spread",
    )(*(pltpu.with_memory_space_constraint(x, pltpu.HBM) for x in (obj, amp, rows, cols)))


def dft_tables(length):
    freqs = np.arange(length)
    angle = (freqs[:, None] * freqs[None, :] % length) * (2.0 * math.pi / length)
    cosine = np.cos(angle) / math.sqrt(length)
    sine = np.sin(angle) / math.sqrt(length)
    forward = np.block([[cosine, -sine], [sine, cosine]]).astype(ml_dtypes.bfloat16)
    inverse = np.block([[cosine, sine], [-sine, cosine]]).astype(ml_dtypes.bfloat16)
    return forward, inverse

def mm(a, b):
    return jnp.dot(a, b, preferred_element_type=jnp.float32)

def patch_kernel(B, slots, counts_ref, list_ref, ext_ref, probe_ref, amp_ref, fwd_ref, inv_ref,
                 acc_ref, pg_ref, patch_ref):
    acc_ref[...] = jnp.zeros_like(acc_ref)
    pg_ref[...] = jnp.zeros_like(pg_ref)
    lane = lax.broadcasted_iota(jnp.int32, (N, N), 1)
    me = lax.axis_index("pa")
    count = counts_ref[lax.axis_index("ty"), lax.axis_index("tx")]
    moved = slots // 2
    split = jnp.maximum((count + 1) // 2, jnp.minimum(count, moved))
    first = jnp.where(me == 0, 0, split)
    last = jnp.where(me == 0, split, count)

    def body(it, _):
        pos = []
        psis = []
        for b in range(B):
            i = first + it * B + b
            number = jnp.minimum(i, last - 1)
            r = list_ref[number // slots, 0, number % slots]
            c = list_ref[number // slots, 1, number % slots]
            slot = number - me * moved
            j = c // N
            s = c % N
            pos.append((slot, i < last, r, j, s))
            back = (N - s) % N
            high = lane >= s
            parts = []
            for p in range(2):
                v = jnp.where(high, ext_ref[p, j, pl.ds(r, N), :], ext_ref[p, j + 1, pl.ds(r, N), :])
                v = pltpu.roll(v, back, 1)
                patch_ref[b, p] = v
                parts.append(v)
            pre, pim = probe_ref[0], probe_ref[1]
            psi_re = pre * parts[0] - pim * parts[1]
            psi_im = pre * parts[1] + pim * parts[0]
            psis.append(jnp.concatenate([psi_re.astype(jnp.bfloat16), psi_im.astype(jnp.bfloat16)], axis=1))
        half = mm(jnp.concatenate(psis, axis=0), fwd_ref[...]).astype(jnp.bfloat16)
        rhs = jnp.concatenate(
            [jnp.concatenate([half[b * N:(b + 1) * N, q * N:(q + 1) * N] for b in range(B)], axis=1) for q in range(2)], axis=0)
        wave = mm(inv_ref[...], rhs)
        chis = [[], []]
        for b in range(B):
            slot, ok, r, j, s = pos[b]
            wre = wave[:N, b * N:(b + 1) * N]
            wim = wave[N:, b * N:(b + 1) * N]
            level = amp_ref[slot].astype(jnp.float32)
            use = ok.astype(jnp.float32)
            factor = (1.0 - level * lax.rsqrt(wre * wre + wim * wim + 1.0)) * use
            chis[0].append((wre * factor).astype(jnp.bfloat16))
            chis[1].append((wim * factor).astype(jnp.bfloat16))
        rhs2 = jnp.concatenate([jnp.concatenate(chis[q], axis=1) for q in range(2)], axis=0)
        bk = mm(fwd_ref[...], rhs2).astype(jnp.bfloat16)
        lhs = jnp.concatenate([jnp.concatenate([bk[q * N:(q + 1) * N, b * N:(b + 1) * N] for q in range(2)], axis=1) for b in range(B)], axis=0)
        grad = mm(lhs, inv_ref[...])
        tre = pg_ref[0]
        tim = pg_ref[1]
        for b in range(B):
            slot, ok, r, j, s = pos[b]
            gre = grad[b * N:(b + 1) * N, :N]
            gim = grad[b * N:(b + 1) * N, N:]
            pre, pim = probe_ref[0], probe_ref[1]
            qre, qim = patch_ref[b, 0], patch_ref[b, 1]
            tre = tre + (qre * gre + qim * gim)
            tim = tim + (qre * gim - qim * gre)
            obj = (pre * gre + pim * gim, pre * gim - pim * gre)
            high = lane >= s
            for p in range(2):
                o = pltpu.roll(obj[p], s, 1)
                acc_ref[p, j, pl.ds(r, N), :] += jnp.where(high, o, 0.0)
                acc_ref[p, j + 1, pl.ds(r, N), :] += jnp.where(high, 0.0, o)
        pg_ref[0] = tre
        pg_ref[1] = tim
        return 0

    lax.fori_loop(0, (last - first + B - 1) // B, body, 0)

def patches(counts, lists, ext, probe, amp, fwd, inv, B):
    smem = pl.BlockSpec(memory_space=pltpu.SMEM)
    vmem = pl.BlockSpec(memory_space=pltpu.VMEM)
    return pl.pallas_call(
        functools.partial(patch_kernel, B, amp.shape[0] * 2 // 3),
        out_shape=(jax.ShapeDtypeStruct(ext.shape, jnp.float32), jax.ShapeDtypeStruct((2, N, N), jnp.float32)),
        in_specs=[smem] * 2 + [vmem] * 5,
        out_specs=(vmem, vmem),
        scratch_shapes=[pltpu.VMEM((B, 2, N, N), jnp.float32)],
        compiler_params=pltpu.CompilerParams(vmem_limit_bytes=40 << 20),
        name="patches",
    )(counts, lists, ext, probe, amp, fwd, inv)


def flush_kernel(a_ref, b_ref, a_out, b_out, sem):
    copies = [pltpu.make_async_copy(a_ref, a_out, sem.at[0]), pltpu.make_async_copy(b_ref, b_out, sem.at[1])]
    for c in copies:
        c.start()
    for c in copies:
        c.wait()


def flush(a, b):
    hbm = pl.BlockSpec(memory_space=pltpu.HBM)
    return pl.pallas_call(
        flush_kernel,
        out_shape=(jax.ShapeDtypeStruct(a.shape, a.dtype), jax.ShapeDtypeStruct(b.shape, b.dtype)),
        in_specs=[pl.BlockSpec(memory_space=pltpu.VMEM)] * 2,
        out_specs=(hbm, hbm),
        scratch_shapes=[pltpu.SemaphoreType.DMA((2,))],
        name="flush",
    )(*(pltpu.with_memory_space_constraint(x, pltpu.VMEM) for x in (a, b)))


def shards(object_field, probe_field, amplitudes, start_row, start_col, counts):
    height, width = object_field.shape[1:]
    extended, shared, lists = spread(object_field, amplitudes[0, 0], start_row, start_col)
    forward, inverse = dft_tables(N)
    grad, probe_part = patches(
        counts, lists, extended, probe_field, shared, jnp.asarray(forward), jnp.asarray(inverse), BLK)
    return flush(*collect(counts, grad, probe_part, height, width))


def solution(mesh):
    return jax.shard_map(
        shards,
        mesh=mesh,
        in_specs=(
            P(None, "ty", "tx"),
            P(),
            P("ty", "tx", "pa", None, None),
            P("ty", "tx", "pa"),
            P("ty", "tx", "pa"),
            P(),
        ),
        out_specs=(P(None, "ty", "tx"), P()),
        check_vma=False,
    )
```

```python
import functools
import math

import jax
import jax.numpy as jnp
import ml_dtypes
import numpy as np
from jax import lax
from jax.experimental import pallas as pl
from jax.experimental.pallas import tpu as pltpu
from jax.sharding import PartitionSpec as P

BLK = 24

N = 128
LEVELS = 32766.0
MESH = pl.DeviceIdType.MESH


def encode(x):
    rows = x.shape[0]
    tiles = x.reshape(rows // 8, 8, N)
    peak = jnp.max(jnp.abs(tiles), axis=0)
    scaled = tiles * (LEVELS / jnp.maximum(peak, 1e-30))[None]
    return jnp.round(scaled.reshape(rows, N)).astype(jnp.int32).astype(jnp.int16), peak * (1.0 / LEVELS)


def decode(code, step):
    rows = code.shape[0]
    value = code.astype(jnp.int32).astype(jnp.float32)
    return (value.reshape(rows // 8, 8, N) * step[None]).reshape(rows, N)


def remote(src, dst, send_sem, recv_sem, where):
    return pltpu.make_async_remote_copy(
        src_ref=src, dst_ref=dst, send_sem=send_sem, recv_sem=recv_sem, device_id=where, device_id_type=MESH)


def collect_kernel(nty, ntx, zh, zl, counts_ref, acc_ref, pg_ref, out_ref, pgo_ref,
                   theirs, pg_theirs, code_out, step_out, code_in, step_in, by_flat, by_deep, part,
                   pair_send, pair_recv, strip_send, strip_recv, flat_send, flat_recv, deep_send, deep_recv, all_send, all_recv):
    ty, tx, me = lax.axis_index("ty"), lax.axis_index("tx"), lax.axis_index("pa")
    other = 1 - me
    height = out_ref.shape[1]
    nq = out_ref.shape[2] // N
    peer = {"pa": other}
    nflat, ndeep = (nty // zh) * (ntx // zl), zh * zl
    chunk = N // nflat
    deep_id = lax.rem(ty, zh) * zl + lax.rem(tx, zl)
    flat_id = (ty // zh) * (ntx // zl) + tx // zl

    def in_deep(k):
        return {"ty": (ty // zh) * zh + k // zl, "tx": (tx // zl) * zl + lax.rem(k, zl)}

    def in_flat(k):
        return {"ty": (k // (ntx // zl)) * zh + lax.rem(ty, zh), "tx": lax.rem(k, ntx // zl) * zl + lax.rem(tx, zl)}

    def next_flat(k):
        return lax.rem(flat_id + k, nflat)

    def next_deep(k):
        return lax.rem(deep_id + k, ndeep)

    sizes = (height, nq * N, N)
    offs = (0, height, height + nq * N)
    targets = ({"tx": lax.rem(tx + 1, ntx)}, {"ty": lax.rem(ty + 1, nty)},
               {"tx": lax.rem(tx + 1, ntx), "ty": lax.rem(ty + 1, nty)})
    sources = ({"tx": lax.rem(tx + ntx - 1, ntx)}, {"ty": lax.rem(ty + nty - 1, nty)},
               {"tx": lax.rem(tx + ntx - 1, ntx), "ty": lax.rem(ty + nty - 1, nty)})
    sends = (tx < ntx - 1, ty < nty - 1, jnp.logical_and(tx < ntx - 1, ty < nty - 1))
    gets = (tx > 0, ty > 0, jnp.logical_and(tx > 0, ty > 0))

    barrier = pltpu.get_barrier_semaphore()
    for where in (peer,) + targets + sources:
        pl.semaphore_signal(barrier, inc=1, device_id=where, device_id_type=MESH)

    @pl.loop(1, nflat)
    def _(k):
        pl.semaphore_signal(barrier, inc=1, device_id=in_flat(next_flat(k)), device_id_type=MESH)

    @pl.loop(1, ndeep)
    def _(k):
        pl.semaphore_signal(barrier, inc=1, device_id=in_deep(next_deep(k)), device_id_type=MESH)

    total = jnp.sum(jnp.sum(counts_ref[...].astype(jnp.float32), axis=1, keepdims=True), axis=0, keepdims=True)
    pl.semaphore_wait(barrier, 1 + 6 + nflat - 1 + ndeep - 1)

    def swap(n, src, dst):
        return remote(src, dst, pair_send.at[n], pair_recv.at[n], peer)

    probe_swap = swap(1 + nq, pg_ref.at[other], pg_theirs)
    right = swap(0, acc_ref.at[other, nq], theirs.at[nq])
    low = [swap(1 + q, acc_ref.at[other, q, pl.ds(height, N)], theirs.at[q, pl.ds(height, N)]) for q in range(nq)]
    body = [swap(2 + nq + q, acc_ref.at[other, q, pl.ds(0, height)], theirs.at[q, pl.ds(0, height)]) for q in range(nq)]
    probe_swap.start()
    for c in low:
        c.start()
    right.start()
    for c in reversed(body):
        c.start()

    def strip(n):
        size, off = sizes[n], offs[n]
        return (remote(code_out.at[pl.ds(off, size)], code_in.at[pl.ds(off, size)],
                       strip_send.at[2 * n], strip_recv.at[2 * n], targets[n]),
                remote(step_out.at[n], step_in.at[n], strip_send.at[2 * n + 1], strip_recv.at[2 * n + 1], targets[n]))

    def pack(n, value):
        code_out[pl.ds(offs[n], sizes[n])], step_out[n] = encode(value)

        @pl.when(sends[n])
        def _():
            for c in strip(n):
                c.start()

    def rows_of(k):
        return pl.ds(pl.multiple_of(k * chunk, chunk), chunk)

    def flat_copy(k):
        return remote(part.at[rows_of(k)], by_flat.at[flat_id], flat_send.at[k], flat_recv.at[flat_id], in_flat(k))

    def flat_arrival(k):
        return remote(part.at[rows_of(k)], by_flat.at[k], flat_send.at[k], flat_recv.at[k], in_flat(k))

    def deep_copy(k):
        return remote(by_deep.at[deep_id], by_deep.at[deep_id], deep_send.at[k], deep_recv.at[deep_id], in_deep(k))

    def deep_arrival(k):
        return remote(by_deep.at[deep_id], by_deep.at[k], deep_send.at[k], deep_recv.at[k], in_deep(k))

    def all_copy(k, at):
        place = pgo_ref.at[me, rows_of(at)]
        return remote(place, place, all_send.at[k], all_recv.at[at], in_flat(k))

    probe_swap.wait()
    part[...] = pg_ref[me] + pg_theirs[...]

    @pl.loop(1, nflat)
    def _(k):
        flat_copy(next_flat(k)).start()

    by_flat[flat_id] = part[rows_of(flat_id)]

    for c in low:
        c.wait()
    pack(1, jnp.concatenate([acc_ref[me, q, height:] + theirs[q, height:] for q in range(nq)], axis=0))
    right.wait()
    pack(2, acc_ref[me, nq, height:] + theirs[nq, height:])
    pack(0, acc_ref[me, nq, :height] + theirs[nq, :height])

    @pl.loop(1, nflat)
    def _(k):
        flat_arrival(next_flat(k)).wait_recv()

    mine = by_flat[0]
    for k in range(1, nflat):
        mine = mine + by_flat[k]
    by_deep[deep_id] = mine

    @pl.loop(1, ndeep)
    def _(k):
        deep_copy(next_deep(k)).start()

    for q in reversed(range(nq)):
        body[q].wait()
        out_ref[me, :, q * N:(q + 1) * N] = acc_ref[me, q, :height] + theirs[q, :height]

    def final(n, rows, columns):
        place = out_ref.at[me, rows, columns]
        return swap(n, place, place)

    rest = pl.ds(N, (nq - 1) * N)
    early = final(2 + 2 * nq, pl.ds(N, height - N), rest)
    early.start()

    @pl.loop(1, ndeep)
    def _(k):
        deep_arrival(next_deep(k)).wait_recv()

    mine = by_deep[0]
    for k in range(1, ndeep):
        mine = mine + by_deep[k]
    pgo_ref[me, rows_of(flat_id)] = mine / total

    @pl.loop(1, nflat)
    def _(k):
        all_copy(next_flat(k), flat_id).start()

    @pl.when(gets[1])
    def _():
        for c in strip(1):
            c.wait_recv()
        for q in range(nq):
            out_ref[me, :N, q * N:(q + 1) * N] += decode(code_in[pl.ds(offs[1] + q * N, N)], step_in[1])

    @pl.when(gets[2])
    def _():
        for c in strip(2):
            c.wait_recv()
        out_ref[me, :N, :N] += decode(code_in[pl.ds(offs[2], N)], step_in[2])

    @pl.when(gets[0])
    def _():
        for c in strip(0):
            c.wait_recv()
        out_ref[me, :, :N] += decode(code_in[pl.ds(0, height)], step_in[0])

    late = [final(3 + 2 * nq, pl.ds(0, height), pl.ds(0, N)), final(4 + 2 * nq, pl.ds(0, N), rest)]
    for c in late:
        c.start()

    @pl.loop(1, nflat)
    def _(k):
        at = next_flat(k)
        all_copy(at, at).wait_recv()

    last = swap(5 + 2 * nq, pgo_ref.at[me], pgo_ref.at[me])
    last.start()

    for n in range(3):
        @pl.when(sends[n])
        def _():
            for c in strip(n):
                c.wait_send()

    @pl.loop(1, nflat)
    def _(k):
        at = next_flat(k)
        flat_copy(at).wait_send()
        all_copy(at, flat_id).wait_send()

    @pl.loop(1, ndeep)
    def _(k):
        deep_copy(next_deep(k)).wait_send()

    early.wait()
    for c in late:
        c.wait()
    last.wait()


def collect(counts, acc, pg, height, width, zh=2, zl=4):
    nty, ntx = lax.axis_size("ty"), lax.axis_size("tx")
    nq = width // N
    rows = height + nq * N + N
    nflat, ndeep = (nty // zh) * (ntx // zl), zh * zl
    chunk = N // nflat
    vmem = pl.BlockSpec(memory_space=pltpu.VMEM)
    dma = pltpu.SemaphoreType.DMA
    return pl.pallas_call(
        functools.partial(collect_kernel, nty, ntx, zh, zl),
        out_shape=(jax.ShapeDtypeStruct((2, height, width), jnp.float32), jax.ShapeDtypeStruct((2, N, N), jnp.float32)),
        in_specs=[vmem] * 3,
        out_specs=(vmem, vmem),
        scratch_shapes=[
            pltpu.VMEM((nq + 1, height + N, N), jnp.float32),
            pltpu.VMEM((N, N), jnp.float32),
            pltpu.VMEM((rows, N), jnp.int16),
            pltpu.VMEM((3, 8, N), jnp.float32),
            pltpu.VMEM((rows, N), jnp.int16),
            pltpu.VMEM((3, 8, N), jnp.float32),
            pltpu.VMEM((nflat, chunk, N), jnp.float32),
            pltpu.VMEM((ndeep, chunk, N), jnp.float32),
            pltpu.VMEM((N, N), jnp.float32),
            dma((6 + 2 * nq,)), dma((6 + 2 * nq,)), dma((6,)), dma((6,)),
            dma((nflat,)), dma((nflat,)), dma((ndeep,)), dma((ndeep,)), dma((nflat,)), dma((nflat,)),
        ],
        compiler_params=pltpu.CompilerParams(collective_id=1, has_side_effects=True, vmem_limit_bytes=40 << 20),
        name="collect",
    )(counts, acc, pg)


WIDE = 524287.0
SPREAD_VMEM = 40 << 20


def encode_wide(x):
    rows = x.shape[0]
    tiles = x.reshape(rows // 8, 8, N)
    peak = jnp.max(jnp.abs(tiles), axis=0)
    scaled = tiles * (WIDE / jnp.maximum(peak, 1e-30))[None]
    number = jnp.round(scaled.reshape(rows, N)).astype(jnp.int32)
    return number, peak * (1.0 / WIDE)


def split_wide(number):
    quarter = number.shape[0] // 4
    low = number & 15
    word = -32768
    for g in range(4):
        word = word + (low[g * quarter:(g + 1) * quarter] << (4 * g))
    return (number >> 4).astype(jnp.int16), word.astype(jnp.int16)


def decode_wide(high, word, step):
    rows = high.shape[0]
    low = word.astype(jnp.int32) + 32768
    low = jnp.concatenate([(low >> (4 * g)) & 15 for g in range(4)], axis=0)
    value = ((high.astype(jnp.int32) << 4) + low).astype(jnp.float32)
    return (value.reshape(rows // 8, 8, N) * step[None]).reshape(rows, N)


def spread_kernel(nty, ntx, cuts, obj_ref, amp_ref, rows_ref, cols_ref, ext_ref, shared_ref, list_ref,
                  spots, code_out, step_out, code_in, step_in, code_pair, step_pair,
                  local_sem, strip_send, strip_recv, pair_send, pair_recv):
    ty, tx, me = lax.axis_index("ty"), lax.axis_index("tx"), lax.axis_index("pa")
    other = 1 - me
    height = obj_ref.shape[1]
    nq = obj_ref.shape[2] // N
    slots = amp_ref.shape[0]
    moved = slots // 2
    peer = {"pa": other}
    up, down = lax.rem(ty + nty - 1, nty), lax.rem(ty + 1, nty)
    left, right = lax.rem(tx + ntx - 1, ntx), lax.rem(tx + 1, ntx)

    barrier = pltpu.get_barrier_semaphore()
    for where in (peer, {"tx": left}, {"tx": right}, {"ty": up}, {"ty": down}, {"tx": left, "ty": up}, {"tx": right, "ty": down}):
        pl.semaphore_signal(barrier, inc=1, device_id=where, device_id_type=MESH)

    def load(p, q):
        return pltpu.make_async_copy(obj_ref.at[p, :, pl.ds(q * N, N)], ext_ref.at[p, q, pl.ds(0, height)], local_sem.at[p * nq + q])

    mine = [load(me, q) for q in range(nq)]
    local = [load(other, q) for q in range(nq)]
    local.append(pltpu.make_async_copy(amp_ref, shared_ref.at[pl.ds(me * moved, slots)], local_sem.at[2 * nq]))
    places = [pltpu.make_async_copy(rows_ref, spots.at[0], local_sem.at[2 * nq + 1]),
              pltpu.make_async_copy(cols_ref, spots.at[1], local_sem.at[2 * nq + 2])]
    for c in mine + places + local:
        c.start()

    size = height // cuts
    long, short = size * 5 // 4, N * 5 // 4
    has_right, has_below = tx < ntx - 1, ty < nty - 1
    gives_left, gives_up = tx > 0, ty > 0
    base = cuts * long
    pieces = [(gives_up, has_below, {"ty": up}, q, height, N, base + q * short, base + q * short, cuts) for q in range(nq)]
    pieces.append((jnp.logical_and(gives_left, gives_up), jnp.logical_and(has_right, has_below), {"tx": left, "ty": up},
                   nq, height, N, base, base + nq * short, cuts + 1))
    pieces += [(gives_left, has_right, {"tx": left}, nq, k * size, size, k * long, k * long, k) for k in range(cuts)]
    steps = [(gives_up, has_below, {"ty": up}, cuts, cuts, 1),
             (jnp.logical_and(gives_left, gives_up), jnp.logical_and(has_right, has_below), {"tx": left, "ty": up}, cuts, cuts + 1, 1),
             (gives_left, has_right, {"tx": left}, 0, 0, cuts)]
    npieces = len(pieces)

    def strip(n):
        _, _, where, _, _, rows, out, into, _ = pieces[n]
        length = rows * 5 // 4
        return remote(code_out.at[pl.ds(out, length)], code_in.at[pl.ds(into, length)], strip_send.at[n], strip_recv.at[n], where)

    def strip_step(n):
        _, _, where, out, into, number = steps[n]
        return remote(step_out.at[pl.ds(out, number)], step_in.at[pl.ds(into, number)],
                      strip_send.at[npieces + n], strip_recv.at[npieces + n], where)

    def forward(n):
        place = pl.ds(pieces[n][7], pieces[n][5] * 5 // 4)
        return remote(code_in.at[place], code_pair.at[place], pair_send.at[n], pair_recv.at[n], peer)

    def forward_step(n):
        place = pl.ds(steps[n][4], steps[n][5])
        return remote(step_in.at[place], step_pair.at[place], pair_send.at[npieces + n], pair_recv.at[npieces + n], peer)

    def store(off, number):
        rows = number.shape[0]
        code_out[off:off + rows], code_out[off + rows:off + rows * 5 // 4] = split_wide(number)

    for c in mine:
        c.wait()
    number, step_out[cuts] = encode_wide(jnp.concatenate([ext_ref[me, q, :N] for q in range(nq)], axis=0))
    for q in range(nq):
        store(base + q * short, number[q * N:(q + 1) * N])
    for k in range(cuts):
        number, step_out[k] = encode_wide(ext_ref[me, 0, k * size:(k + 1) * size])
        store(k * long, number)
    for c in places:
        c.wait()
    list_ref[me, 0:1, :slots] = spots[0, 0]
    list_ref[me, 1:2, :slots] = spots[1, 0]

    pl.semaphore_wait(barrier, 7)
    for n in range(3):
        @pl.when(steps[n][0])
        def _():
            strip_step(n).start()
    for n in range(npieces):
        @pl.when(pieces[n][0])
        def _():
            strip(n).start()

    extra = npieces + 3
    lists = remote(list_ref.at[me], list_ref.at[me], pair_send.at[extra], pair_recv.at[extra], peer)
    lists.start()
    move = remote(amp_ref.at[pl.ds(moved, slots - moved)], shared_ref.at[pl.ds(0, slots - moved)],
                  pair_send.at[extra + 1], pair_recv.at[extra + 1], peer)

    @pl.when(me == 0)
    def _():
        move.start()

    for n in range(npieces):
        @pl.when(jnp.logical_not(pieces[n][1]))
        def _():
            for p in range(2):
                ext_ref[p, pieces[n][3], pieces[n][4]:pieces[n][4] + pieces[n][5]] = jnp.zeros((pieces[n][5], N), jnp.float32)

    def place(n, p, code, step):
        _, _, _, q, row, rows, _, off, which = pieces[n]
        ext_ref[p, q, row:row + rows] = decode_wide(code[off:off + rows], code[off + rows:off + rows * 5 // 4], step[which])

    for n in range(3):
        @pl.when(steps[n][1])
        def _():
            strip_step(n).wait_recv()
            forward_step(n).start()

    order = list(range(nq + 1, npieces)) + list(range(nq + 1))
    for n in order:
        @pl.when(pieces[n][1])
        def _():
            strip(n).wait_recv()
            forward(n).start()
            place(n, me, code_in, step_in)

    for n in range(3):
        @pl.when(steps[n][1])
        def _():
            forward_step(n).wait_recv()

    for n in order:
        @pl.when(pieces[n][1])
        def _():
            forward(n).wait_recv()
            place(n, other, code_pair, step_pair)

    for c in local:
        c.wait()
    lists.wait()

    @pl.when(me == 0)
    def _():
        move.wait_send()

    @pl.when(me == 1)
    def _():
        move.wait_recv()

    for n in range(npieces):
        @pl.when(pieces[n][0])
        def _():
            strip(n).wait_send()

        @pl.when(pieces[n][1])
        def _():
            forward(n).wait_send()

    for n in range(3):
        @pl.when(steps[n][0])
        def _():
            strip_step(n).wait_send()

        @pl.when(steps[n][1])
        def _():
            forward_step(n).wait_send()


def spread(obj, amp, rows, cols, cuts=4):
    nty, ntx = lax.axis_size("ty"), lax.axis_size("tx")
    height, width = obj.shape[1:]
    slots = amp.shape[0]
    nq = width // N
    copies = nq + 1 + cuts + 3
    total = height * 5 // 4 + (nq + 1) * (N * 5 // 4)
    vmem = pl.BlockSpec(memory_space=pltpu.VMEM)
    hbm = pl.BlockSpec(memory_space=pltpu.HBM)
    dma = pltpu.SemaphoreType.DMA
    code, step = pltpu.VMEM((total, N), jnp.int16), pltpu.VMEM((cuts + 2, 8, N), jnp.float32)
    return pl.pallas_call(
        functools.partial(spread_kernel, nty, ntx, cuts),
        out_shape=(
            jax.ShapeDtypeStruct((2, nq + 1, height + N, N), jnp.float32),
            jax.ShapeDtypeStruct((slots + slots // 2, N, N), jnp.bfloat16),
            jax.ShapeDtypeStruct((2, 8, N), jnp.int32),
        ),
        in_specs=[hbm] * 4,
        out_specs=(vmem, vmem, vmem),
        scratch_shapes=[
            pltpu.VMEM((2, 1, 1, slots), jnp.int32),
            code, step, code, step, code, step,
            dma((2 * nq + 3,)), dma((copies,)), dma((copies,)), dma((copies + 2,)), dma((copies + 2,)),
        ],
        compiler_params=pltpu.CompilerParams(collective_id=0, has_side_effects=True, vmem_limit_bytes=SPREAD_VMEM),
        name="spread",
    )(*(pltpu.with_memory_space_constraint(x, pltpu.HBM) for x in (obj, amp, rows, cols)))


def dft_tables(length):
    freqs = np.arange(length)
    angle = (freqs[:, None] * freqs[None, :] % length) * (2.0 * math.pi / length)
    cosine = np.cos(angle) / math.sqrt(length)
    sine = np.sin(angle) / math.sqrt(length)
    forward = np.block([[cosine, -sine], [sine, cosine]]).astype(ml_dtypes.bfloat16)
    inverse = np.block([[cosine, sine], [-sine, cosine]]).astype(ml_dtypes.bfloat16)
    return forward, inverse

def mm(a, b):
    return jnp.dot(a, b, preferred_element_type=jnp.float32)

def patch_kernel(B, slots, counts_ref, list_ref, ext_ref, probe_ref, amp_ref, fwd_ref, inv_ref,
                 acc_ref, pg_ref, patch_ref):
    acc_ref[...] = jnp.zeros_like(acc_ref)
    pg_ref[...] = jnp.zeros_like(pg_ref)
    lane = lax.broadcasted_iota(jnp.int32, (N, N), 1)
    me = lax.axis_index("pa")
    count = counts_ref[lax.axis_index("ty"), lax.axis_index("tx")]
    moved = slots // 2
    split = jnp.maximum((count + 1) // 2, jnp.minimum(count, moved))
    first = jnp.where(me == 0, 0, split)
    last = jnp.where(me == 0, split, count)

    def body(it, _):
        pos = []
        psis = []
        for b in range(B):
            i = first + it * B + b
            number = jnp.minimum(i, last - 1)
            r = list_ref[number // slots, 0, number % slots]
            c = list_ref[number // slots, 1, number % slots]
            slot = number - me * moved
            j = c // N
            s = c % N
            pos.append((slot, i < last, r, j, s))
            back = (N - s) % N
            high = lane >= s
            parts = []
            for p in range(2):
                v = jnp.where(high, ext_ref[p, j, pl.ds(r, N), :], ext_ref[p, j + 1, pl.ds(r, N), :])
                v = pltpu.roll(v, back, 1)
                patch_ref[b, p] = v
                parts.append(v)
            pre, pim = probe_ref[0], probe_ref[1]
            psi_re = pre * parts[0] - pim * parts[1]
            psi_im = pre * parts[1] + pim * parts[0]
            psis.append(jnp.concatenate([psi_re.astype(jnp.bfloat16), psi_im.astype(jnp.bfloat16)], axis=1))
        half = mm(jnp.concatenate(psis, axis=0), fwd_ref[...]).astype(jnp.bfloat16)
        rhs = jnp.concatenate(
            [jnp.concatenate([half[b * N:(b + 1) * N, q * N:(q + 1) * N] for b in range(B)], axis=1) for q in range(2)], axis=0)
        wave = mm(inv_ref[...], rhs)
        chis = [[], []]
        for b in range(B):
            slot, ok, r, j, s = pos[b]
            wre = wave[:N, b * N:(b + 1) * N]
            wim = wave[N:, b * N:(b + 1) * N]
            level = amp_ref[slot].astype(jnp.float32)
            use = ok.astype(jnp.float32)
            factor = (1.0 - level * lax.rsqrt(wre * wre + wim * wim + 1.0)) * use
            chis[0].append((wre * factor).astype(jnp.bfloat16))
            chis[1].append((wim * factor).astype(jnp.bfloat16))
        rhs2 = jnp.concatenate([jnp.concatenate(chis[q], axis=1) for q in range(2)], axis=0)
        bk = mm(fwd_ref[...], rhs2).astype(jnp.bfloat16)
        lhs = jnp.concatenate([jnp.concatenate([bk[q * N:(q + 1) * N, b * N:(b + 1) * N] for q in range(2)], axis=1) for b in range(B)], axis=0)
        grad = mm(lhs, inv_ref[...])
        tre = pg_ref[0]
        tim = pg_ref[1]
        for b in range(B):
            slot, ok, r, j, s = pos[b]
            gre = grad[b * N:(b + 1) * N, :N]
            gim = grad[b * N:(b + 1) * N, N:]
            pre, pim = probe_ref[0], probe_ref[1]
            qre, qim = patch_ref[b, 0], patch_ref[b, 1]
            tre = tre + (qre * gre + qim * gim)
            tim = tim + (qre * gim - qim * gre)
            obj = (pre * gre + pim * gim, pre * gim - pim * gre)
            high = lane >= s
            low = lane < s
            for p in range(2):
                o = pltpu.roll(obj[p], s, 1)
                u = acc_ref[p, j, pl.ds(r, N), :]
                v = acc_ref[p, j + 1, pl.ds(r, N), :]
                pltpu.store(acc_ref.at[p, j, pl.ds(r, N), :], u + o, mask=high)
                pltpu.store(acc_ref.at[p, j + 1, pl.ds(r, N), :], v + o, mask=low)
        pg_ref[0] = tre
        pg_ref[1] = tim
        return 0

    lax.fori_loop(0, (last - first + B - 1) // B, body, 0)

def patches(counts, lists, ext, probe, amp, fwd, inv, B):
    smem = pl.BlockSpec(memory_space=pltpu.SMEM)
    vmem = pl.BlockSpec(memory_space=pltpu.VMEM)
    return pl.pallas_call(
        functools.partial(patch_kernel, B, amp.shape[0] * 2 // 3),
        out_shape=(jax.ShapeDtypeStruct(ext.shape, jnp.float32), jax.ShapeDtypeStruct((2, N, N), jnp.float32)),
        in_specs=[smem] * 2 + [vmem] * 5,
        out_specs=(vmem, vmem),
        scratch_shapes=[pltpu.VMEM((B, 2, N, N), jnp.float32)],
        compiler_params=pltpu.CompilerParams(vmem_limit_bytes=40 << 20),
        name="patches",
    )(counts, lists, ext, probe, amp, fwd, inv)


def flush_kernel(a_ref, b_ref, a_out, b_out, sem):
    copies = [pltpu.make_async_copy(a_ref, a_out, sem.at[0]), pltpu.make_async_copy(b_ref, b_out, sem.at[1])]
    for c in copies:
        c.start()
    for c in copies:
        c.wait()


def flush(a, b):
    hbm = pl.BlockSpec(memory_space=pltpu.HBM)
    return pl.pallas_call(
        flush_kernel,
        out_shape=(jax.ShapeDtypeStruct(a.shape, a.dtype), jax.ShapeDtypeStruct(b.shape, b.dtype)),
        in_specs=[pl.BlockSpec(memory_space=pltpu.VMEM)] * 2,
        out_specs=(hbm, hbm),
        scratch_shapes=[pltpu.SemaphoreType.DMA((2,))],
        name="flush",
    )(*(pltpu.with_memory_space_constraint(x, pltpu.VMEM) for x in (a, b)))


def shards(object_field, probe_field, amplitudes, start_row, start_col, counts):
    height, width = object_field.shape[1:]
    extended, shared, lists = spread(object_field, amplitudes[0, 0], start_row, start_col)
    forward, inverse = dft_tables(N)
    grad, probe_part = patches(
        counts, lists, extended, probe_field, shared, jnp.asarray(forward), jnp.asarray(inverse), BLK)
    return flush(*collect(counts, grad, probe_part, height, width))


def solution(mesh):
    return jax.shard_map(
        shards,
        mesh=mesh,
        in_specs=(
            P(None, "ty", "tx"),
            P(),
            P("ty", "tx", "pa", None, None),
            P("ty", "tx", "pa"),
            P("ty", "tx", "pa"),
            P(),
        ),
        out_specs=(P(None, "ty", "tx"), P()),
        check_vma=False,
    )
```

```python
import functools
import math

import jax
import jax.numpy as jnp
import ml_dtypes
import numpy as np
from jax import lax
from jax.experimental import pallas as pl
from jax.experimental.pallas import tpu as pltpu
from jax.sharding import PartitionSpec as P

BLK = 24

N = 128
LEVELS = 32766.0
MESH = pl.DeviceIdType.MESH


def encode(x):
    rows = x.shape[0]
    tiles = x.reshape(rows // 8, 8, N)
    peak = jnp.max(jnp.abs(tiles), axis=0)
    scaled = tiles * (LEVELS / jnp.maximum(peak, 1e-30))[None]
    return jnp.round(scaled.reshape(rows, N)).astype(jnp.int32).astype(jnp.int16), peak * (1.0 / LEVELS)


def decode(code, step):
    rows = code.shape[0]
    value = code.astype(jnp.int32).astype(jnp.float32)
    return (value.reshape(rows // 8, 8, N) * step[None]).reshape(rows, N)


def remote(src, dst, send_sem, recv_sem, where):
    return pltpu.make_async_remote_copy(
        src_ref=src, dst_ref=dst, send_sem=send_sem, recv_sem=recv_sem, device_id=where, device_id_type=MESH)


def collect_kernel(nty, ntx, zh, zl, counts_ref, acc_ref, pg_ref, out_ref, pgo_ref,
                   theirs, pg_theirs, code_out, step_out, code_in, step_in, by_line, by_plane, part,
                   pair_send, pair_recv, strip_send, strip_recv, line_send, line_recv, plane_send, plane_recv, all_send, all_recv):
    ty, tx, me = lax.axis_index("ty"), lax.axis_index("tx"), lax.axis_index("pa")
    other = 1 - me
    height = out_ref.shape[1]
    nq = out_ref.shape[2] // N
    peer = {"pa": other}
    nline, nplane = zh * zl, (nty // zh) * (ntx // zl)
    chunk = N // nline
    line_id = lax.rem(ty, zh) * zl + lax.rem(tx, zl)
    plane_id = (ty // zh) * (ntx // zl) + tx // zl

    def in_line(k):
        return {"ty": (ty // zh) * zh + k // zl, "tx": (tx // zl) * zl + lax.rem(k, zl)}

    def in_plane(k):
        return {"ty": (k // (ntx // zl)) * zh + lax.rem(ty, zh), "tx": lax.rem(k, ntx // zl) * zl + lax.rem(tx, zl)}

    def next_in_line(k):
        return lax.rem(line_id + k, nline)

    def next_in_plane(k):
        return lax.rem(plane_id + k, nplane)

    sizes = (height, nq * N, N)
    offs = (0, height, height + nq * N)
    targets = ({"tx": lax.rem(tx + 1, ntx)}, {"ty": lax.rem(ty + 1, nty)},
               {"tx": lax.rem(tx + 1, ntx), "ty": lax.rem(ty + 1, nty)})
    sources = ({"tx": lax.rem(tx + ntx - 1, ntx)}, {"ty": lax.rem(ty + nty - 1, nty)},
               {"tx": lax.rem(tx + ntx - 1, ntx), "ty": lax.rem(ty + nty - 1, nty)})
    sends = (tx < ntx - 1, ty < nty - 1, jnp.logical_and(tx < ntx - 1, ty < nty - 1))
    gets = (tx > 0, ty > 0, jnp.logical_and(tx > 0, ty > 0))

    barrier = pltpu.get_barrier_semaphore()
    for where in (peer,) + targets + sources:
        pl.semaphore_signal(barrier, inc=1, device_id=where, device_id_type=MESH)

    @pl.loop(1, nline)
    def _(k):
        pl.semaphore_signal(barrier, inc=1, device_id=in_line(next_in_line(k)), device_id_type=MESH)

    @pl.loop(1, nplane)
    def _(k):
        pl.semaphore_signal(barrier, inc=1, device_id=in_plane(next_in_plane(k)), device_id_type=MESH)

    total = jnp.sum(jnp.sum(counts_ref[...].astype(jnp.float32), axis=1, keepdims=True), axis=0, keepdims=True)
    pl.semaphore_wait(barrier, 1 + 6 + nline - 1 + nplane - 1)

    def swap(n, src, dst):
        return remote(src, dst, pair_send.at[n], pair_recv.at[n], peer)

    probe_swap = swap(1 + nq, pg_ref.at[other], pg_theirs)
    right = swap(0, acc_ref.at[other, nq], theirs.at[nq])
    low = [swap(1 + q, acc_ref.at[other, q, pl.ds(height, N)], theirs.at[q, pl.ds(height, N)]) for q in range(nq)]
    body = [swap(2 + nq + q, acc_ref.at[other, q, pl.ds(0, height)], theirs.at[q, pl.ds(0, height)]) for q in range(nq)]
    probe_swap.start()
    for c in low:
        c.start()
    right.start()
    for c in reversed(body):
        c.start()

    def strip(n):
        size, off = sizes[n], offs[n]
        return (remote(code_out.at[pl.ds(off, size)], code_in.at[pl.ds(off, size)],
                       strip_send.at[2 * n], strip_recv.at[2 * n], targets[n]),
                remote(step_out.at[n], step_in.at[n], strip_send.at[2 * n + 1], strip_recv.at[2 * n + 1], targets[n]))

    def pack(n, value):
        code_out[pl.ds(offs[n], sizes[n])], step_out[n] = encode(value)

    def leave(n):
        @pl.when(sends[n])
        def _():
            for c in strip(n):
                c.start()

    def rows_of(k):
        return pl.ds(pl.multiple_of(k * chunk, chunk), chunk)

    def line_copy(k):
        return remote(part.at[rows_of(k)], by_line.at[line_id], line_send.at[k], line_recv.at[line_id], in_line(k))

    def line_arrival(k):
        return remote(part.at[rows_of(k)], by_line.at[k], line_send.at[k], line_recv.at[k], in_line(k))

    def plane_copy(k):
        return remote(by_plane.at[plane_id], by_plane.at[plane_id], plane_send.at[k], plane_recv.at[plane_id], in_plane(k))

    def plane_arrival(k):
        return remote(by_plane.at[plane_id], by_plane.at[k], plane_send.at[k], plane_recv.at[k], in_plane(k))

    def all_copy(k, at):
        place = pgo_ref.at[me, rows_of(at)]
        return remote(place, place, all_send.at[k], all_recv.at[at], in_line(k))

    probe_swap.wait()
    part[...] = pg_ref[me] + pg_theirs[...]

    @pl.loop(1, nline)
    def _(k):
        line_copy(next_in_line(k)).start()

    by_line[line_id] = part[rows_of(line_id)]

    for c in low:
        c.wait()
    pack(1, jnp.concatenate([acc_ref[me, q, height:] + theirs[q, height:] for q in range(nq)], axis=0))
    right.wait()
    pack(2, acc_ref[me, nq, height:] + theirs[nq, height:])
    leave(1)
    leave(2)
    pack(0, acc_ref[me, nq, :height] + theirs[nq, :height])

    @pl.loop(1, nline)
    def _(k):
        line_arrival(next_in_line(k)).wait_recv()

    mine = by_line[0]
    for k in range(1, nline):
        mine = mine + by_line[k]
    by_plane[plane_id] = mine

    @pl.loop(1, nplane)
    def _(k):
        plane_copy(next_in_plane(k)).start()

    leave(0)

    for q in reversed(range(nq)):
        body[q].wait()
        out_ref[me, :, q * N:(q + 1) * N] = acc_ref[me, q, :height] + theirs[q, :height]

    def final(n, rows, columns):
        place = out_ref.at[me, rows, columns]
        return swap(n, place, place)

    rest = pl.ds(N, (nq - 1) * N)
    early = final(2 + 2 * nq, pl.ds(N, height - N), rest)
    early.start()

    @pl.loop(1, nplane)
    def _(k):
        plane_arrival(next_in_plane(k)).wait_recv()

    mine = by_plane[0]
    for k in range(1, nplane):
        mine = mine + by_plane[k]
    pgo_ref[me, rows_of(line_id)] = mine / total

    @pl.loop(1, nline)
    def _(k):
        all_copy(next_in_line(k), line_id).start()

    @pl.when(gets[1])
    def _():
        for c in strip(1):
            c.wait_recv()
        for q in range(nq):
            out_ref[me, :N, q * N:(q + 1) * N] += decode(code_in[pl.ds(offs[1] + q * N, N)], step_in[1])

    @pl.when(gets[2])
    def _():
        for c in strip(2):
            c.wait_recv()
        out_ref[me, :N, :N] += decode(code_in[pl.ds(offs[2], N)], step_in[2])

    @pl.when(gets[0])
    def _():
        for c in strip(0):
            c.wait_recv()
        out_ref[me, :, :N] += decode(code_in[pl.ds(0, height)], step_in[0])

    late = [final(3 + 2 * nq, pl.ds(0, height), pl.ds(0, N)), final(4 + 2 * nq, pl.ds(0, N), rest)]
    for c in late:
        c.start()

    @pl.loop(1, nline)
    def _(k):
        at = next_in_line(k)
        all_copy(at, at).wait_recv()

    last = swap(5 + 2 * nq, pgo_ref.at[me], pgo_ref.at[me])
    last.start()

    for n in range(3):
        @pl.when(sends[n])
        def _():
            for c in strip(n):
                c.wait_send()

    @pl.loop(1, nline)
    def _(k):
        at = next_in_line(k)
        line_copy(at).wait_send()
        all_copy(at, line_id).wait_send()

    @pl.loop(1, nplane)
    def _(k):
        plane_copy(next_in_plane(k)).wait_send()

    early.wait()
    for c in late:
        c.wait()
    last.wait()


def collect(counts, acc, pg, height, width, zh=2, zl=4):
    nty, ntx = lax.axis_size("ty"), lax.axis_size("tx")
    nq = width // N
    rows = height + nq * N + N
    nline, nplane = zh * zl, (nty // zh) * (ntx // zl)
    chunk = N // nline
    vmem = pl.BlockSpec(memory_space=pltpu.VMEM)
    dma = pltpu.SemaphoreType.DMA
    return pl.pallas_call(
        functools.partial(collect_kernel, nty, ntx, zh, zl),
        out_shape=(jax.ShapeDtypeStruct((2, height, width), jnp.float32), jax.ShapeDtypeStruct((2, N, N), jnp.float32)),
        in_specs=[vmem] * 3,
        out_specs=(vmem, vmem),
        scratch_shapes=[
            pltpu.VMEM((nq + 1, height + N, N), jnp.float32),
            pltpu.VMEM((N, N), jnp.float32),
            pltpu.VMEM((rows, N), jnp.int16),
            pltpu.VMEM((3, 8, N), jnp.float32),
            pltpu.VMEM((rows, N), jnp.int16),
            pltpu.VMEM((3, 8, N), jnp.float32),
            pltpu.VMEM((nline, chunk, N), jnp.float32),
            pltpu.VMEM((nplane, chunk, N), jnp.float32),
            pltpu.VMEM((N, N), jnp.float32),
            dma((6 + 2 * nq,)), dma((6 + 2 * nq,)), dma((6,)), dma((6,)),
            dma((nline,)), dma((nline,)), dma((nplane,)), dma((nplane,)), dma((nline,)), dma((nline,)),
        ],
        compiler_params=pltpu.CompilerParams(collective_id=1, has_side_effects=True, vmem_limit_bytes=40 << 20),
        name="collect",
    )(counts, acc, pg)


WIDE = 524287.0
SPREAD_VMEM = 40 << 20


def encode_wide(x):
    rows = x.shape[0]
    tiles = x.reshape(rows // 8, 8, N)
    peak = jnp.max(jnp.abs(tiles), axis=0)
    scaled = tiles * (WIDE / jnp.maximum(peak, 1e-30))[None]
    number = jnp.round(scaled.reshape(rows, N)).astype(jnp.int32)
    return number, peak * (1.0 / WIDE)


def split_wide(number):
    quarter = number.shape[0] // 4
    low = number & 15
    word = -32768
    for g in range(4):
        word = word + (low[g * quarter:(g + 1) * quarter] << (4 * g))
    return (number >> 4).astype(jnp.int16), word.astype(jnp.int16)


def decode_wide(high, word, step):
    rows = high.shape[0]
    low = word.astype(jnp.int32) + 32768
    low = jnp.concatenate([(low >> (4 * g)) & 15 for g in range(4)], axis=0)
    value = ((high.astype(jnp.int32) << 4) + low).astype(jnp.float32)
    return (value.reshape(rows // 8, 8, N) * step[None]).reshape(rows, N)


def spread_kernel(nty, ntx, cuts, obj_ref, amp_ref, rows_ref, cols_ref, ext_ref, shared_ref, list_ref,
                  spots, code_out, step_out, code_in, step_in, code_pair, step_pair,
                  local_sem, strip_send, strip_recv, pair_send, pair_recv):
    ty, tx, me = lax.axis_index("ty"), lax.axis_index("tx"), lax.axis_index("pa")
    other = 1 - me
    height = obj_ref.shape[1]
    nq = obj_ref.shape[2] // N
    slots = amp_ref.shape[0]
    moved = slots // 2
    peer = {"pa": other}
    up, down = lax.rem(ty + nty - 1, nty), lax.rem(ty + 1, nty)
    left, right = lax.rem(tx + ntx - 1, ntx), lax.rem(tx + 1, ntx)

    barrier = pltpu.get_barrier_semaphore()
    for where in (peer, {"tx": left}, {"tx": right}, {"ty": up}, {"ty": down}, {"tx": left, "ty": up}, {"tx": right, "ty": down}):
        pl.semaphore_signal(barrier, inc=1, device_id=where, device_id_type=MESH)

    def load(p, q):
        return pltpu.make_async_copy(obj_ref.at[p, :, pl.ds(q * N, N)], ext_ref.at[p, q, pl.ds(0, height)], local_sem.at[p * nq + q])

    mine = [load(me, q) for q in range(nq)]
    local = [load(other, q) for q in range(nq)]
    local.append(pltpu.make_async_copy(amp_ref, shared_ref.at[pl.ds(me * moved, slots)], local_sem.at[2 * nq]))
    places = [pltpu.make_async_copy(rows_ref, spots.at[0], local_sem.at[2 * nq + 1]),
              pltpu.make_async_copy(cols_ref, spots.at[1], local_sem.at[2 * nq + 2])]
    for c in mine + places + local:
        c.start()

    size = height // cuts
    long, short = size * 5 // 4, N * 5 // 4
    has_right, has_below = tx < ntx - 1, ty < nty - 1
    gives_left, gives_up = tx > 0, ty > 0
    base = cuts * long
    pieces = [(gives_up, has_below, {"ty": up}, q, height, N, base + q * short, base + q * short, cuts) for q in range(nq)]
    pieces.append((jnp.logical_and(gives_left, gives_up), jnp.logical_and(has_right, has_below), {"tx": left, "ty": up},
                   nq, height, N, base, base + nq * short, cuts + 1))
    pieces += [(gives_left, has_right, {"tx": left}, nq, k * size, size, k * long, k * long, k) for k in range(cuts)]
    steps = [(gives_up, has_below, {"ty": up}, cuts, cuts, 1),
             (jnp.logical_and(gives_left, gives_up), jnp.logical_and(has_right, has_below), {"tx": left, "ty": up}, cuts, cuts + 1, 1),
             (gives_left, has_right, {"tx": left}, 0, 0, cuts)]
    npieces = len(pieces)

    def strip(n):
        _, _, where, _, _, rows, out, into, _ = pieces[n]
        length = rows * 5 // 4
        return remote(code_out.at[pl.ds(out, length)], code_in.at[pl.ds(into, length)], strip_send.at[n], strip_recv.at[n], where)

    def strip_step(n):
        _, _, where, out, into, number = steps[n]
        return remote(step_out.at[pl.ds(out, number)], step_in.at[pl.ds(into, number)],
                      strip_send.at[npieces + n], strip_recv.at[npieces + n], where)

    def forward(n):
        place = pl.ds(pieces[n][7], pieces[n][5] * 5 // 4)
        return remote(code_in.at[place], code_pair.at[place], pair_send.at[n], pair_recv.at[n], peer)

    def forward_step(n):
        place = pl.ds(steps[n][4], steps[n][5])
        return remote(step_in.at[place], step_pair.at[place], pair_send.at[npieces + n], pair_recv.at[npieces + n], peer)

    def store(off, number):
        rows = number.shape[0]
        code_out[off:off + rows], code_out[off + rows:off + rows * 5 // 4] = split_wide(number)

    for c in mine:
        c.wait()
    number, step_out[cuts] = encode_wide(jnp.concatenate([ext_ref[me, q, :N] for q in range(nq)], axis=0))
    for q in range(nq):
        store(base + q * short, number[q * N:(q + 1) * N])
    for k in range(cuts):
        number, step_out[k] = encode_wide(ext_ref[me, 0, k * size:(k + 1) * size])
        store(k * long, number)
    for c in places:
        c.wait()
    list_ref[me, 0:1, :slots] = spots[0, 0]
    list_ref[me, 1:2, :slots] = spots[1, 0]

    pl.semaphore_wait(barrier, 7)
    for n in range(3):
        @pl.when(steps[n][0])
        def _():
            strip_step(n).start()
    for n in range(npieces):
        @pl.when(pieces[n][0])
        def _():
            strip(n).start()

    extra = npieces + 3
    lists = remote(list_ref.at[me], list_ref.at[me], pair_send.at[extra], pair_recv.at[extra], peer)
    lists.start()
    move = remote(amp_ref.at[pl.ds(moved, slots - moved)], shared_ref.at[pl.ds(0, slots - moved)],
                  pair_send.at[extra + 1], pair_recv.at[extra + 1], peer)

    @pl.when(me == 0)
    def _():
        move.start()

    for n in range(npieces):
        @pl.when(jnp.logical_not(pieces[n][1]))
        def _():
            for p in range(2):
                ext_ref[p, pieces[n][3], pieces[n][4]:pieces[n][4] + pieces[n][5]] = jnp.zeros((pieces[n][5], N), jnp.float32)

    def place(n, p, code, step):
        _, _, _, q, row, rows, _, off, which = pieces[n]
        ext_ref[p, q, row:row + rows] = decode_wide(code[off:off + rows], code[off + rows:off + rows * 5 // 4], step[which])

    for n in range(3):
        @pl.when(steps[n][1])
        def _():
            strip_step(n).wait_recv()
            forward_step(n).start()

    order = list(range(nq + 1, npieces)) + list(range(nq + 1))
    for n in order:
        @pl.when(pieces[n][1])
        def _():
            strip(n).wait_recv()
            forward(n).start()
            place(n, me, code_in, step_in)

    for n in range(3):
        @pl.when(steps[n][1])
        def _():
            forward_step(n).wait_recv()

    for n in order:
        @pl.when(pieces[n][1])
        def _():
            forward(n).wait_recv()
            place(n, other, code_pair, step_pair)

    for c in local:
        c.wait()
    lists.wait()

    @pl.when(me == 0)
    def _():
        move.wait_send()

    @pl.when(me == 1)
    def _():
        move.wait_recv()

    for n in range(npieces):
        @pl.when(pieces[n][0])
        def _():
            strip(n).wait_send()

        @pl.when(pieces[n][1])
        def _():
            forward(n).wait_send()

    for n in range(3):
        @pl.when(steps[n][0])
        def _():
            strip_step(n).wait_send()

        @pl.when(steps[n][1])
        def _():
            forward_step(n).wait_send()


def spread(obj, amp, rows, cols, cuts=4):
    nty, ntx = lax.axis_size("ty"), lax.axis_size("tx")
    height, width = obj.shape[1:]
    slots = amp.shape[0]
    nq = width // N
    copies = nq + 1 + cuts + 3
    total = height * 5 // 4 + (nq + 1) * (N * 5 // 4)
    vmem = pl.BlockSpec(memory_space=pltpu.VMEM)
    hbm = pl.BlockSpec(memory_space=pltpu.HBM)
    dma = pltpu.SemaphoreType.DMA
    code, step = pltpu.VMEM((total, N), jnp.int16), pltpu.VMEM((cuts + 2, 8, N), jnp.float32)
    return pl.pallas_call(
        functools.partial(spread_kernel, nty, ntx, cuts),
        out_shape=(
            jax.ShapeDtypeStruct((2, nq + 1, height + N, N), jnp.float32),
            jax.ShapeDtypeStruct((slots + slots // 2, N, N), jnp.bfloat16),
            jax.ShapeDtypeStruct((2, 8, N), jnp.int32),
        ),
        in_specs=[hbm] * 4,
        out_specs=(vmem, vmem, vmem),
        scratch_shapes=[
            pltpu.VMEM((2, 1, 1, slots), jnp.int32),
            code, step, code, step, code, step,
            dma((2 * nq + 3,)), dma((copies,)), dma((copies,)), dma((copies + 2,)), dma((copies + 2,)),
        ],
        compiler_params=pltpu.CompilerParams(collective_id=0, has_side_effects=True, vmem_limit_bytes=SPREAD_VMEM),
        name="spread",
    )(*(pltpu.with_memory_space_constraint(x, pltpu.HBM) for x in (obj, amp, rows, cols)))


def dft_tables(length):
    freqs = np.arange(length)
    angle = (freqs[:, None] * freqs[None, :] % length) * (2.0 * math.pi / length)
    cosine = np.cos(angle) / math.sqrt(length)
    sine = np.sin(angle) / math.sqrt(length)
    forward = np.block([[cosine, -sine], [sine, cosine]]).astype(ml_dtypes.bfloat16)
    inverse = np.block([[cosine, sine], [-sine, cosine]]).astype(ml_dtypes.bfloat16)
    return forward, inverse

def mm(a, b):
    return jnp.dot(a, b, preferred_element_type=jnp.float32)

def patch_kernel(B, slots, counts_ref, list_ref, ext_ref, probe_ref, amp_ref, fwd_ref, inv_ref,
                 acc_ref, pg_ref, patch_ref):
    acc_ref[...] = jnp.zeros_like(acc_ref)
    pg_ref[...] = jnp.zeros_like(pg_ref)
    lane = lax.broadcasted_iota(jnp.int32, (N, N), 1)
    me = lax.axis_index("pa")
    count = counts_ref[lax.axis_index("ty"), lax.axis_index("tx")]
    moved = slots // 2
    split = jnp.maximum((count + 1) // 2, jnp.minimum(count, moved))
    first = jnp.where(me == 0, 0, split)
    last = jnp.where(me == 0, split, count)

    def body(it, _):
        pos = []
        psis = []
        for b in range(B):
            i = first + it * B + b
            number = jnp.minimum(i, last - 1)
            r = list_ref[number // slots, 0, number % slots]
            c = list_ref[number // slots, 1, number % slots]
            slot = number - me * moved
            j = c // N
            s = c % N
            pos.append((slot, i < last, r, j, s))
            back = (N - s) % N
            high = lane >= s
            parts = []
            for p in range(2):
                v = jnp.where(high, ext_ref[p, j, pl.ds(r, N), :], ext_ref[p, j + 1, pl.ds(r, N), :])
                v = pltpu.roll(v, back, 1)
                patch_ref[b, p] = v
                parts.append(v)
            pre, pim = probe_ref[0], probe_ref[1]
            psi_re = pre * parts[0] - pim * parts[1]
            psi_im = pre * parts[1] + pim * parts[0]
            psis.append(jnp.concatenate([psi_re.astype(jnp.bfloat16), psi_im.astype(jnp.bfloat16)], axis=1))
        half = mm(jnp.concatenate(psis, axis=0), fwd_ref[...]).astype(jnp.bfloat16)
        rhs = jnp.concatenate(
            [jnp.concatenate([half[b * N:(b + 1) * N, q * N:(q + 1) * N] for b in range(B)], axis=1) for q in range(2)], axis=0)
        wave = mm(inv_ref[...], rhs)
        chis = [[], []]
        for b in range(B):
            slot, ok, r, j, s = pos[b]
            wre = wave[:N, b * N:(b + 1) * N]
            wim = wave[N:, b * N:(b + 1) * N]
            level = amp_ref[slot].astype(jnp.float32)
            use = ok.astype(jnp.float32)
            factor = (1.0 - level * lax.rsqrt(wre * wre + wim * wim + 1.0)) * use
            chis[0].append((wre * factor).astype(jnp.bfloat16))
            chis[1].append((wim * factor).astype(jnp.bfloat16))
        rhs2 = jnp.concatenate([jnp.concatenate(chis[q], axis=1) for q in range(2)], axis=0)
        bk = mm(fwd_ref[...], rhs2).astype(jnp.bfloat16)
        lhs = jnp.concatenate([jnp.concatenate([bk[q * N:(q + 1) * N, b * N:(b + 1) * N] for q in range(2)], axis=1) for b in range(B)], axis=0)
        grad = mm(lhs, inv_ref[...])
        tre = pg_ref[0]
        tim = pg_ref[1]
        for b in range(B):
            slot, ok, r, j, s = pos[b]
            gre = grad[b * N:(b + 1) * N, :N]
            gim = grad[b * N:(b + 1) * N, N:]
            pre, pim = probe_ref[0], probe_ref[1]
            qre, qim = patch_ref[b, 0], patch_ref[b, 1]
            tre = tre + (qre * gre + qim * gim)
            tim = tim + (qre * gim - qim * gre)
            obj = (pre * gre + pim * gim, pre * gim - pim * gre)
            high = lane >= s
            low = lane < s
            for p in range(2):
                o = pltpu.roll(obj[p], s, 1)
                u = acc_ref[p, j, pl.ds(r, N), :]
                v = acc_ref[p, j + 1, pl.ds(r, N), :]
                pltpu.store(acc_ref.at[p, j, pl.ds(r, N), :], u + o, mask=high)
                pltpu.store(acc_ref.at[p, j + 1, pl.ds(r, N), :], v + o, mask=low)
        pg_ref[0] = tre
        pg_ref[1] = tim
        return 0

    lax.fori_loop(0, (last - first + B - 1) // B, body, 0)

def patches(counts, lists, ext, probe, amp, fwd, inv, B):
    smem = pl.BlockSpec(memory_space=pltpu.SMEM)
    vmem = pl.BlockSpec(memory_space=pltpu.VMEM)
    return pl.pallas_call(
        functools.partial(patch_kernel, B, amp.shape[0] * 2 // 3),
        out_shape=(jax.ShapeDtypeStruct(ext.shape, jnp.float32), jax.ShapeDtypeStruct((2, N, N), jnp.float32)),
        in_specs=[smem] * 2 + [vmem] * 5,
        out_specs=(vmem, vmem),
        scratch_shapes=[pltpu.VMEM((B, 2, N, N), jnp.float32)],
        compiler_params=pltpu.CompilerParams(vmem_limit_bytes=40 << 20),
        name="patches",
    )(counts, lists, ext, probe, amp, fwd, inv)


def flush_kernel(a_ref, b_ref, a_out, b_out, sem):
    size = a_ref.shape[1] // 4
    copies = [pltpu.make_async_copy(b_ref, b_out, sem.at[8])]
    for n in range(8):
        place = (n // 4, pl.ds(n % 4 * size, size))
        copies.append(pltpu.make_async_copy(a_ref.at[place], a_out.at[place], sem.at[n]))
    for c in copies:
        c.start()
    for c in copies:
        c.wait()


def flush(a, b):
    hbm = pl.BlockSpec(memory_space=pltpu.HBM)
    return pl.pallas_call(
        flush_kernel,
        out_shape=(jax.ShapeDtypeStruct(a.shape, a.dtype), jax.ShapeDtypeStruct(b.shape, b.dtype)),
        in_specs=[pl.BlockSpec(memory_space=pltpu.VMEM)] * 2,
        out_specs=(hbm, hbm),
        scratch_shapes=[pltpu.SemaphoreType.DMA((9,))],
        name="flush",
    )(*(pltpu.with_memory_space_constraint(x, pltpu.VMEM) for x in (a, b)))


def shards(object_field, probe_field, amplitudes, start_row, start_col, counts):
    height, width = object_field.shape[1:]
    extended, shared, lists = spread(object_field, amplitudes[0, 0], start_row, start_col)
    forward, inverse = dft_tables(N)
    grad, probe_part = patches(
        counts, lists, extended, probe_field, shared, jnp.asarray(forward), jnp.asarray(inverse), BLK)
    return flush(*collect(counts, grad, probe_part, height, width))


def solution(mesh):
    return jax.shard_map(
        shards,
        mesh=mesh,
        in_specs=(
            P(None, "ty", "tx"),
            P(),
            P("ty", "tx", "pa", None, None),
            P("ty", "tx", "pa"),
            P("ty", "tx", "pa"),
            P(),
        ),
        out_specs=(P(None, "ty", "tx"), P()),
        check_vma=False,
    )
```

```python
import functools
import math

import jax
import jax.numpy as jnp
import ml_dtypes
import numpy as np
from jax import lax
from jax.experimental import pallas as pl
from jax.experimental.pallas import tpu as pltpu
from jax.sharding import PartitionSpec as P

BLK = 24

N = 128
LEVELS = 32766.0
MESH = pl.DeviceIdType.MESH


def encode(x):
    rows = x.shape[0]
    tiles = x.reshape(rows // 8, 8, N)
    peak = jnp.max(jnp.abs(tiles), axis=0)
    scaled = tiles * (LEVELS / jnp.maximum(peak, 1e-30))[None]
    return jnp.round(scaled.reshape(rows, N)).astype(jnp.int32).astype(jnp.int16), peak * (1.0 / LEVELS)


def decode(code, step):
    rows = code.shape[0]
    value = code.astype(jnp.int32).astype(jnp.float32)
    return (value.reshape(rows // 8, 8, N) * step[None]).reshape(rows, N)


def remote(src, dst, send_sem, recv_sem, where):
    return pltpu.make_async_remote_copy(
        src_ref=src, dst_ref=dst, send_sem=send_sem, recv_sem=recv_sem, device_id=where, device_id_type=MESH)


def collect_kernel(nty, ntx, zh, zl, counts_ref, acc_ref, pg_ref, out_ref, pgo_ref,
                   theirs, code_out, step_out, code_in, step_in, by_line, by_plane,
                   pair_send, pair_recv, strip_send, strip_recv, line_send, line_recv, plane_send, plane_recv, all_send, all_recv):
    ty, tx, me = lax.axis_index("ty"), lax.axis_index("tx"), lax.axis_index("pa")
    other = 1 - me
    height = out_ref.shape[1]
    nq = out_ref.shape[2] // N
    peer = {"pa": other}
    nline, nplane = zh * zl, (nty // zh) * (ntx // zl)
    chunk = N // nline
    line_id = lax.rem(ty, zh) * zl + lax.rem(tx, zl)
    plane_id = (ty // zh) * (ntx // zl) + tx // zl

    nmember = 2 * nline
    member_id = me * nline + line_id

    def in_line(a):
        k = lax.rem(a, nline)
        return {"ty": (ty // zh) * zh + k // zl, "tx": (tx // zl) * zl + lax.rem(k, zl), "pa": a // nline}

    def in_plane(k):
        return {"ty": (k // (ntx // zl)) * zh + lax.rem(ty, zh), "tx": lax.rem(k, ntx // zl) * zl + lax.rem(tx, zl)}

    def next_in_line(k):
        return lax.rem(member_id + k, nmember)

    def next_in_plane(k):
        return lax.rem(plane_id + k, nplane)

    sizes = (height, nq * N, N)
    offs = (0, height, height + nq * N)
    targets = ({"tx": lax.rem(tx + 1, ntx)}, {"ty": lax.rem(ty + 1, nty)},
               {"tx": lax.rem(tx + 1, ntx), "ty": lax.rem(ty + 1, nty)})
    sources = ({"tx": lax.rem(tx + ntx - 1, ntx)}, {"ty": lax.rem(ty + nty - 1, nty)},
               {"tx": lax.rem(tx + ntx - 1, ntx), "ty": lax.rem(ty + nty - 1, nty)})
    sends = (tx < ntx - 1, ty < nty - 1, jnp.logical_and(tx < ntx - 1, ty < nty - 1))
    gets = (tx > 0, ty > 0, jnp.logical_and(tx > 0, ty > 0))

    barrier = pltpu.get_barrier_semaphore()
    for where in targets + sources:
        pl.semaphore_signal(barrier, inc=1, device_id=where, device_id_type=MESH)

    @pl.loop(1, nmember)
    def _(k):
        pl.semaphore_signal(barrier, inc=1, device_id=in_line(next_in_line(k)), device_id_type=MESH)

    @pl.loop(1, nplane)
    def _(k):
        pl.semaphore_signal(barrier, inc=1, device_id=in_plane(next_in_plane(k)), device_id_type=MESH)

    total = jnp.sum(jnp.sum(counts_ref[...].astype(jnp.float32), axis=1, keepdims=True), axis=0, keepdims=True)
    pl.semaphore_wait(barrier, 6 + nmember - 1 + nplane - 1)

    def rows_of(k):
        return pl.ds(pl.multiple_of(k * chunk, chunk), chunk)

    def line_copy(a):
        return remote(pg_ref.at[a // nline, rows_of(lax.rem(a, nline))], by_line.at[member_id],
                      line_send.at[a], line_recv.at[member_id], in_line(a))

    def line_arrival(a):
        return remote(pg_ref.at[me, rows_of(line_id)], by_line.at[a], line_send.at[a], line_recv.at[a], in_line(a))

    @pl.loop(1, nmember)
    def _(k):
        line_copy(next_in_line(k)).start()

    by_line[member_id] = pg_ref[me, rows_of(line_id)]

    def swap(n, src, dst):
        return remote(src, dst, pair_send.at[n], pair_recv.at[n], peer)

    right = swap(0, acc_ref.at[other, nq], theirs.at[nq])
    low = [swap(1 + q, acc_ref.at[other, q, pl.ds(height, N)], theirs.at[q, pl.ds(height, N)]) for q in range(nq)]
    body = [swap(2 + nq + q, acc_ref.at[other, q, pl.ds(0, height)], theirs.at[q, pl.ds(0, height)]) for q in range(nq)]
    for c in low:
        c.start()
    right.start()
    for c in reversed(body):
        c.start()

    def strip(n):
        size, off = sizes[n], offs[n]
        return (remote(code_out.at[pl.ds(off, size)], code_in.at[pl.ds(off, size)],
                       strip_send.at[2 * n], strip_recv.at[2 * n], targets[n]),
                remote(step_out.at[n], step_in.at[n], strip_send.at[2 * n + 1], strip_recv.at[2 * n + 1], targets[n]))

    def pack(n, value):
        code_out[pl.ds(offs[n], sizes[n])], step_out[n] = encode(value)

    def leave(n):
        @pl.when(sends[n])
        def _():
            for c in strip(n):
                c.start()

    def plane_copy(k):
        return remote(by_plane.at[plane_id], by_plane.at[plane_id], plane_send.at[k], plane_recv.at[plane_id], in_plane(k))

    def plane_arrival(k):
        return remote(by_plane.at[plane_id], by_plane.at[k], plane_send.at[k], plane_recv.at[k], in_plane(k))

    def all_copy(a, source):
        place = pgo_ref.at[source // nline, rows_of(lax.rem(source, nline))]
        return remote(place, place, all_send.at[a], all_recv.at[source], in_line(a))

    for c in low:
        c.wait()
    pack(1, jnp.concatenate([acc_ref[me, q, height:] + theirs[q, height:] for q in range(nq)], axis=0))
    right.wait()
    pack(2, acc_ref[me, nq, height:] + theirs[nq, height:])
    leave(1)
    leave(2)
    pack(0, acc_ref[me, nq, :height] + theirs[nq, :height])

    @pl.loop(1, nmember)
    def _(k):
        line_arrival(next_in_line(k)).wait_recv()

    mine = by_line[0]
    for k in range(1, nmember):
        mine = mine + by_line[k]
    by_plane[plane_id] = mine

    @pl.loop(1, nplane)
    def _(k):
        plane_copy(next_in_plane(k)).start()

    leave(0)

    for q in reversed(range(nq)):
        body[q].wait()
        out_ref[me, :, q * N:(q + 1) * N] = acc_ref[me, q, :height] + theirs[q, :height]

    def final(n, rows, columns):
        place = out_ref.at[me, rows, columns]
        return swap(n, place, place)

    rest = pl.ds(N, (nq - 1) * N)
    early = final(2 + 2 * nq, pl.ds(N, height - N), rest)
    early.start()

    @pl.loop(1, nplane)
    def _(k):
        plane_arrival(next_in_plane(k)).wait_recv()

    mine = by_plane[0]
    for k in range(1, nplane):
        mine = mine + by_plane[k]
    pgo_ref[me, rows_of(line_id)] = mine / total

    @pl.loop(1, nmember)
    def _(k):
        all_copy(next_in_line(k), member_id).start()

    @pl.when(gets[1])
    def _():
        for c in strip(1):
            c.wait_recv()
        for q in range(nq):
            out_ref[me, :N, q * N:(q + 1) * N] += decode(code_in[pl.ds(offs[1] + q * N, N)], step_in[1])

    @pl.when(gets[2])
    def _():
        for c in strip(2):
            c.wait_recv()
        out_ref[me, :N, :N] += decode(code_in[pl.ds(offs[2], N)], step_in[2])

    @pl.when(gets[0])
    def _():
        for c in strip(0):
            c.wait_recv()
        out_ref[me, :, :N] += decode(code_in[pl.ds(0, height)], step_in[0])

    late = [final(3 + 2 * nq, pl.ds(0, height), pl.ds(0, N)), final(4 + 2 * nq, pl.ds(0, N), rest)]
    for c in late:
        c.start()

    @pl.loop(1, nmember)
    def _(k):
        at = next_in_line(k)
        all_copy(at, at).wait_recv()

    for n in range(3):
        @pl.when(sends[n])
        def _():
            for c in strip(n):
                c.wait_send()

    @pl.loop(1, nmember)
    def _(k):
        at = next_in_line(k)
        line_copy(at).wait_send()
        all_copy(at, member_id).wait_send()

    @pl.loop(1, nplane)
    def _(k):
        plane_copy(next_in_plane(k)).wait_send()

    early.wait()
    for c in late:
        c.wait()


def collect(counts, acc, pg, height, width, zh=2, zl=4):
    nty, ntx = lax.axis_size("ty"), lax.axis_size("tx")
    nq = width // N
    rows = height + nq * N + N
    nline, nplane = zh * zl, (nty // zh) * (ntx // zl)
    chunk = N // nline
    vmem = pl.BlockSpec(memory_space=pltpu.VMEM)
    dma = pltpu.SemaphoreType.DMA
    return pl.pallas_call(
        functools.partial(collect_kernel, nty, ntx, zh, zl),
        out_shape=(jax.ShapeDtypeStruct((2, height, width), jnp.float32), jax.ShapeDtypeStruct((2, N, N), jnp.float32)),
        in_specs=[vmem] * 3,
        out_specs=(vmem, vmem),
        scratch_shapes=[
            pltpu.VMEM((nq + 1, height + N, N), jnp.float32),
            pltpu.VMEM((rows, N), jnp.int16),
            pltpu.VMEM((3, 8, N), jnp.float32),
            pltpu.VMEM((rows, N), jnp.int16),
            pltpu.VMEM((3, 8, N), jnp.float32),
            pltpu.VMEM((2 * nline, chunk, N), jnp.float32),
            pltpu.VMEM((nplane, chunk, N), jnp.float32),
            dma((6 + 2 * nq,)), dma((6 + 2 * nq,)), dma((6,)), dma((6,)),
            dma((2 * nline,)), dma((2 * nline,)), dma((nplane,)), dma((nplane,)), dma((2 * nline,)), dma((2 * nline,)),
        ],
        compiler_params=pltpu.CompilerParams(collective_id=1, has_side_effects=True, vmem_limit_bytes=40 << 20),
        name="collect",
    )(counts, acc, pg)


WIDE = 524287.0
SPREAD_VMEM = 40 << 20


def encode_wide(x):
    rows = x.shape[0]
    tiles = x.reshape(rows // 8, 8, N)
    peak = jnp.max(jnp.abs(tiles), axis=0)
    scaled = tiles * (WIDE / jnp.maximum(peak, 1e-30))[None]
    number = jnp.round(scaled.reshape(rows, N)).astype(jnp.int32)
    return number, peak * (1.0 / WIDE)


def split_wide(number):
    quarter = number.shape[0] // 4
    low = number & 15
    word = -32768
    for g in range(4):
        word = word + (low[g * quarter:(g + 1) * quarter] << (4 * g))
    return (number >> 4).astype(jnp.int16), word.astype(jnp.int16)


def decode_wide(high, word, step):
    rows = high.shape[0]
    low = word.astype(jnp.int32) + 32768
    low = jnp.concatenate([(low >> (4 * g)) & 15 for g in range(4)], axis=0)
    value = ((high.astype(jnp.int32) << 4) + low).astype(jnp.float32)
    return (value.reshape(rows // 8, 8, N) * step[None]).reshape(rows, N)


def spread_kernel(nty, ntx, cuts, obj_ref, amp_ref, rows_ref, cols_ref, ext_ref, shared_ref, list_ref,
                  spots, code_out, step_out, code_in, step_in, code_pair, step_pair,
                  local_sem, strip_send, strip_recv, pair_send, pair_recv):
    ty, tx, me = lax.axis_index("ty"), lax.axis_index("tx"), lax.axis_index("pa")
    other = 1 - me
    height = obj_ref.shape[1]
    nq = obj_ref.shape[2] // N
    slots = amp_ref.shape[0]
    moved = slots // 2
    peer = {"pa": other}
    up, down = lax.rem(ty + nty - 1, nty), lax.rem(ty + 1, nty)
    left, right = lax.rem(tx + ntx - 1, ntx), lax.rem(tx + 1, ntx)

    barrier = pltpu.get_barrier_semaphore()
    for where in (peer, {"tx": left}, {"tx": right}, {"ty": up}, {"ty": down}, {"tx": left, "ty": up}, {"tx": right, "ty": down}):
        pl.semaphore_signal(barrier, inc=1, device_id=where, device_id_type=MESH)

    def load(p, q):
        return pltpu.make_async_copy(obj_ref.at[p, :, pl.ds(q * N, N)], ext_ref.at[p, q, pl.ds(0, height)], local_sem.at[p * nq + q])

    mine = [load(me, q) for q in range(nq)]
    local = [load(other, q) for q in range(nq)]
    local.append(pltpu.make_async_copy(amp_ref, shared_ref.at[pl.ds(me * moved, slots)], local_sem.at[2 * nq]))
    places = [pltpu.make_async_copy(rows_ref, spots.at[0], local_sem.at[2 * nq + 1]),
              pltpu.make_async_copy(cols_ref, spots.at[1], local_sem.at[2 * nq + 2])]
    for c in mine + places + local:
        c.start()

    size = height // cuts
    long, short = size * 5 // 4, N * 5 // 4
    has_right, has_below = tx < ntx - 1, ty < nty - 1
    gives_left, gives_up = tx > 0, ty > 0
    base = cuts * long
    pieces = [(gives_up, has_below, {"ty": up}, q, height, N, base + q * short, base + q * short, cuts) for q in range(nq)]
    pieces.append((jnp.logical_and(gives_left, gives_up), jnp.logical_and(has_right, has_below), {"tx": left, "ty": up},
                   nq, height, N, base, base + nq * short, cuts + 1))
    pieces += [(gives_left, has_right, {"tx": left}, nq, k * size, size, k * long, k * long, k) for k in range(cuts)]
    steps = [(gives_up, has_below, {"ty": up}, cuts, cuts, 1),
             (jnp.logical_and(gives_left, gives_up), jnp.logical_and(has_right, has_below), {"tx": left, "ty": up}, cuts, cuts + 1, 1),
             (gives_left, has_right, {"tx": left}, 0, 0, cuts)]
    npieces = len(pieces)

    def strip(n):
        _, _, where, _, _, rows, out, into, _ = pieces[n]
        length = rows * 5 // 4
        return remote(code_out.at[pl.ds(out, length)], code_in.at[pl.ds(into, length)], strip_send.at[n], strip_recv.at[n], where)

    def strip_step(n):
        _, _, where, out, into, number = steps[n]
        return remote(step_out.at[pl.ds(out, number)], step_in.at[pl.ds(into, number)],
                      strip_send.at[npieces + n], strip_recv.at[npieces + n], where)

    def forward(n):
        place = pl.ds(pieces[n][7], pieces[n][5] * 5 // 4)
        return remote(code_in.at[place], code_pair.at[place], pair_send.at[n], pair_recv.at[n], peer)

    def forward_step(n):
        place = pl.ds(steps[n][4], steps[n][5])
        return remote(step_in.at[place], step_pair.at[place], pair_send.at[npieces + n], pair_recv.at[npieces + n], peer)

    def store(off, number):
        rows = number.shape[0]
        code_out[off:off + rows], code_out[off + rows:off + rows * 5 // 4] = split_wide(number)

    for c in mine:
        c.wait()
    number, step_out[cuts] = encode_wide(jnp.concatenate([ext_ref[me, q, :N] for q in range(nq)], axis=0))
    for q in range(nq):
        store(base + q * short, number[q * N:(q + 1) * N])
    for k in range(cuts):
        number, step_out[k] = encode_wide(ext_ref[me, 0, k * size:(k + 1) * size])
        store(k * long, number)
    for c in places:
        c.wait()
    list_ref[me, 0:1, :slots] = spots[0, 0]
    list_ref[me, 1:2, :slots] = spots[1, 0]

    pl.semaphore_wait(barrier, 7)
    for n in range(3):
        @pl.when(steps[n][0])
        def _():
            strip_step(n).start()
    for n in range(npieces):
        @pl.when(pieces[n][0])
        def _():
            strip(n).start()

    extra = npieces + 3
    lists = remote(list_ref.at[me], list_ref.at[me], pair_send.at[extra], pair_recv.at[extra], peer)
    lists.start()
    move = remote(amp_ref.at[pl.ds(moved, slots - moved)], shared_ref.at[pl.ds(0, slots - moved)],
                  pair_send.at[extra + 1], pair_recv.at[extra + 1], peer)

    @pl.when(me == 0)
    def _():
        move.start()

    for n in range(npieces):
        @pl.when(jnp.logical_not(pieces[n][1]))
        def _():
            for p in range(2):
                ext_ref[p, pieces[n][3], pieces[n][4]:pieces[n][4] + pieces[n][5]] = jnp.zeros((pieces[n][5], N), jnp.float32)

    def place(n, p, code, step):
        _, _, _, q, row, rows, _, off, which = pieces[n]
        ext_ref[p, q, row:row + rows] = decode_wide(code[off:off + rows], code[off + rows:off + rows * 5 // 4], step[which])

    for n in range(3):
        @pl.when(steps[n][1])
        def _():
            strip_step(n).wait_recv()
            forward_step(n).start()

    order = list(range(nq + 1, npieces)) + list(range(nq + 1))
    for n in order:
        @pl.when(pieces[n][1])
        def _():
            strip(n).wait_recv()
            forward(n).start()
            place(n, me, code_in, step_in)

    for n in range(3):
        @pl.when(steps[n][1])
        def _():
            forward_step(n).wait_recv()

    for n in order:
        @pl.when(pieces[n][1])
        def _():
            forward(n).wait_recv()
            place(n, other, code_pair, step_pair)

    for c in local:
        c.wait()
    lists.wait()

    @pl.when(me == 0)
    def _():
        move.wait_send()

    @pl.when(me == 1)
    def _():
        move.wait_recv()

    for n in range(npieces):
        @pl.when(pieces[n][0])
        def _():
            strip(n).wait_send()

        @pl.when(pieces[n][1])
        def _():
            forward(n).wait_send()

    for n in range(3):
        @pl.when(steps[n][0])
        def _():
            strip_step(n).wait_send()

        @pl.when(steps[n][1])
        def _():
            forward_step(n).wait_send()


def spread(obj, amp, rows, cols, cuts=4):
    nty, ntx = lax.axis_size("ty"), lax.axis_size("tx")
    height, width = obj.shape[1:]
    slots = amp.shape[0]
    nq = width // N
    copies = nq + 1 + cuts + 3
    total = height * 5 // 4 + (nq + 1) * (N * 5 // 4)
    vmem = pl.BlockSpec(memory_space=pltpu.VMEM)
    hbm = pl.BlockSpec(memory_space=pltpu.HBM)
    dma = pltpu.SemaphoreType.DMA
    code, step = pltpu.VMEM((total, N), jnp.int16), pltpu.VMEM((cuts + 2, 8, N), jnp.float32)
    return pl.pallas_call(
        functools.partial(spread_kernel, nty, ntx, cuts),
        out_shape=(
            jax.ShapeDtypeStruct((2, nq + 1, height + N, N), jnp.float32),
            jax.ShapeDtypeStruct((slots + slots // 2, N, N), jnp.bfloat16),
            jax.ShapeDtypeStruct((2, 8, N), jnp.int32),
        ),
        in_specs=[hbm] * 4,
        out_specs=(vmem, vmem, vmem),
        scratch_shapes=[
            pltpu.VMEM((2, 1, 1, slots), jnp.int32),
            code, step, code, step, code, step,
            dma((2 * nq + 3,)), dma((copies,)), dma((copies,)), dma((copies + 2,)), dma((copies + 2,)),
        ],
        compiler_params=pltpu.CompilerParams(collective_id=0, has_side_effects=True, vmem_limit_bytes=SPREAD_VMEM),
        name="spread",
    )(*(pltpu.with_memory_space_constraint(x, pltpu.HBM) for x in (obj, amp, rows, cols)))


def dft_tables(length):
    freqs = np.arange(length)
    angle = (freqs[:, None] * freqs[None, :] % length) * (2.0 * math.pi / length)
    cosine = np.cos(angle) / math.sqrt(length)
    sine = np.sin(angle) / math.sqrt(length)
    forward = np.block([[cosine, -sine], [sine, cosine]]).astype(ml_dtypes.bfloat16)
    inverse = np.block([[cosine, sine], [-sine, cosine]]).astype(ml_dtypes.bfloat16)
    return forward, inverse

def mm(a, b):
    return jnp.dot(a, b, preferred_element_type=jnp.float32)

def patch_kernel(B, slots, counts_ref, list_ref, ext_ref, probe_ref, amp_ref, fwd_ref, inv_ref,
                 acc_ref, pg_ref, patch_ref):
    acc_ref[...] = jnp.zeros_like(acc_ref)
    pg_ref[...] = jnp.zeros_like(pg_ref)
    lane = lax.broadcasted_iota(jnp.int32, (N, N), 1)
    me = lax.axis_index("pa")
    count = counts_ref[lax.axis_index("ty"), lax.axis_index("tx")]
    moved = slots // 2
    split = jnp.maximum((count + 1) // 2, jnp.minimum(count, moved))
    first = jnp.where(me == 0, 0, split)
    last = jnp.where(me == 0, split, count)

    def body(it, _):
        pos = []
        psis = []
        for b in range(B):
            i = first + it * B + b
            number = jnp.minimum(i, last - 1)
            r = list_ref[number // slots, 0, number % slots]
            c = list_ref[number // slots, 1, number % slots]
            slot = number - me * moved
            j = c // N
            s = c % N
            pos.append((slot, i < last, r, j, s))
            back = (N - s) % N
            high = lane >= s
            parts = []
            for p in range(2):
                v = jnp.where(high, ext_ref[p, j, pl.ds(r, N), :], ext_ref[p, j + 1, pl.ds(r, N), :])
                v = pltpu.roll(v, back, 1)
                patch_ref[b, p] = v
                parts.append(v)
            pre, pim = probe_ref[0], probe_ref[1]
            psi_re = pre * parts[0] - pim * parts[1]
            psi_im = pre * parts[1] + pim * parts[0]
            psis.append(jnp.concatenate([psi_re.astype(jnp.bfloat16), psi_im.astype(jnp.bfloat16)], axis=1))
        half = mm(jnp.concatenate(psis, axis=0), fwd_ref[...]).astype(jnp.bfloat16)
        rhs = jnp.concatenate(
            [jnp.concatenate([half[b * N:(b + 1) * N, q * N:(q + 1) * N] for b in range(B)], axis=1) for q in range(2)], axis=0)
        wave = mm(inv_ref[...], rhs)
        chis = [[], []]
        for b in range(B):
            slot, ok, r, j, s = pos[b]
            wre = wave[:N, b * N:(b + 1) * N]
            wim = wave[N:, b * N:(b + 1) * N]
            level = amp_ref[slot].astype(jnp.float32)
            use = ok.astype(jnp.float32)
            factor = (1.0 - level * lax.rsqrt(wre * wre + wim * wim + 1.0)) * use
            chis[0].append((wre * factor).astype(jnp.bfloat16))
            chis[1].append((wim * factor).astype(jnp.bfloat16))
        rhs2 = jnp.concatenate([jnp.concatenate(chis[q], axis=1) for q in range(2)], axis=0)
        bk = mm(fwd_ref[...], rhs2).astype(jnp.bfloat16)
        lhs = jnp.concatenate([jnp.concatenate([bk[q * N:(q + 1) * N, b * N:(b + 1) * N] for q in range(2)], axis=1) for b in range(B)], axis=0)
        grad = mm(lhs, inv_ref[...])
        tre = pg_ref[0]
        tim = pg_ref[1]
        for b in range(B):
            slot, ok, r, j, s = pos[b]
            gre = grad[b * N:(b + 1) * N, :N]
            gim = grad[b * N:(b + 1) * N, N:]
            pre, pim = probe_ref[0], probe_ref[1]
            qre, qim = patch_ref[b, 0], patch_ref[b, 1]
            tre = tre + (qre * gre + qim * gim)
            tim = tim + (qre * gim - qim * gre)
            obj = (pre * gre + pim * gim, pre * gim - pim * gre)
            high = lane >= s
            low = lane < s
            for p in range(2):
                o = pltpu.roll(obj[p], s, 1)
                u = acc_ref[p, j, pl.ds(r, N), :]
                v = acc_ref[p, j + 1, pl.ds(r, N), :]
                pltpu.store(acc_ref.at[p, j, pl.ds(r, N), :], u + o, mask=high)
                pltpu.store(acc_ref.at[p, j + 1, pl.ds(r, N), :], v + o, mask=low)
        pg_ref[0] = tre
        pg_ref[1] = tim
        return 0

    lax.fori_loop(0, (last - first + B - 1) // B, body, 0)

def patches(counts, lists, ext, probe, amp, fwd, inv, B):
    smem = pl.BlockSpec(memory_space=pltpu.SMEM)
    vmem = pl.BlockSpec(memory_space=pltpu.VMEM)
    return pl.pallas_call(
        functools.partial(patch_kernel, B, amp.shape[0] * 2 // 3),
        out_shape=(jax.ShapeDtypeStruct(ext.shape, jnp.float32), jax.ShapeDtypeStruct((2, N, N), jnp.float32)),
        in_specs=[smem] * 2 + [vmem] * 5,
        out_specs=(vmem, vmem),
        scratch_shapes=[pltpu.VMEM((B, 2, N, N), jnp.float32)],
        compiler_params=pltpu.CompilerParams(vmem_limit_bytes=40 << 20),
        name="patches",
    )(counts, lists, ext, probe, amp, fwd, inv)


def flush_kernel(a_ref, b_ref, a_out, b_out, sem):
    size = a_ref.shape[1] // 4
    copies = [pltpu.make_async_copy(b_ref, b_out, sem.at[8])]
    for n in range(8):
        place = (n // 4, pl.ds(n % 4 * size, size))
        copies.append(pltpu.make_async_copy(a_ref.at[place], a_out.at[place], sem.at[n]))
    for c in copies:
        c.start()
    for c in copies:
        c.wait()


def flush(a, b):
    hbm = pl.BlockSpec(memory_space=pltpu.HBM)
    return pl.pallas_call(
        flush_kernel,
        out_shape=(jax.ShapeDtypeStruct(a.shape, a.dtype), jax.ShapeDtypeStruct(b.shape, b.dtype)),
        in_specs=[pl.BlockSpec(memory_space=pltpu.VMEM)] * 2,
        out_specs=(hbm, hbm),
        scratch_shapes=[pltpu.SemaphoreType.DMA((9,))],
        name="flush",
    )(*(pltpu.with_memory_space_constraint(x, pltpu.VMEM) for x in (a, b)))


def shards(object_field, probe_field, amplitudes, start_row, start_col, counts):
    height, width = object_field.shape[1:]
    extended, shared, lists = spread(object_field, amplitudes[0, 0], start_row, start_col)
    forward, inverse = dft_tables(N)
    grad, probe_part = patches(
        counts, lists, extended, probe_field, shared, jnp.asarray(forward), jnp.asarray(inverse), BLK)
    return flush(*collect(counts, grad, probe_part, height, width))


def solution(mesh):
    return jax.shard_map(
        shards,
        mesh=mesh,
        in_specs=(
            P(None, "ty", "tx"),
            P(),
            P("ty", "tx", "pa", None, None),
            P("ty", "tx", "pa"),
            P("ty", "tx", "pa"),
            P(),
        ),
        out_specs=(P(None, "ty", "tx"), P()),
        check_vma=False,
    )
```

```python
import functools
import math

import jax
import jax.numpy as jnp
import ml_dtypes
import numpy as np
from jax import lax
from jax.experimental import pallas as pl
from jax.experimental.pallas import tpu as pltpu
from jax.sharding import PartitionSpec as P

BLK = 24

N = 128
LEVELS = 32766.0
MESH = pl.DeviceIdType.MESH


def encode(x):
    rows = x.shape[0]
    tiles = x.reshape(rows // 8, 8, N)
    peak = jnp.max(jnp.abs(tiles), axis=0)
    scaled = tiles * (LEVELS / jnp.maximum(peak, 1e-30))[None]
    return jnp.round(scaled.reshape(rows, N)).astype(jnp.int32).astype(jnp.int16), peak * (1.0 / LEVELS)


def decode(code, step):
    rows = code.shape[0]
    value = code.astype(jnp.int32).astype(jnp.float32)
    return (value.reshape(rows // 8, 8, N) * step[None]).reshape(rows, N)


def remote(src, dst, send_sem, recv_sem, where):
    return pltpu.make_async_remote_copy(
        src_ref=src, dst_ref=dst, send_sem=send_sem, recv_sem=recv_sem, device_id=where, device_id_type=MESH)


def collect_kernel(nty, ntx, zh, zl, counts_ref, acc_ref, pg_ref, out_ref, pgo_ref,
                   theirs, pg_theirs, code_out, step_out, code_in, step_in, by_line, by_plane, part,
                   pair_send, pair_recv, strip_send, strip_recv, line_send, line_recv, plane_send, plane_recv, all_send, all_recv):
    ty, tx, me = lax.axis_index("ty"), lax.axis_index("tx"), lax.axis_index("pa")
    other = 1 - me
    height = out_ref.shape[1]
    nq = out_ref.shape[2] // N
    peer = {"pa": other}
    nline, nplane = zh * zl, (nty // zh) * (ntx // zl)
    chunk = N // nline
    line_id = lax.rem(ty, zh) * zl + lax.rem(tx, zl)
    plane_id = (ty // zh) * (ntx // zl) + tx // zl

    def in_line(k):
        return {"ty": (ty // zh) * zh + k // zl, "tx": (tx // zl) * zl + lax.rem(k, zl)}

    def in_plane(k):
        return {"ty": (k // (ntx // zl)) * zh + lax.rem(ty, zh), "tx": lax.rem(k, ntx // zl) * zl + lax.rem(tx, zl)}

    def next_in_line(k):
        return lax.rem(line_id + k, nline)

    def next_in_plane(k):
        return lax.rem(plane_id + k, nplane)

    sizes = (height, nq * N, N)
    offs = (0, height, height + nq * N)
    targets = ({"tx": lax.rem(tx + 1, ntx)}, {"ty": lax.rem(ty + 1, nty)},
               {"tx": lax.rem(tx + 1, ntx), "ty": lax.rem(ty + 1, nty)})
    sources = ({"tx": lax.rem(tx + ntx - 1, ntx)}, {"ty": lax.rem(ty + nty - 1, nty)},
               {"tx": lax.rem(tx + ntx - 1, ntx), "ty": lax.rem(ty + nty - 1, nty)})
    sends = (tx < ntx - 1, ty < nty - 1, jnp.logical_and(tx < ntx - 1, ty < nty - 1))
    gets = (tx > 0, ty > 0, jnp.logical_and(tx > 0, ty > 0))

    barrier = pltpu.get_barrier_semaphore()
    for where in (peer,) + targets + sources:
        pl.semaphore_signal(barrier, inc=1, device_id=where, device_id_type=MESH)

    @pl.loop(1, nline)
    def _(k):
        pl.semaphore_signal(barrier, inc=1, device_id=in_line(next_in_line(k)), device_id_type=MESH)

    @pl.loop(1, nplane)
    def _(k):
        pl.semaphore_signal(barrier, inc=1, device_id=in_plane(next_in_plane(k)), device_id_type=MESH)

    total = jnp.sum(jnp.sum(counts_ref[...].astype(jnp.float32), axis=1, keepdims=True), axis=0, keepdims=True)
    pl.semaphore_wait(barrier, 1 + 6 + nline - 1 + nplane - 1)

    def swap(n, src, dst):
        return remote(src, dst, pair_send.at[n], pair_recv.at[n], peer)

    probe_swap = swap(1 + nq, pg_ref.at[other], pg_theirs)
    right = swap(0, acc_ref.at[other, nq], theirs.at[nq])
    low = [swap(1 + q, acc_ref.at[other, q, pl.ds(height, N)], theirs.at[q, pl.ds(height, N)]) for q in range(nq)]
    body = [swap(2 + nq + q, acc_ref.at[other, q, pl.ds(0, height)], theirs.at[q, pl.ds(0, height)]) for q in range(nq)]
    probe_swap.start()
    for c in low:
        c.start()
    right.start()
    for c in reversed(body):
        c.start()

    def strip(n):
        size, off = sizes[n], offs[n]
        return (remote(code_out.at[pl.ds(off, size)], code_in.at[pl.ds(off, size)],
                       strip_send.at[2 * n], strip_recv.at[2 * n], targets[n]),
                remote(step_out.at[n], step_in.at[n], strip_send.at[2 * n + 1], strip_recv.at[2 * n + 1], targets[n]))

    def pack(n, value):
        code_out[pl.ds(offs[n], sizes[n])], step_out[n] = encode(value)

    def leave(n):
        @pl.when(sends[n])
        def _():
            for c in strip(n):
                c.start()

    def rows_of(k):
        return pl.ds(pl.multiple_of(k * chunk, chunk), chunk)

    def line_copy(k):
        return remote(part.at[rows_of(k)], by_line.at[line_id], line_send.at[k], line_recv.at[line_id], in_line(k))

    def line_arrival(k):
        return remote(part.at[rows_of(k)], by_line.at[k], line_send.at[k], line_recv.at[k], in_line(k))

    def plane_copy(k):
        return remote(by_plane.at[plane_id], by_plane.at[plane_id], plane_send.at[k], plane_recv.at[plane_id], in_plane(k))

    def plane_arrival(k):
        return remote(by_plane.at[plane_id], by_plane.at[k], plane_send.at[k], plane_recv.at[k], in_plane(k))

    def all_copy(k, at):
        place = pgo_ref.at[me, rows_of(at)]
        return remote(place, place, all_send.at[k], all_recv.at[at], in_line(k))

    probe_swap.wait()
    part[...] = pg_ref[me] + pg_theirs[...]

    @pl.loop(1, nline)
    def _(k):
        line_copy(next_in_line(k)).start()

    by_line[line_id] = part[rows_of(line_id)]

    for c in low:
        c.wait()
    pack(1, jnp.concatenate([acc_ref[me, q, height:] + theirs[q, height:] for q in range(nq)], axis=0))
    right.wait()
    pack(2, acc_ref[me, nq, height:] + theirs[nq, height:])
    leave(1)
    leave(2)
    pack(0, acc_ref[me, nq, :height] + theirs[nq, :height])

    @pl.loop(1, nline)
    def _(k):
        line_arrival(next_in_line(k)).wait_recv()

    mine = by_line[0]
    for k in range(1, nline):
        mine = mine + by_line[k]
    by_plane[plane_id] = mine

    @pl.loop(1, nplane)
    def _(k):
        plane_copy(next_in_plane(k)).start()

    leave(0)

    for q in reversed(range(nq)):
        body[q].wait()
        out_ref[me, :, q * N:(q + 1) * N] = acc_ref[me, q, :height] + theirs[q, :height]

    def final(n, rows, columns):
        place = out_ref.at[me, rows, columns]
        return swap(n, place, place)

    rest = pl.ds(N, (nq - 1) * N)
    early = final(2 + 2 * nq, pl.ds(N, height - N), rest)
    early.start()

    @pl.loop(1, nplane)
    def _(k):
        plane_arrival(next_in_plane(k)).wait_recv()

    mine = by_plane[0]
    for k in range(1, nplane):
        mine = mine + by_plane[k]
    pgo_ref[me, rows_of(line_id)] = mine / total

    @pl.loop(1, nline)
    def _(k):
        all_copy(next_in_line(k), line_id).start()

    @pl.when(gets[1])
    def _():
        for c in strip(1):
            c.wait_recv()
        for q in range(nq):
            out_ref[me, :N, q * N:(q + 1) * N] += decode(code_in[pl.ds(offs[1] + q * N, N)], step_in[1])

    @pl.when(gets[2])
    def _():
        for c in strip(2):
            c.wait_recv()
        out_ref[me, :N, :N] += decode(code_in[pl.ds(offs[2], N)], step_in[2])

    @pl.when(gets[0])
    def _():
        for c in strip(0):
            c.wait_recv()
        out_ref[me, :, :N] += decode(code_in[pl.ds(0, height)], step_in[0])

    late = [final(3 + 2 * nq, pl.ds(0, height), pl.ds(0, N)), final(4 + 2 * nq, pl.ds(0, N), rest)]
    for c in late:
        c.start()

    @pl.loop(1, nline)
    def _(k):
        at = next_in_line(k)
        all_copy(at, at).wait_recv()

    last = swap(5 + 2 * nq, pgo_ref.at[me], pgo_ref.at[me])
    last.start()

    for n in range(3):
        @pl.when(sends[n])
        def _():
            for c in strip(n):
                c.wait_send()

    @pl.loop(1, nline)
    def _(k):
        at = next_in_line(k)
        line_copy(at).wait_send()
        all_copy(at, line_id).wait_send()

    @pl.loop(1, nplane)
    def _(k):
        plane_copy(next_in_plane(k)).wait_send()

    early.wait()
    for c in late:
        c.wait()
    last.wait()


def collect(counts, acc, pg, height, width, zh=2, zl=4):
    nty, ntx = lax.axis_size("ty"), lax.axis_size("tx")
    nq = width // N
    rows = height + nq * N + N
    nline, nplane = zh * zl, (nty // zh) * (ntx // zl)
    chunk = N // nline
    vmem = pl.BlockSpec(memory_space=pltpu.VMEM)
    dma = pltpu.SemaphoreType.DMA
    return pl.pallas_call(
        functools.partial(collect_kernel, nty, ntx, zh, zl),
        out_shape=(jax.ShapeDtypeStruct((2, height, width), jnp.float32), jax.ShapeDtypeStruct((2, N, N), jnp.float32)),
        in_specs=[vmem] * 3,
        out_specs=(vmem, vmem),
        scratch_shapes=[
            pltpu.VMEM((nq + 1, height + N, N), jnp.float32),
            pltpu.VMEM((N, N), jnp.float32),
            pltpu.VMEM((rows, N), jnp.int16),
            pltpu.VMEM((3, 8, N), jnp.float32),
            pltpu.VMEM((rows, N), jnp.int16),
            pltpu.VMEM((3, 8, N), jnp.float32),
            pltpu.VMEM((nline, chunk, N), jnp.float32),
            pltpu.VMEM((nplane, chunk, N), jnp.float32),
            pltpu.VMEM((N, N), jnp.float32),
            dma((6 + 2 * nq,)), dma((6 + 2 * nq,)), dma((6,)), dma((6,)),
            dma((nline,)), dma((nline,)), dma((nplane,)), dma((nplane,)), dma((nline,)), dma((nline,)),
        ],
        compiler_params=pltpu.CompilerParams(collective_id=1, has_side_effects=True, vmem_limit_bytes=40 << 20),
        name="collect",
    )(counts, acc, pg)


WIDE = 524287.0
SPREAD_VMEM = 40 << 20


def encode_wide(x):
    rows = x.shape[0]
    tiles = x.reshape(rows // 8, 8, N)
    peak = jnp.max(jnp.abs(tiles), axis=0)
    scaled = tiles * (WIDE / jnp.maximum(peak, 1e-30))[None]
    number = jnp.round(scaled.reshape(rows, N)).astype(jnp.int32)
    return number, peak * (1.0 / WIDE)


def split_wide(number):
    quarter = number.shape[0] // 4
    low = number & 15
    word = -32768
    for g in range(4):
        word = word + (low[g * quarter:(g + 1) * quarter] << (4 * g))
    return (number >> 4).astype(jnp.int16), word.astype(jnp.int16)


def decode_wide(high, word, step):
    rows = high.shape[0]
    low = word.astype(jnp.int32) + 32768
    low = jnp.concatenate([(low >> (4 * g)) & 15 for g in range(4)], axis=0)
    value = ((high.astype(jnp.int32) << 4) + low).astype(jnp.float32)
    return (value.reshape(rows // 8, 8, N) * step[None]).reshape(rows, N)


def spread_kernel(nty, ntx, cuts, obj_ref, amp_ref, rows_ref, cols_ref, ext_ref, shared_ref, list_ref,
                  spots, code_out, step_out, code_in, step_in, code_pair, step_pair,
                  local_sem, strip_send, strip_recv, pair_send, pair_recv):
    ty, tx, me = lax.axis_index("ty"), lax.axis_index("tx"), lax.axis_index("pa")
    other = 1 - me
    height = obj_ref.shape[1]
    nq = obj_ref.shape[2] // N
    slots = amp_ref.shape[0]
    moved = slots // 2
    peer = {"pa": other}
    up, down = lax.rem(ty + nty - 1, nty), lax.rem(ty + 1, nty)
    left, right = lax.rem(tx + ntx - 1, ntx), lax.rem(tx + 1, ntx)

    barrier = pltpu.get_barrier_semaphore()
    for where in (peer, {"tx": left}, {"tx": right}, {"ty": up}, {"ty": down}, {"tx": left, "ty": up}, {"tx": right, "ty": down}):
        pl.semaphore_signal(barrier, inc=1, device_id=where, device_id_type=MESH)

    def load(p, q):
        return pltpu.make_async_copy(obj_ref.at[p, :, pl.ds(q * N, N)], ext_ref.at[p, q, pl.ds(0, height)], local_sem.at[p * nq + q])

    mine = [load(me, q) for q in range(nq)]
    local = [load(other, q) for q in range(nq)]
    local.append(pltpu.make_async_copy(amp_ref, shared_ref.at[pl.ds(me * moved, slots)], local_sem.at[2 * nq]))
    places = [pltpu.make_async_copy(rows_ref, spots.at[0], local_sem.at[2 * nq + 1]),
              pltpu.make_async_copy(cols_ref, spots.at[1], local_sem.at[2 * nq + 2])]
    for c in mine + places + local:
        c.start()

    size = height // cuts
    long, short = size * 5 // 4, N * 5 // 4
    has_right, has_below = tx < ntx - 1, ty < nty - 1
    gives_left, gives_up = tx > 0, ty > 0
    base = cuts * long
    pieces = [(gives_up, has_below, {"ty": up}, q, height, N, base + q * short, base + q * short, cuts) for q in range(nq)]
    pieces.append((jnp.logical_and(gives_left, gives_up), jnp.logical_and(has_right, has_below), {"tx": left, "ty": up},
                   nq, height, N, base, base + nq * short, cuts + 1))
    pieces += [(gives_left, has_right, {"tx": left}, nq, k * size, size, k * long, k * long, k) for k in range(cuts)]
    steps = [(gives_up, has_below, {"ty": up}, cuts, cuts, 1),
             (jnp.logical_and(gives_left, gives_up), jnp.logical_and(has_right, has_below), {"tx": left, "ty": up}, cuts, cuts + 1, 1),
             (gives_left, has_right, {"tx": left}, 0, 0, cuts)]
    npieces = len(pieces)

    def strip(n):
        _, _, where, _, _, rows, out, into, _ = pieces[n]
        length = rows * 5 // 4
        return remote(code_out.at[pl.ds(out, length)], code_in.at[pl.ds(into, length)], strip_send.at[n], strip_recv.at[n], where)

    def strip_step(n):
        _, _, where, out, into, number = steps[n]
        return remote(step_out.at[pl.ds(out, number)], step_in.at[pl.ds(into, number)],
                      strip_send.at[npieces + n], strip_recv.at[npieces + n], where)

    def forward(n):
        place = pl.ds(pieces[n][7], pieces[n][5] * 5 // 4)
        return remote(code_in.at[place], code_pair.at[place], pair_send.at[n], pair_recv.at[n], peer)

    def forward_step(n):
        place = pl.ds(steps[n][4], steps[n][5])
        return remote(step_in.at[place], step_pair.at[place], pair_send.at[npieces + n], pair_recv.at[npieces + n], peer)

    def store(off, number):
        rows = number.shape[0]
        code_out[off:off + rows], code_out[off + rows:off + rows * 5 // 4] = split_wide(number)

    for c in mine:
        c.wait()
    number, step_out[cuts] = encode_wide(jnp.concatenate([ext_ref[me, q, :N] for q in range(nq)], axis=0))
    for q in range(nq):
        store(base + q * short, number[q * N:(q + 1) * N])
    for k in range(cuts):
        number, step_out[k] = encode_wide(ext_ref[me, 0, k * size:(k + 1) * size])
        store(k * long, number)
    for c in places:
        c.wait()
    list_ref[me, 0:1, :slots] = spots[0, 0]
    list_ref[me, 1:2, :slots] = spots[1, 0]

    pl.semaphore_wait(barrier, 7)
    for n in range(3):
        @pl.when(steps[n][0])
        def _():
            strip_step(n).start()
    for n in range(npieces):
        @pl.when(pieces[n][0])
        def _():
            strip(n).start()

    extra = npieces + 3
    lists = remote(list_ref.at[me], list_ref.at[me], pair_send.at[extra], pair_recv.at[extra], peer)
    lists.start()
    move = remote(amp_ref.at[pl.ds(moved, slots - moved)], shared_ref.at[pl.ds(0, slots - moved)],
                  pair_send.at[extra + 1], pair_recv.at[extra + 1], peer)

    @pl.when(me == 0)
    def _():
        move.start()

    for n in range(npieces):
        @pl.when(jnp.logical_not(pieces[n][1]))
        def _():
            for p in range(2):
                ext_ref[p, pieces[n][3], pieces[n][4]:pieces[n][4] + pieces[n][5]] = jnp.zeros((pieces[n][5], N), jnp.float32)

    def place(n, p, code, step):
        _, _, _, q, row, rows, _, off, which = pieces[n]
        ext_ref[p, q, row:row + rows] = decode_wide(code[off:off + rows], code[off + rows:off + rows * 5 // 4], step[which])

    for n in range(3):
        @pl.when(steps[n][1])
        def _():
            strip_step(n).wait_recv()
            forward_step(n).start()

    order = list(range(nq + 1, npieces)) + list(range(nq + 1))
    for n in order:
        @pl.when(pieces[n][1])
        def _():
            strip(n).wait_recv()
            forward(n).start()
            place(n, me, code_in, step_in)

    for n in range(3):
        @pl.when(steps[n][1])
        def _():
            forward_step(n).wait_recv()

    for n in order:
        @pl.when(pieces[n][1])
        def _():
            forward(n).wait_recv()
            place(n, other, code_pair, step_pair)

    for c in local:
        c.wait()
    lists.wait()

    @pl.when(me == 0)
    def _():
        move.wait_send()

    @pl.when(me == 1)
    def _():
        move.wait_recv()

    for n in range(npieces):
        @pl.when(pieces[n][0])
        def _():
            strip(n).wait_send()

        @pl.when(pieces[n][1])
        def _():
            forward(n).wait_send()

    for n in range(3):
        @pl.when(steps[n][0])
        def _():
            strip_step(n).wait_send()

        @pl.when(steps[n][1])
        def _():
            forward_step(n).wait_send()


def spread(obj, amp, rows, cols, cuts=2):
    nty, ntx = lax.axis_size("ty"), lax.axis_size("tx")
    height, width = obj.shape[1:]
    slots = amp.shape[0]
    nq = width // N
    copies = nq + 1 + cuts + 3
    total = height * 5 // 4 + (nq + 1) * (N * 5 // 4)
    vmem = pl.BlockSpec(memory_space=pltpu.VMEM)
    hbm = pl.BlockSpec(memory_space=pltpu.HBM)
    dma = pltpu.SemaphoreType.DMA
    code, step = pltpu.VMEM((total, N), jnp.int16), pltpu.VMEM((cuts + 2, 8, N), jnp.float32)
    return pl.pallas_call(
        functools.partial(spread_kernel, nty, ntx, cuts),
        out_shape=(
            jax.ShapeDtypeStruct((2, nq + 1, height + N, N), jnp.float32),
            jax.ShapeDtypeStruct((slots + slots // 2, N, N), jnp.bfloat16),
            jax.ShapeDtypeStruct((2, 8, N), jnp.int32),
        ),
        in_specs=[hbm] * 4,
        out_specs=(vmem, vmem, vmem),
        scratch_shapes=[
            pltpu.VMEM((2, 1, 1, slots), jnp.int32),
            code, step, code, step, code, step,
            dma((2 * nq + 3,)), dma((copies,)), dma((copies,)), dma((copies + 2,)), dma((copies + 2,)),
        ],
        compiler_params=pltpu.CompilerParams(collective_id=0, has_side_effects=True, vmem_limit_bytes=SPREAD_VMEM),
        name="spread",
    )(*(pltpu.with_memory_space_constraint(x, pltpu.HBM) for x in (obj, amp, rows, cols)))


def dft_tables(length):
    freqs = np.arange(length)
    angle = (freqs[:, None] * freqs[None, :] % length) * (2.0 * math.pi / length)
    cosine = np.cos(angle) / math.sqrt(length)
    sine = np.sin(angle) / math.sqrt(length)
    forward = np.block([[cosine, -sine], [sine, cosine]]).astype(ml_dtypes.bfloat16)
    inverse = np.block([[cosine, sine], [-sine, cosine]]).astype(ml_dtypes.bfloat16)
    return forward, inverse

def mm(a, b):
    return jnp.dot(a, b, preferred_element_type=jnp.float32)

def patch_kernel(B, slots, counts_ref, list_ref, ext_ref, probe_ref, amp_ref, fwd_ref, inv_ref,
                 acc_ref, pg_ref, patch_ref):
    acc_ref[...] = jnp.zeros_like(acc_ref)
    pg_ref[...] = jnp.zeros_like(pg_ref)
    lane = lax.broadcasted_iota(jnp.int32, (N, N), 1)
    me = lax.axis_index("pa")
    count = counts_ref[lax.axis_index("ty"), lax.axis_index("tx")]
    moved = slots // 2
    split = jnp.maximum((count + 1) // 2, jnp.minimum(count, moved))
    first = jnp.where(me == 0, 0, split)
    last = jnp.where(me == 0, split, count)

    def body(it, _):
        pos = []
        psis = []
        for b in range(B):
            i = first + it * B + b
            number = jnp.minimum(i, last - 1)
            r = list_ref[number // slots, 0, number % slots]
            c = list_ref[number // slots, 1, number % slots]
            slot = number - me * moved
            j = c // N
            s = c % N
            pos.append((slot, i < last, r, j, s))
            back = (N - s) % N
            high = lane >= s
            parts = []
            for p in range(2):
                v = jnp.where(high, ext_ref[p, j, pl.ds(r, N), :], ext_ref[p, j + 1, pl.ds(r, N), :])
                v = pltpu.roll(v, back, 1)
                patch_ref[b, p] = v
                parts.append(v)
            pre, pim = probe_ref[0], probe_ref[1]
            psi_re = pre * parts[0] - pim * parts[1]
            psi_im = pre * parts[1] + pim * parts[0]
            psis.append(jnp.concatenate([psi_re.astype(jnp.bfloat16), psi_im.astype(jnp.bfloat16)], axis=1))
        half = mm(jnp.concatenate(psis, axis=0), fwd_ref[...]).astype(jnp.bfloat16)
        rhs = jnp.concatenate(
            [jnp.concatenate([half[b * N:(b + 1) * N, q * N:(q + 1) * N] for b in range(B)], axis=1) for q in range(2)], axis=0)
        wave = mm(inv_ref[...], rhs)
        chis = [[], []]
        for b in range(B):
            slot, ok, r, j, s = pos[b]
            wre = wave[:N, b * N:(b + 1) * N]
            wim = wave[N:, b * N:(b + 1) * N]
            level = amp_ref[slot].astype(jnp.float32)
            use = ok.astype(jnp.float32)
            factor = (1.0 - level * lax.rsqrt(wre * wre + wim * wim + 1.0)) * use
            chis[0].append((wre * factor).astype(jnp.bfloat16))
            chis[1].append((wim * factor).astype(jnp.bfloat16))
        rhs2 = jnp.concatenate([jnp.concatenate(chis[q], axis=1) for q in range(2)], axis=0)
        bk = mm(fwd_ref[...], rhs2).astype(jnp.bfloat16)
        lhs = jnp.concatenate([jnp.concatenate([bk[q * N:(q + 1) * N, b * N:(b + 1) * N] for q in range(2)], axis=1) for b in range(B)], axis=0)
        grad = mm(lhs, inv_ref[...])
        tre = pg_ref[0]
        tim = pg_ref[1]
        for b in range(B):
            slot, ok, r, j, s = pos[b]
            gre = grad[b * N:(b + 1) * N, :N]
            gim = grad[b * N:(b + 1) * N, N:]
            pre, pim = probe_ref[0], probe_ref[1]
            qre, qim = patch_ref[b, 0], patch_ref[b, 1]
            tre = tre + (qre * gre + qim * gim)
            tim = tim + (qre * gim - qim * gre)
            obj = (pre * gre + pim * gim, pre * gim - pim * gre)
            high = lane >= s
            low = lane < s
            for p in range(2):
                o = pltpu.roll(obj[p], s, 1)
                u = acc_ref[p, j, pl.ds(r, N), :]
                v = acc_ref[p, j + 1, pl.ds(r, N), :]
                pltpu.store(acc_ref.at[p, j, pl.ds(r, N), :], u + o, mask=high)
                pltpu.store(acc_ref.at[p, j + 1, pl.ds(r, N), :], v + o, mask=low)
        pg_ref[0] = tre
        pg_ref[1] = tim
        return 0

    lax.fori_loop(0, (last - first + B - 1) // B, body, 0)

def patches(counts, lists, ext, probe, amp, fwd, inv, B):
    smem = pl.BlockSpec(memory_space=pltpu.SMEM)
    vmem = pl.BlockSpec(memory_space=pltpu.VMEM)
    return pl.pallas_call(
        functools.partial(patch_kernel, B, amp.shape[0] * 2 // 3),
        out_shape=(jax.ShapeDtypeStruct(ext.shape, jnp.float32), jax.ShapeDtypeStruct((2, N, N), jnp.float32)),
        in_specs=[smem] * 2 + [vmem] * 5,
        out_specs=(vmem, vmem),
        scratch_shapes=[pltpu.VMEM((B, 2, N, N), jnp.float32)],
        compiler_params=pltpu.CompilerParams(vmem_limit_bytes=40 << 20),
        name="patches",
    )(counts, lists, ext, probe, amp, fwd, inv)


def flush_kernel(a_ref, b_ref, a_out, b_out, sem):
    size = a_ref.shape[1] // 4
    copies = [pltpu.make_async_copy(b_ref, b_out, sem.at[8])]
    for n in range(8):
        place = (n // 4, pl.ds(n % 4 * size, size))
        copies.append(pltpu.make_async_copy(a_ref.at[place], a_out.at[place], sem.at[n]))
    for c in copies:
        c.start()
    for c in copies:
        c.wait()


def flush(a, b):
    hbm = pl.BlockSpec(memory_space=pltpu.HBM)
    return pl.pallas_call(
        flush_kernel,
        out_shape=(jax.ShapeDtypeStruct(a.shape, a.dtype), jax.ShapeDtypeStruct(b.shape, b.dtype)),
        in_specs=[pl.BlockSpec(memory_space=pltpu.VMEM)] * 2,
        out_specs=(hbm, hbm),
        scratch_shapes=[pltpu.SemaphoreType.DMA((9,))],
        name="flush",
    )(*(pltpu.with_memory_space_constraint(x, pltpu.VMEM) for x in (a, b)))


def shards(object_field, probe_field, amplitudes, start_row, start_col, counts):
    height, width = object_field.shape[1:]
    extended, shared, lists = spread(object_field, amplitudes[0, 0], start_row, start_col)
    forward, inverse = dft_tables(N)
    grad, probe_part = patches(
        counts, lists, extended, probe_field, shared, jnp.asarray(forward), jnp.asarray(inverse), BLK)
    return flush(*collect(counts, grad, probe_part, height, width))


def solution(mesh):
    return jax.shard_map(
        shards,
        mesh=mesh,
        in_specs=(
            P(None, "ty", "tx"),
            P(),
            P("ty", "tx", "pa", None, None),
            P("ty", "tx", "pa"),
            P("ty", "tx", "pa"),
            P(),
        ),
        out_specs=(P(None, "ty", "tx"), P()),
        check_vma=False,
    )
```

```python
import functools
import math

import jax
import jax.numpy as jnp
import ml_dtypes
import numpy as np
from jax import lax
from jax.experimental import pallas as pl
from jax.experimental.pallas import tpu as pltpu
from jax.sharding import PartitionSpec as P

BLK = 24

N = 128
LEVELS = 32766.0
MESH = pl.DeviceIdType.MESH


def encode(x):
    rows = x.shape[0]
    tiles = x.reshape(rows // 8, 8, N)
    peak = jnp.max(jnp.abs(tiles), axis=0)
    scaled = tiles * (LEVELS / jnp.maximum(peak, 1e-30))[None]
    return jnp.round(scaled.reshape(rows, N)).astype(jnp.int32).astype(jnp.int16), peak * (1.0 / LEVELS)


def decode(code, step):
    rows = code.shape[0]
    value = code.astype(jnp.int32).astype(jnp.float32)
    return (value.reshape(rows // 8, 8, N) * step[None]).reshape(rows, N)


def remote(src, dst, send_sem, recv_sem, where):
    return pltpu.make_async_remote_copy(
        src_ref=src, dst_ref=dst, send_sem=send_sem, recv_sem=recv_sem, device_id=where, device_id_type=MESH)


def collect_kernel(nty, ntx, zh, zl, counts_ref, acc_ref, pg_ref, out_ref, pgo_ref,
                   theirs, pg_theirs, code_out, step_out, code_in, step_in, by_line, by_plane, part,
                   pair_send, pair_recv, strip_send, strip_recv, line_send, line_recv, plane_send, plane_recv, all_send, all_recv):
    ty, tx, me = lax.axis_index("ty"), lax.axis_index("tx"), lax.axis_index("pa")
    other = 1 - me
    height = out_ref.shape[1]
    nq = out_ref.shape[2] // N
    peer = {"pa": other}
    nline, nplane = zh * zl, (nty // zh) * (ntx // zl)
    chunk = N // nline
    line_id = lax.rem(ty, zh) * zl + lax.rem(tx, zl)
    plane_id = (ty // zh) * (ntx // zl) + tx // zl

    def in_line(k):
        return {"ty": (ty // zh) * zh + k // zl, "tx": (tx // zl) * zl + lax.rem(k, zl)}

    def in_plane(k):
        return {"ty": (k // (ntx // zl)) * zh + lax.rem(ty, zh), "tx": lax.rem(k, ntx // zl) * zl + lax.rem(tx, zl)}

    def next_in_line(k):
        return lax.rem(line_id + k, nline)

    def next_in_plane(k):
        return lax.rem(plane_id + k, nplane)

    sizes = (height, nq * N, N)
    offs = (0, height, height + nq * N)
    targets = ({"tx": lax.rem(tx + 1, ntx)}, {"ty": lax.rem(ty + 1, nty)},
               {"tx": lax.rem(tx + 1, ntx), "ty": lax.rem(ty + 1, nty)})
    sources = ({"tx": lax.rem(tx + ntx - 1, ntx)}, {"ty": lax.rem(ty + nty - 1, nty)},
               {"tx": lax.rem(tx + ntx - 1, ntx), "ty": lax.rem(ty + nty - 1, nty)})
    sends = (tx < ntx - 1, ty < nty - 1, jnp.logical_and(tx < ntx - 1, ty < nty - 1))
    gets = (tx > 0, ty > 0, jnp.logical_and(tx > 0, ty > 0))

    barrier = pltpu.get_barrier_semaphore()
    for where in (peer,) + targets + sources:
        pl.semaphore_signal(barrier, inc=1, device_id=where, device_id_type=MESH)

    @pl.loop(1, nline)
    def _(k):
        pl.semaphore_signal(barrier, inc=1, device_id=in_line(next_in_line(k)), device_id_type=MESH)

    @pl.loop(1, nplane)
    def _(k):
        pl.semaphore_signal(barrier, inc=1, device_id=in_plane(next_in_plane(k)), device_id_type=MESH)

    total = jnp.sum(jnp.sum(counts_ref[...].astype(jnp.float32), axis=1, keepdims=True), axis=0, keepdims=True)
    pl.semaphore_wait(barrier, 1 + 6 + nline - 1 + nplane - 1)

    def swap(n, src, dst):
        return remote(src, dst, pair_send.at[n], pair_recv.at[n], peer)

    probe_swap = swap(1 + nq, pg_ref.at[other], pg_theirs)
    right = swap(0, acc_ref.at[other, nq], theirs.at[nq])
    low = [swap(1 + q, acc_ref.at[other, q, pl.ds(height, N)], theirs.at[q, pl.ds(height, N)]) for q in range(nq)]
    body = [swap(2 + nq + q, acc_ref.at[other, q, pl.ds(0, height)], theirs.at[q, pl.ds(0, height)]) for q in range(nq)]
    probe_swap.start()
    for c in low:
        c.start()
    right.start()
    for c in reversed(body):
        c.start()

    def strip(n):
        size, off = sizes[n], offs[n]
        return (remote(code_out.at[pl.ds(off, size)], code_in.at[pl.ds(off, size)],
                       strip_send.at[2 * n], strip_recv.at[2 * n], targets[n]),
                remote(step_out.at[n], step_in.at[n], strip_send.at[2 * n + 1], strip_recv.at[2 * n + 1], targets[n]))

    def pack(n, value):
        code_out[pl.ds(offs[n], sizes[n])], step_out[n] = encode(value)

    def leave(n):
        @pl.when(sends[n])
        def _():
            for c in strip(n):
                c.start()

    def rows_of(k):
        return pl.ds(pl.multiple_of(k * chunk, chunk), chunk)

    def line_copy(k):
        return remote(part.at[rows_of(k)], by_line.at[line_id], line_send.at[k], line_recv.at[line_id], in_line(k))

    def line_arrival(k):
        return remote(part.at[rows_of(k)], by_line.at[k], line_send.at[k], line_recv.at[k], in_line(k))

    def plane_copy(k):
        return remote(by_plane.at[plane_id], by_plane.at[plane_id], plane_send.at[k], plane_recv.at[plane_id], in_plane(k))

    def plane_arrival(k):
        return remote(by_plane.at[plane_id], by_plane.at[k], plane_send.at[k], plane_recv.at[k], in_plane(k))

    def all_copy(k, at):
        place = pgo_ref.at[me, rows_of(at)]
        return remote(place, place, all_send.at[k], all_recv.at[at], in_line(k))

    probe_swap.wait()
    part[...] = pg_ref[me] + pg_theirs[...]

    @pl.loop(1, nline)
    def _(k):
        line_copy(next_in_line(k)).start()

    by_line[line_id] = part[rows_of(line_id)]

    for c in low:
        c.wait()
    pack(1, jnp.concatenate([acc_ref[me, q, height:] + theirs[q, height:] for q in range(nq)], axis=0))
    right.wait()
    pack(2, acc_ref[me, nq, height:] + theirs[nq, height:])
    leave(1)
    leave(2)
    pack(0, acc_ref[me, nq, :height] + theirs[nq, :height])

    @pl.loop(1, nline)
    def _(k):
        line_arrival(next_in_line(k)).wait_recv()

    mine = by_line[0]
    for k in range(1, nline):
        mine = mine + by_line[k]
    by_plane[plane_id] = mine

    @pl.loop(1, nplane)
    def _(k):
        plane_copy(next_in_plane(k)).start()

    leave(0)

    for q in reversed(range(nq)):
        body[q].wait()
        out_ref[me, :, q * N:(q + 1) * N] = acc_ref[me, q, :height] + theirs[q, :height]

    def final(n, rows, columns):
        place = out_ref.at[me, rows, columns]
        return swap(n, place, place)

    rest = pl.ds(N, (nq - 1) * N)
    early = final(2 + 2 * nq, pl.ds(N, height - N), rest)
    early.start()

    @pl.loop(1, nplane)
    def _(k):
        plane_arrival(next_in_plane(k)).wait_recv()

    mine = by_plane[0]
    for k in range(1, nplane):
        mine = mine + by_plane[k]
    pgo_ref[me, rows_of(line_id)] = mine / total

    @pl.loop(1, nline)
    def _(k):
        all_copy(next_in_line(k), line_id).start()

    @pl.when(gets[1])
    def _():
        for c in strip(1):
            c.wait_recv()
        for q in range(nq):
            out_ref[me, :N, q * N:(q + 1) * N] += decode(code_in[pl.ds(offs[1] + q * N, N)], step_in[1])

    top = final(4 + 2 * nq, pl.ds(0, N), rest)
    top.start()

    @pl.when(gets[2])
    def _():
        for c in strip(2):
            c.wait_recv()
        out_ref[me, :N, :N] += decode(code_in[pl.ds(offs[2], N)], step_in[2])

    @pl.when(gets[0])
    def _():
        for c in strip(0):
            c.wait_recv()
        out_ref[me, :, :N] += decode(code_in[pl.ds(0, height)], step_in[0])

    late = [final(3 + 2 * nq, pl.ds(0, height), pl.ds(0, N)), top]
    late[0].start()

    @pl.loop(1, nline)
    def _(k):
        at = next_in_line(k)
        all_copy(at, at).wait_recv()

    last = swap(5 + 2 * nq, pgo_ref.at[me], pgo_ref.at[me])
    last.start()

    for n in range(3):
        @pl.when(sends[n])
        def _():
            for c in strip(n):
                c.wait_send()

    @pl.loop(1, nline)
    def _(k):
        at = next_in_line(k)
        line_copy(at).wait_send()
        all_copy(at, line_id).wait_send()

    @pl.loop(1, nplane)
    def _(k):
        plane_copy(next_in_plane(k)).wait_send()

    early.wait()
    for c in late:
        c.wait()
    last.wait()


def collect(counts, acc, pg, height, width, zh=2, zl=4):
    nty, ntx = lax.axis_size("ty"), lax.axis_size("tx")
    nq = width // N
    rows = height + nq * N + N
    nline, nplane = zh * zl, (nty // zh) * (ntx // zl)
    chunk = N // nline
    vmem = pl.BlockSpec(memory_space=pltpu.VMEM)
    dma = pltpu.SemaphoreType.DMA
    return pl.pallas_call(
        functools.partial(collect_kernel, nty, ntx, zh, zl),
        out_shape=(jax.ShapeDtypeStruct((2, height, width), jnp.float32), jax.ShapeDtypeStruct((2, N, N), jnp.float32)),
        in_specs=[vmem] * 3,
        out_specs=(vmem, vmem),
        scratch_shapes=[
            pltpu.VMEM((nq + 1, height + N, N), jnp.float32),
            pltpu.VMEM((N, N), jnp.float32),
            pltpu.VMEM((rows, N), jnp.int16),
            pltpu.VMEM((3, 8, N), jnp.float32),
            pltpu.VMEM((rows, N), jnp.int16),
            pltpu.VMEM((3, 8, N), jnp.float32),
            pltpu.VMEM((nline, chunk, N), jnp.float32),
            pltpu.VMEM((nplane, chunk, N), jnp.float32),
            pltpu.VMEM((N, N), jnp.float32),
            dma((6 + 2 * nq,)), dma((6 + 2 * nq,)), dma((6,)), dma((6,)),
            dma((nline,)), dma((nline,)), dma((nplane,)), dma((nplane,)), dma((nline,)), dma((nline,)),
        ],
        compiler_params=pltpu.CompilerParams(collective_id=1, has_side_effects=True, vmem_limit_bytes=40 << 20),
        name="collect",
    )(counts, acc, pg)


WIDE = 524287.0
SPREAD_VMEM = 40 << 20


def encode_wide(x):
    rows = x.shape[0]
    tiles = x.reshape(rows // 8, 8, N)
    peak = jnp.max(jnp.abs(tiles), axis=0)
    scaled = tiles * (WIDE / jnp.maximum(peak, 1e-30))[None]
    number = jnp.round(scaled.reshape(rows, N)).astype(jnp.int32)
    return number, peak * (1.0 / WIDE)


def split_wide(number):
    quarter = number.shape[0] // 4
    low = number & 15
    word = -32768
    for g in range(4):
        word = word + (low[g * quarter:(g + 1) * quarter] << (4 * g))
    return (number >> 4).astype(jnp.int16), word.astype(jnp.int16)


def decode_wide(high, word, step):
    rows = high.shape[0]
    low = word.astype(jnp.int32) + 32768
    low = jnp.concatenate([(low >> (4 * g)) & 15 for g in range(4)], axis=0)
    value = ((high.astype(jnp.int32) << 4) + low).astype(jnp.float32)
    return (value.reshape(rows // 8, 8, N) * step[None]).reshape(rows, N)


def spread_kernel(nty, ntx, cuts, obj_ref, amp_ref, rows_ref, cols_ref, ext_ref, shared_ref, list_ref,
                  spots, code_out, step_out, code_in, step_in, code_pair, step_pair,
                  local_sem, strip_send, strip_recv, pair_send, pair_recv):
    ty, tx, me = lax.axis_index("ty"), lax.axis_index("tx"), lax.axis_index("pa")
    other = 1 - me
    height = obj_ref.shape[1]
    nq = obj_ref.shape[2] // N
    slots = amp_ref.shape[0]
    moved = slots // 2
    peer = {"pa": other}
    up, down = lax.rem(ty + nty - 1, nty), lax.rem(ty + 1, nty)
    left, right = lax.rem(tx + ntx - 1, ntx), lax.rem(tx + 1, ntx)

    barrier = pltpu.get_barrier_semaphore()
    for where in (peer, {"tx": left}, {"tx": right}, {"ty": up}, {"ty": down}, {"tx": left, "ty": up}, {"tx": right, "ty": down}):
        pl.semaphore_signal(barrier, inc=1, device_id=where, device_id_type=MESH)

    def load(p, q):
        return pltpu.make_async_copy(obj_ref.at[p, :, pl.ds(q * N, N)], ext_ref.at[p, q, pl.ds(0, height)], local_sem.at[p * nq + q])

    mine = [load(me, q) for q in range(nq)]
    local = [load(other, q) for q in range(nq)]
    local.append(pltpu.make_async_copy(amp_ref, shared_ref.at[pl.ds(me * moved, slots)], local_sem.at[2 * nq]))
    places = [pltpu.make_async_copy(rows_ref, spots.at[0], local_sem.at[2 * nq + 1]),
              pltpu.make_async_copy(cols_ref, spots.at[1], local_sem.at[2 * nq + 2])]
    for c in mine + places + local:
        c.start()

    size = height // cuts
    long, short = size * 5 // 4, N * 5 // 4
    has_right, has_below = tx < ntx - 1, ty < nty - 1
    gives_left, gives_up = tx > 0, ty > 0
    base = cuts * long
    pieces = [(gives_up, has_below, {"ty": up}, q, height, N, base + q * short, base + q * short, cuts) for q in range(nq)]
    pieces.append((jnp.logical_and(gives_left, gives_up), jnp.logical_and(has_right, has_below), {"tx": left, "ty": up},
                   nq, height, N, base, base + nq * short, cuts + 1))
    pieces += [(gives_left, has_right, {"tx": left}, nq, k * size, size, k * long, k * long, k) for k in range(cuts)]
    steps = [(gives_up, has_below, {"ty": up}, cuts, cuts, 1),
             (jnp.logical_and(gives_left, gives_up), jnp.logical_and(has_right, has_below), {"tx": left, "ty": up}, cuts, cuts + 1, 1),
             (gives_left, has_right, {"tx": left}, 0, 0, cuts)]
    npieces = len(pieces)

    def strip(n):
        _, _, where, _, _, rows, out, into, _ = pieces[n]
        length = rows * 5 // 4
        return remote(code_out.at[pl.ds(out, length)], code_in.at[pl.ds(into, length)], strip_send.at[n], strip_recv.at[n], where)

    def strip_step(n):
        _, _, where, out, into, number = steps[n]
        return remote(step_out.at[pl.ds(out, number)], step_in.at[pl.ds(into, number)],
                      strip_send.at[npieces + n], strip_recv.at[npieces + n], where)

    def forward(n):
        place = pl.ds(pieces[n][7], pieces[n][5] * 5 // 4)
        return remote(code_in.at[place], code_pair.at[place], pair_send.at[n], pair_recv.at[n], peer)

    def forward_step(n):
        place = pl.ds(steps[n][4], steps[n][5])
        return remote(step_in.at[place], step_pair.at[place], pair_send.at[npieces + n], pair_recv.at[npieces + n], peer)

    def store(off, number):
        rows = number.shape[0]
        code_out[off:off + rows], code_out[off + rows:off + rows * 5 // 4] = split_wide(number)

    for c in mine:
        c.wait()
    number, step_out[cuts] = encode_wide(jnp.concatenate([ext_ref[me, q, :N] for q in range(nq)], axis=0))
    for q in range(nq):
        store(base + q * short, number[q * N:(q + 1) * N])
    for k in range(cuts):
        number, step_out[k] = encode_wide(ext_ref[me, 0, k * size:(k + 1) * size])
        store(k * long, number)
    for c in places:
        c.wait()
    list_ref[me, 0:1, :slots] = spots[0, 0]
    list_ref[me, 1:2, :slots] = spots[1, 0]

    pl.semaphore_wait(barrier, 7)
    for n in range(3):
        @pl.when(steps[n][0])
        def _():
            strip_step(n).start()
    for n in range(npieces):
        @pl.when(pieces[n][0])
        def _():
            strip(n).start()

    extra = npieces + 3
    lists = remote(list_ref.at[me], list_ref.at[me], pair_send.at[extra], pair_recv.at[extra], peer)
    lists.start()
    move = remote(amp_ref.at[pl.ds(moved, slots - moved)], shared_ref.at[pl.ds(0, slots - moved)],
                  pair_send.at[extra + 1], pair_recv.at[extra + 1], peer)

    @pl.when(me == 0)
    def _():
        move.start()

    for n in range(npieces):
        @pl.when(jnp.logical_not(pieces[n][1]))
        def _():
            for p in range(2):
                ext_ref[p, pieces[n][3], pieces[n][4]:pieces[n][4] + pieces[n][5]] = jnp.zeros((pieces[n][5], N), jnp.float32)

    def place(n, p, code, step):
        _, _, _, q, row, rows, _, off, which = pieces[n]
        ext_ref[p, q, row:row + rows] = decode_wide(code[off:off + rows], code[off + rows:off + rows * 5 // 4], step[which])

    for n in range(3):
        @pl.when(steps[n][1])
        def _():
            strip_step(n).wait_recv()
            forward_step(n).start()

    order = list(range(nq + 1, npieces)) + list(range(nq + 1))
    for n in order:
        @pl.when(pieces[n][1])
        def _():
            strip(n).wait_recv()
            forward(n).start()
            place(n, me, code_in, step_in)

    for n in range(3):
        @pl.when(steps[n][1])
        def _():
            forward_step(n).wait_recv()

    for n in order:
        @pl.when(pieces[n][1])
        def _():
            forward(n).wait_recv()
            place(n, other, code_pair, step_pair)

    for c in local:
        c.wait()
    lists.wait()

    @pl.when(me == 0)
    def _():
        move.wait_send()

    @pl.when(me == 1)
    def _():
        move.wait_recv()

    for n in range(npieces):
        @pl.when(pieces[n][0])
        def _():
            strip(n).wait_send()

        @pl.when(pieces[n][1])
        def _():
            forward(n).wait_send()

    for n in range(3):
        @pl.when(steps[n][0])
        def _():
            strip_step(n).wait_send()

        @pl.when(steps[n][1])
        def _():
            forward_step(n).wait_send()


def spread(obj, amp, rows, cols, cuts=4):
    nty, ntx = lax.axis_size("ty"), lax.axis_size("tx")
    height, width = obj.shape[1:]
    slots = amp.shape[0]
    nq = width // N
    copies = nq + 1 + cuts + 3
    total = height * 5 // 4 + (nq + 1) * (N * 5 // 4)
    vmem = pl.BlockSpec(memory_space=pltpu.VMEM)
    hbm = pl.BlockSpec(memory_space=pltpu.HBM)
    dma = pltpu.SemaphoreType.DMA
    code, step = pltpu.VMEM((total, N), jnp.int16), pltpu.VMEM((cuts + 2, 8, N), jnp.float32)
    return pl.pallas_call(
        functools.partial(spread_kernel, nty, ntx, cuts),
        out_shape=(
            jax.ShapeDtypeStruct((2, nq + 1, height + N, N), jnp.float32),
            jax.ShapeDtypeStruct((slots + slots // 2, N, N), jnp.bfloat16),
            jax.ShapeDtypeStruct((2, 8, N), jnp.int32),
        ),
        in_specs=[hbm] * 4,
        out_specs=(vmem, vmem, vmem),
        scratch_shapes=[
            pltpu.VMEM((2, 1, 1, slots), jnp.int32),
            code, step, code, step, code, step,
            dma((2 * nq + 3,)), dma((copies,)), dma((copies,)), dma((copies + 2,)), dma((copies + 2,)),
        ],
        compiler_params=pltpu.CompilerParams(collective_id=0, has_side_effects=True, vmem_limit_bytes=SPREAD_VMEM),
        name="spread",
    )(*(pltpu.with_memory_space_constraint(x, pltpu.HBM) for x in (obj, amp, rows, cols)))


def dft_tables(length):
    freqs = np.arange(length)
    angle = (freqs[:, None] * freqs[None, :] % length) * (2.0 * math.pi / length)
    cosine = np.cos(angle) / math.sqrt(length)
    sine = np.sin(angle) / math.sqrt(length)
    forward = np.block([[cosine, -sine], [sine, cosine]]).astype(ml_dtypes.bfloat16)
    inverse = np.block([[cosine, sine], [-sine, cosine]]).astype(ml_dtypes.bfloat16)
    return forward, inverse

def mm(a, b):
    return jnp.dot(a, b, preferred_element_type=jnp.float32)

def patch_kernel(B, slots, counts_ref, list_ref, ext_ref, probe_ref, amp_ref, fwd_ref, inv_ref,
                 acc_ref, pg_ref, patch_ref):
    acc_ref[...] = jnp.zeros_like(acc_ref)
    pg_ref[...] = jnp.zeros_like(pg_ref)
    lane = lax.broadcasted_iota(jnp.int32, (N, N), 1)
    me = lax.axis_index("pa")
    count = counts_ref[lax.axis_index("ty"), lax.axis_index("tx")]
    moved = slots // 2
    split = jnp.maximum((count + 1) // 2, jnp.minimum(count, moved))
    first = jnp.where(me == 0, 0, split)
    last = jnp.where(me == 0, split, count)

    def body(it, _):
        pos = []
        psis = []
        for b in range(B):
            i = first + it * B + b
            number = jnp.minimum(i, last - 1)
            r = list_ref[number // slots, 0, number % slots]
            c = list_ref[number // slots, 1, number % slots]
            slot = number - me * moved
            j = c // N
            s = c % N
            pos.append((slot, i < last, r, j, s))
            back = (N - s) % N
            high = lane >= s
            parts = []
            for p in range(2):
                v = jnp.where(high, ext_ref[p, j, pl.ds(r, N), :], ext_ref[p, j + 1, pl.ds(r, N), :])
                v = pltpu.roll(v, back, 1)
                patch_ref[b, p] = v
                parts.append(v)
            pre, pim = probe_ref[0], probe_ref[1]
            psi_re = pre * parts[0] - pim * parts[1]
            psi_im = pre * parts[1] + pim * parts[0]
            psis.append(jnp.concatenate([psi_re.astype(jnp.bfloat16), psi_im.astype(jnp.bfloat16)], axis=1))
        half = mm(jnp.concatenate(psis, axis=0), fwd_ref[...]).astype(jnp.bfloat16)
        rhs = jnp.concatenate(
            [jnp.concatenate([half[b * N:(b + 1) * N, q * N:(q + 1) * N] for b in range(B)], axis=1) for q in range(2)], axis=0)
        wave = mm(inv_ref[...], rhs)
        chis = [[], []]
        for b in range(B):
            slot, ok, r, j, s = pos[b]
            wre = wave[:N, b * N:(b + 1) * N]
            wim = wave[N:, b * N:(b + 1) * N]
            level = amp_ref[slot].astype(jnp.float32)
            use = ok.astype(jnp.float32)
            factor = (1.0 - level * lax.rsqrt(wre * wre + wim * wim + 1.0)) * use
            chis[0].append((wre * factor).astype(jnp.bfloat16))
            chis[1].append((wim * factor).astype(jnp.bfloat16))
        rhs2 = jnp.concatenate([jnp.concatenate(chis[q], axis=1) for q in range(2)], axis=0)
        bk = mm(fwd_ref[...], rhs2).astype(jnp.bfloat16)
        lhs = jnp.concatenate([jnp.concatenate([bk[q * N:(q + 1) * N, b * N:(b + 1) * N] for q in range(2)], axis=1) for b in range(B)], axis=0)
        grad = mm(lhs, inv_ref[...])
        tre = pg_ref[0]
        tim = pg_ref[1]
        for b in range(B):
            slot, ok, r, j, s = pos[b]
            gre = grad[b * N:(b + 1) * N, :N]
            gim = grad[b * N:(b + 1) * N, N:]
            pre, pim = probe_ref[0], probe_ref[1]
            qre, qim = patch_ref[b, 0], patch_ref[b, 1]
            tre = tre + (qre * gre + qim * gim)
            tim = tim + (qre * gim - qim * gre)
            obj = (pre * gre + pim * gim, pre * gim - pim * gre)
            high = lane >= s
            low = lane < s
            for p in range(2):
                o = pltpu.roll(obj[p], s, 1)
                u = acc_ref[p, j, pl.ds(r, N), :]
                v = acc_ref[p, j + 1, pl.ds(r, N), :]
                pltpu.store(acc_ref.at[p, j, pl.ds(r, N), :], u + o, mask=high)
                pltpu.store(acc_ref.at[p, j + 1, pl.ds(r, N), :], v + o, mask=low)
        pg_ref[0] = tre
        pg_ref[1] = tim
        return 0

    lax.fori_loop(0, (last - first + B - 1) // B, body, 0)

def patches(counts, lists, ext, probe, amp, fwd, inv, B):
    smem = pl.BlockSpec(memory_space=pltpu.SMEM)
    vmem = pl.BlockSpec(memory_space=pltpu.VMEM)
    return pl.pallas_call(
        functools.partial(patch_kernel, B, amp.shape[0] * 2 // 3),
        out_shape=(jax.ShapeDtypeStruct(ext.shape, jnp.float32), jax.ShapeDtypeStruct((2, N, N), jnp.float32)),
        in_specs=[smem] * 2 + [vmem] * 5,
        out_specs=(vmem, vmem),
        scratch_shapes=[pltpu.VMEM((B, 2, N, N), jnp.float32)],
        compiler_params=pltpu.CompilerParams(vmem_limit_bytes=40 << 20),
        name="patches",
    )(counts, lists, ext, probe, amp, fwd, inv)


def flush_kernel(a_ref, b_ref, a_out, b_out, sem):
    size = a_ref.shape[1] // 4
    copies = [pltpu.make_async_copy(b_ref, b_out, sem.at[8])]
    for n in range(8):
        place = (n // 4, pl.ds(n % 4 * size, size))
        copies.append(pltpu.make_async_copy(a_ref.at[place], a_out.at[place], sem.at[n]))
    for c in copies:
        c.start()
    for c in copies:
        c.wait()


def flush(a, b):
    hbm = pl.BlockSpec(memory_space=pltpu.HBM)
    return pl.pallas_call(
        flush_kernel,
        out_shape=(jax.ShapeDtypeStruct(a.shape, a.dtype), jax.ShapeDtypeStruct(b.shape, b.dtype)),
        in_specs=[pl.BlockSpec(memory_space=pltpu.VMEM)] * 2,
        out_specs=(hbm, hbm),
        scratch_shapes=[pltpu.SemaphoreType.DMA((9,))],
        name="flush",
    )(*(pltpu.with_memory_space_constraint(x, pltpu.VMEM) for x in (a, b)))


def shards(object_field, probe_field, amplitudes, start_row, start_col, counts):
    height, width = object_field.shape[1:]
    extended, shared, lists = spread(object_field, amplitudes[0, 0], start_row, start_col)
    forward, inverse = dft_tables(N)
    grad, probe_part = patches(
        counts, lists, extended, probe_field, shared, jnp.asarray(forward), jnp.asarray(inverse), BLK)
    return flush(*collect(counts, grad, probe_part, height, width))


def solution(mesh):
    return jax.shard_map(
        shards,
        mesh=mesh,
        in_specs=(
            P(None, "ty", "tx"),
            P(),
            P("ty", "tx", "pa", None, None),
            P("ty", "tx", "pa"),
            P("ty", "tx", "pa"),
            P(),
        ),
        out_specs=(P(None, "ty", "tx"), P()),
        check_vma=False,
    )
```
